256 devices in a mesh: row: 8 (over z_lo, core), col: 32 (over z_hi, x, y).
Axes of the slice: x: 4, y: 4, z: 8 (z_hi: 2, z_lo: 4; z = z_hi * 4 + z_lo), core: 2. Of those that a mesh axis runs over, the one named last changes fastest.
Arguments:
- movie: bfloat16 [512, 2048, 256], P('row', 'col'), may hold values from 0 to 1.5
- footprints: float32 [8, 32, 12, 4096], P('row', 'col'), may hold values from 0.05 to 1
- anchors: int32 [8, 32, 12, 2], P('row', 'col'), may hold values from 0 to 63, as said below
- groups: int32 [8, 32, 12], P('row', 'col'), may hold values from 0 to 3, as said below
- counts: int32 [8, 32], P('row', 'col'), may hold values from 1 to 12, as said below
- temporal: float32 [8, 32, 12, 256], P('row', 'col'), may hold values from 0.2 to 2
- back_spatial: bfloat16 [2, 512, 2048], P(None, 'row', 'col'), may hold values from 0 to 0.5
- back_temporal: float32 [2, 256], replicated, may hold values from 0.5 to 1
- window: int32 [2], replicated, may hold values from 0 to 256, as said below
Outputs:
- new_footprints: float32 [8, 32, 12, 4096], P('row', 'col')
- new_traces: float32 [8, 32, 12, 256], P('row', 'col')
The draws below stay inside these ranges and needn't reach their ends.
Inputs may be any that keep to these rules, and one draw needn't show every extreme that they name: `anchors`: a block's anchor lies in its tile; on the last tile row the row offset is at most 0, on the last tile column the column offset at most 0. `counts`: slots below the count are live, the others are ignored; some tile has 12 live slots. `groups`: every tile has exactly 3 slots, live or not, in each group. window[0] is at most 64 and window[1] at least 192.
All inputs are finite; a program needn't handle non-finite values.
Results may differ from the reference program's by a relative error of at most 0.00084.
Values may be sent and summed in bfloat16 or wider, within the bound.
A program may use at most 64 MiB of HBM per device.

```python
import math
from functools import partial
import jax
import jax.numpy as jnp
from jax import lax

TH = 64
TW = 64
FRAMES = 256
FP = 64
MAXN = 12
GROUPS = 4
HEIGHT = 512
WIDTH = 2048
N_ROW = 8
N_COL = 32


def draw_anchors(key, part):
    grid_rows = HEIGHT // TH
    grid_cols = WIDTH // TW
    row_ids = jnp.arange(grid_rows, dtype=jnp.int32)[:, None, None]
    col_ids = jnp.arange(grid_cols, dtype=jnp.int32)[None, :, None]
    high_rows = jnp.broadcast_to(jnp.where(row_ids == grid_rows - 1, TH - FP + 1, TH), (grid_rows, grid_cols, MAXN))
    high_cols = jnp.broadcast_to(jnp.where(col_ids == grid_cols - 1, TW - FP + 1, TW), (grid_rows, grid_cols, MAXN))
    downs = jax.random.randint(jax.random.fold_in(key, 11), (grid_rows, grid_cols, MAXN), 0, high_rows)
    rights = jax.random.randint(jax.random.fold_in(key, 12), (grid_rows, grid_cols, MAXN), 0, high_cols)
    return jnp.stack([downs, rights], axis=-1).astype(jnp.int32)


def draw_groups(key, part):
    grid_rows = HEIGHT // TH
    grid_cols = WIDTH // TW
    slot_ids = jnp.arange(MAXN, dtype=jnp.int32)[None, None, :]
    scores = jax.random.randint(jax.random.fold_in(key, 41), (grid_rows, grid_cols, MAXN), 0, 1 << 20) * MAXN + slot_ids
    ordering = jnp.argsort(scores, axis=-1, stable=True)
    ranking = jnp.argsort(ordering, axis=-1, stable=True)
    return (ranking % GROUPS).astype(jnp.int32)


def draw_counts(key, part):
    grid_rows = HEIGHT // TH
    grid_cols = WIDTH // TW
    layout = (grid_rows, grid_cols)
    base = jax.random.randint(jax.random.fold_in(key, 21), layout, 1, min(MAXN // 2 + 3, MAXN + 1))
    crowded = jax.random.randint(jax.random.fold_in(key, 22), layout, 0, 8) == 0
    marked_at = jax.random.randint(jax.random.fold_in(key, 23), (), 0, grid_rows * grid_cols)
    marked = jnp.arange(grid_rows * grid_cols, dtype=jnp.int32).reshape(layout) == marked_at
    return jnp.where(crowded | marked, MAXN, base).astype(jnp.int32)


def draw_window(key, part):
    first = jax.random.randint(jax.random.fold_in(key, 31), (), 0, FRAMES // 4 + 1)
    last = jax.random.randint(jax.random.fold_in(key, 32), (), 3 * FRAMES // 4, FRAMES + 1)
    return jnp.stack([first, last]).astype(jnp.int32)


def block_scale(rng, shape, pieces, least, high):
    def one(axis_at, blocks):
        steps = jax.random.uniform(jax.random.fold_in(jax.random.fold_in(rng, 6), axis_at), (blocks,), jnp.float32, least / len(pieces), high / len(pieces))
        return jnp.repeat(jnp.exp(steps), shape[axis_at] // blocks).reshape((-1,) + (1,) * (len(shape) - axis_at - 1))

    loudness = one(*pieces[0])
    for cut in pieces[1:]:
        loudness = loudness * one(*cut)
    return loudness


def setup_inputs(seed: int = 0) -> dict:
    arg_keys = jax.random.split(jax.random.key(seed), 10)
    return {
        "movie": jnp.clip(1.5 * jax.random.uniform(arg_keys[0], (HEIGHT, WIDTH, FRAMES), jnp.float32) ** block_scale(arg_keys[0], (HEIGHT, WIDTH, FRAMES), ((0, 8), (1, 32)), -0.2, 0.2), 0.0, 1.5).astype(jnp.bfloat16),
        "footprints": jnp.clip(jnp.exp(math.log(1.0) - 2.9957323 * jax.random.uniform(arg_keys[1], (N_ROW, N_COL, MAXN, FP * FP), jnp.float32) ** block_scale(arg_keys[1], (N_ROW, N_COL, MAXN, FP * FP), ((0, 8), (1, 32)), -0.2, 0.2)), 0.05, 1.0),
        "anchors": draw_anchors(jax.random.fold_in(arg_keys[9], 71), 0),
        "groups": draw_groups(jax.random.fold_in(arg_keys[9], 71), 0),
        "counts": draw_counts(jax.random.fold_in(arg_keys[9], 71), 0),
        "temporal": jnp.clip(jnp.exp(math.log(2.0) - 2.3025851 * jax.random.uniform(arg_keys[5], (N_ROW, N_COL, MAXN, FRAMES), jnp.float32) ** block_scale(arg_keys[5], (N_ROW, N_COL, MAXN, FRAMES), ((0, 8), (1, 32)), -0.2, 0.2)), 0.2, 2.0),
        "back_spatial": jnp.clip(0.5 * jax.random.uniform(arg_keys[6], (2, HEIGHT, WIDTH), jnp.float32) ** block_scale(arg_keys[6], (2, HEIGHT, WIDTH), ((1, 8), (2, 32)), -0.2, 0.2), 0.0, 0.5).astype(jnp.bfloat16),
        "back_temporal": jnp.clip(jax.random.uniform(arg_keys[7], (2, FRAMES), jnp.float32, 0.5, 1.0), 0.5, 1.0),
        "window": draw_window(jax.random.fold_in(arg_keys[9], 71), 0),
    }


exact_mode = lax.Precision.HIGHEST


def grid_pad(values):
    widths = [(1, 1), (1, 1)] + [(0, 0)] * (values.ndim - 2)
    return jnp.pad(values, widths)


def near_block(padded, row_at, col_at):
    nought = jnp.zeros((), jnp.int32)
    starts = (row_at, col_at) + (nought,) * (padded.ndim - 2)
    return lax.dynamic_slice(padded, starts, (3, 3) + padded.shape[2:])


def place_block(block, top_row, left_col, height, width):
    sheet = jnp.zeros((height + 2 * FP, width + 2 * FP), jnp.float32)
    within = ((top_row >= -FP) & (top_row <= height) & (left_col >= -FP) & (left_col <= width)).astype(jnp.float32)
    at_row = jnp.clip(top_row + FP, 0, height + FP).astype(jnp.int32)
    at_col = jnp.clip(left_col + FP, 0, width + FP).astype(jnp.int32)
    sheet = lax.dynamic_update_slice(sheet, block * within, (at_row, at_col))
    return sheet[FP:FP + height, FP:FP + width]


def lift_block(values, top_row, left_col, height, width):
    padded = jnp.pad(values, FP)
    within = ((top_row >= -FP) & (left_col >= -FP)).astype(jnp.float32)
    at_row = jnp.clip(top_row + FP, 0, height + FP).astype(jnp.int32)
    at_col = jnp.clip(left_col + FP, 0, width + FP).astype(jnp.int32)
    return lax.dynamic_slice(padded, (at_row, at_col), (FP, FP)) * within


def reference(movie, footprints, anchors, groups, counts, temporal, back_spatial, back_temporal, window):
    living = (jnp.arange(MAXN, dtype=jnp.int32)[None, None, :] < counts[:, :, None]).astype(jnp.float32)
    shapes = footprints * living[..., None]
    shape_grid = grid_pad(shapes)
    anchor_grid = grid_pad(anchors)
    group_grid = grid_pad(groups)
    living_grid = grid_pad(living)
    trace_grid = grid_pad(temporal)
    movie_padded = jnp.pad(movie, ((0, FP), (0, FP), (0, 0)))
    back_padded = jnp.pad(back_spatial, ((0, 0), (0, FP), (0, FP)))
    moments = jnp.arange(FRAMES, dtype=jnp.int32)
    inside = ((moments >= window[0]) & (moments < window[1])).astype(jnp.float32)
    tile_step = jnp.arange(3, dtype=jnp.int32) - 1
    nought = jnp.zeros((), jnp.int32)

    def tile_work(index):
        row_at = (index // N_COL).astype(jnp.int32)
        col_at = (index % N_COL).astype(jnp.int32)
        near_shape = near_block(shape_grid, row_at, col_at).reshape(9 * MAXN, FP, FP)
        near_anchor = near_block(anchor_grid, row_at, col_at)
        top_rows = (near_anchor[..., 0] + tile_step[:, None, None] * TH).reshape(9 * MAXN)
        left_cols = (near_anchor[..., 1] + tile_step[None, :, None] * TW).reshape(9 * MAXN)
        near_group = near_block(group_grid, row_at, col_at)[:2, :2].reshape(4 * MAXN)
        near_living = near_block(living_grid, row_at, col_at)[:2, :2].reshape(4 * MAXN)
        canvas = jax.vmap(partial(place_block, height=TH + FP, width=TW + FP))(near_shape, top_rows, left_cols)
        flattened = canvas.reshape(9 * MAXN, (TH + FP) * (TW + FP))
        owned = flattened[4 * MAXN:5 * MAXN]
        coupling = jnp.dot(owned, flattened.T, precision=exact_mode)
        movie_ext = lax.dynamic_slice(movie_padded, (row_at * TH, col_at * TW, nought), (TH + FP, TW + FP, FRAMES))
        movie_ext = movie_ext.astype(jnp.float32).reshape((TH + FP) * (TW + FP), FRAMES)
        back_ext = lax.dynamic_slice(back_padded, (nought, row_at * TH, col_at * TW), (2, TH + FP, TW + FP))
        back_ext = back_ext.astype(jnp.float32).reshape(2, (TH + FP) * (TW + FP))
        rounded = lax.optimization_barrier(owned.astype(jnp.bfloat16)).astype(jnp.float32)
        loadings = jnp.dot(owned, back_ext.T, precision=exact_mode)
        drives = jnp.dot(rounded, movie_ext, precision=exact_mode) - jnp.dot(loadings, back_temporal, precision=exact_mode)

        tile_canvas = canvas.reshape(3, 3, MAXN, TH + FP, TW + FP)[:2, :2, :, :TH, :TW].reshape(4 * MAXN, TH * TW)
        tile_top = top_rows.reshape(3, 3, MAXN)[:2, :2].reshape(4 * MAXN)
        tile_left = left_cols.reshape(3, 3, MAXN)[:2, :2].reshape(4 * MAXN)
        ones = jnp.ones((4 * MAXN, FP, FP), jnp.float32)
        cover = jax.vmap(partial(place_block, height=TH, width=TW))(ones, tile_top, tile_left).reshape(4 * MAXN, TH * TW)
        cover = cover * near_living[:, None]
        tile_traces = near_block(trace_grid, row_at, col_at)[:2, :2].reshape(4 * MAXN, FRAMES)
        weighted = tile_traces * inside[None, :]
        intersection_time = jnp.dot(weighted, weighted.T, precision=exact_mode)
        masses = jnp.diagonal(intersection_time)
        safe_mass = jnp.where(near_living > 0, masses, 1.0)
        tile_movie = lax.dynamic_slice(movie, (row_at * TH, col_at * TW, nought), (TH, TW, FRAMES))
        tile_movie = tile_movie.astype(jnp.float32).reshape(TH * TW, FRAMES)
        tile_back = lax.dynamic_slice(back_spatial, (nought, row_at * TH, col_at * TW), (2, TH, TW))
        tile_back = tile_back.astype(jnp.float32).reshape(2, TH * TW)
        trace_round = lax.optimization_barrier(weighted.astype(jnp.bfloat16)).astype(jnp.float32)
        back_loads = jnp.dot(weighted, back_temporal.T, precision=exact_mode)
        target = jnp.dot(trace_round, tile_movie.T, precision=exact_mode) - jnp.dot(back_loads, tile_back, precision=exact_mode)
        values = tile_canvas
        for step in range(GROUPS):
            coupled = jnp.dot(intersection_time, values, precision=exact_mode)
            chosen = cover * (near_group == step).astype(jnp.float32)[:, None]
            updated = jnp.maximum(values + (target - coupled) / safe_mass[:, None], 0.0)
            values = jnp.where(chosen > 0, updated, values)
        blocks = jax.vmap(partial(lift_block, height=TH, width=TW))(values.reshape(4 * MAXN, TH, TW), tile_top, tile_left)
        return drives, coupling, blocks.reshape(2, 2, MAXN, FP * FP)

    drives, couplings, blocks = lax.map(tile_work, jnp.arange(N_ROW * N_COL, dtype=jnp.int32))
    drives = drives.reshape(N_ROW, N_COL, MAXN, FRAMES)
    couplings = couplings.reshape(N_ROW, N_COL, MAXN, 9 * MAXN)
    blocks = blocks.reshape(N_ROW, N_COL, 2, 2, MAXN, FP * FP)
    padded = jnp.pad(blocks, ((0, 1), (0, 1), (0, 0), (0, 0), (0, 0), (0, 0)))
    new_shapes = padded[:-1, :-1, 1, 1] + padded[:-1, 1:, 1, 0] + padded[1:, :-1, 0, 1] + padded[1:, 1:, 0, 0]
    self_weight = jnp.diagonal(couplings[..., 4 * MAXN:5 * MAXN], axis1=2, axis2=3)
    safe_self = jnp.where(living > 0, self_weight, 1.0)
    traces = temporal
    for step in range(GROUPS):
        grid = grid_pad(traces)
        nearby = jnp.stack([grid[down_at:down_at + N_ROW, right_at:right_at + N_COL] for down_at in range(3) for right_at in range(3)], axis=2)
        nearby = nearby.reshape(N_ROW, N_COL, 9 * MAXN, FRAMES)
        coupled = jnp.einsum('rcnm,rcmt->rcnt', couplings, nearby, precision=exact_mode)
        chosen = living * (groups == step).astype(jnp.float32)
        updated = jnp.maximum(traces + (drives - coupled) / safe_self[..., None], 0.0)
        traces = jnp.where(chosen[..., None] > 0, updated, traces)
    return new_shapes, traces
```

```python
import functools

import jax
import jax.numpy as jnp
from jax import lax
from jax.experimental import pallas as pl
from jax.experimental.pallas import tpu as pltpu
from jax.sharding import PartitionSpec as P

MESH = pl.DeviceIdType.MESH
F32 = jnp.float32
BF16 = jnp.bfloat16
I32 = jnp.int32
I16 = jnp.int16

SIDE = 64
PIX = SIDE * SIDE
FRAMES = 256
SLOTS = 12
GROUPS = 4
PAD = 16
NEAR = 4 * PAD
BIG = 1e30
TOP = 8.0

DIRS = ((-1, -1), (-1, 0), (-1, 1), (0, -1), (0, 1), (1, -1), (1, 0), (1, 1))
UL, UP, UR, LEFT, RIGHT, DL, DOWN, DR = range(8)
OWN = 8
TILE_SETS = (
    (UL, UP, LEFT, OWN),
    (UP, UR, OWN, RIGHT),
    (LEFT, OWN, DL, DOWN),
    (OWN, RIGHT, DOWN, DR),
)
SELF_AT = (3, 2, 1, 0)


def nt(a, b):
    return lax.dot_general(a, b, (((1,), (1,)), ((), ())), preferred_element_type=F32)


def mm(a, b):
    return jnp.dot(a, b, preferred_element_type=F32)


def split(x):
    high = x.astype(BF16)
    return high, (x - high.astype(F32)).astype(BF16)


def turn(x, shift, forward):
    for bit in range(12):
        step = 1 << bit
        chosen = ((shift >> bit) & 1) == 1
        by = step if forward else PIX - step
        if by % 128 == 0:
            moved = jnp.concatenate([x[:, PIX - by :], x[:, : PIX - by]], axis=1)
        else:
            moved = pltpu.roll(x, by, 1)
        x = jnp.where(chosen, moved, x)
    return x


def half_turn(x, forward):
    return pltpu.roll(x, SIDE if forward else PIX - SIDE, 1)


def kernel(
    rows, cols,
    anchors, groups, counts, window,
    footprints, temporal, back, back_time, movie_hbm,
    out_shapes, out_traces,
    movie, pad_f, hl, code, r_code, cm, r_cm, near_cm, target, canvas, x3,
    shares, share_out, r_share, wave, r_wave, call_f, c_high, c_low, temp,
    piece_up, r_piece, merged, r_merged,
    movie_sem, cm_send, cm_recv, r_send, r_recv, s_send, s_recv, t_send, t_recv, p_send, p_recv, m_send, m_recv,
):
    r = lax.axis_index("row")
    c = lax.axis_index("col")

    def there(d):
        down, right = DIRS[d]
        ok = None
        for at, step, count in ((r, down, rows), (c, right, cols)):
            if step:
                one = at + step >= 0 if step < 0 else at + step < count
                ok = one if ok is None else ok & one
        return ok

    def place(d):
        return (r + DIRS[d][0], c + DIRS[d][1])

    barrier = pltpu.get_barrier_semaphore()

    r_cm[...] = jnp.zeros_like(r_cm)
    r_share[...] = jnp.zeros_like(r_share)
    r_wave[...] = jnp.zeros_like(r_wave)

    expected = 0
    for d in range(8):
        ok = there(d)

        @pl.when(ok)
        def _(d=d):
            pl.semaphore_signal(barrier, inc=1, device_id=place(d), device_id_type=MESH)

        expected = expected + ok.astype(I32)

    load_movie = pltpu.make_async_copy(movie_hbm, movie, movie_sem)
    load_movie.start()

    sub = lax.broadcasted_iota(I32, (PAD, 128), 0)
    lane = lax.broadcasted_iota(I32, (PAD, 128), 1)
    g_sub = jnp.full((PAD, 128), -1, I32)
    g_lane = jnp.full((PAD, 128), -1, I32)
    a_lane = jnp.zeros((PAD, 128), I32)
    b_lane = jnp.zeros((PAD, 128), I32)
    count = counts[0, 0]
    for m in range(SLOTS):
        g_sub = jnp.where(sub == m, groups[0, 0, m], g_sub)
        g_lane = jnp.where(lane == m, groups[0, 0, m], g_lane)
        a_lane = jnp.where(lane == m, anchors[0, 0, m, 0], a_lane)
        b_lane = jnp.where(lane == m, anchors[0, 0, m, 1], b_lane)
    alive_lane = lane < count
    alive_sub = sub < count
    a_lane = jnp.where(alive_lane, a_lane, 0)
    b_lane = jnp.where(alive_lane, b_lane, 0)
    same = g_sub == g_lane
    before_lane = jnp.sum(jnp.where(same & (sub < lane), 1.0, 0.0), axis=0, keepdims=True)
    before_sub = jnp.sum(jnp.where(same & (lane < sub), 1.0, 0.0), axis=1, keepdims=True)
    pos_lane = g_lane.astype(F32) * 4.0 + before_lane
    pos_sub = g_sub.astype(F32) * 4.0 + before_sub
    pick = jnp.where((sub.astype(F32) == pos_lane) & (lane < SLOTS), 1.0, 0.0)
    unpick = jnp.where((lane.astype(F32) == pos_sub) & (sub < SLOTS), 1.0, 0.0)
    a_own = jnp.sum(pick * a_lane.astype(F32), axis=1, keepdims=True)
    b_own = jnp.sum(pick * b_lane.astype(F32), axis=1, keepdims=True)
    live_own = jnp.sum(pick * jnp.where(alive_lane, 1.0, 0.0), axis=1, keepdims=True)
    shift_own = (a_own * float(SIDE) + b_own).astype(I32)
    pick16 = pick[:, :PAD]
    unpick16 = unpick[:, :PAD]

    pad_f[SLOTS:PAD, :] = jnp.zeros((PAD - SLOTS, PIX), F32)
    pad_f[:SLOTS, :FRAMES] = temporal[...]
    cm[:, :FRAMES] = jnp.dot(pick16, pad_f[:, :FRAMES], precision=lax.Precision.HIGHEST, preferred_element_type=F32)
    cm[:, FRAMES:] = jnp.where(lane == 0, a_own, jnp.where(lane == 1, b_own, jnp.where(lane == 2, live_own, 0.0)))

    pad_f[:SLOTS, :] = footprints[...]
    whole = jnp.floor(pad_f[...] * 65535.0 + 0.5)
    upper = jnp.floor(whole * (1.0 / 256.0))
    hl[:PAD, :] = upper.astype(BF16)
    hl[PAD:, :] = (whole - upper * 256.0).astype(BF16)
    pick_hl = jnp.concatenate([pick16 * 256.0, pick16], axis=1).astype(BF16)
    pad_f[...] = mm(pick_hl, hl[...])
    for half in range(2):
        part = slice(half * 8, half * 8 + 8)
        pad_f[part, :] = turn(pad_f[part, :], shift_own[part], True)
    code[...] = (pad_f[...] - 32768.0).astype(I32).astype(I16)

    pl.semaphore_wait(barrier, expected)

    def remote(src, dst, send, recv, d):
        return pltpu.make_async_remote_copy(
            src_ref=src, dst_ref=dst, send_sem=send, recv_sem=recv, device_id=place(d), device_id_type=MESH
        )

    pending = []

    def start(copy, ok):
        @pl.when(ok)
        def _():
            copy.start()

        pending.append((copy, ok))

    def arrived(copy, ok):
        @pl.when(ok)
        def _():
            copy.wait_recv()

    def cm_copy(src, slot, d):
        return remote(src, r_cm.at[slot], cm_send.at[slot], cm_recv.at[slot], d)

    for d in (RIGHT, LEFT, DOWN, UP):
        start(cm_copy(cm, 7 - d, d), there(d))
    start(remote(code, r_code.at[2], r_send.at[2], r_recv.at[2], RIGHT), there(RIGHT))
    start(remote(code, r_code.at[1], r_send.at[1], r_recv.at[1], DOWN), there(DOWN))

    arrived(cm_copy(cm, LEFT, LEFT), there(LEFT))
    start(cm_copy(r_cm.at[LEFT], DL, UP), there(UP) & there(LEFT))
    start(cm_copy(r_cm.at[LEFT], UL, DOWN), there(DOWN) & there(LEFT))
    arrived(cm_copy(cm, RIGHT, RIGHT), there(RIGHT))
    start(cm_copy(r_cm.at[RIGHT], DR, UP), there(UP) & there(RIGHT))
    start(cm_copy(r_cm.at[RIGHT], UR, DOWN), there(DOWN) & there(RIGHT))
    for d in (UP, UL, DOWN, UR, DL, DR):
        arrived(cm_copy(cm, d, d), there(d))

    def cm_of(tile, rows_at, lanes_at):
        if tile == OWN:
            return cm[rows_at, lanes_at]
        return r_cm[tile, rows_at, lanes_at]

    for g in range(GROUPS):
        for t in range(4):
            at = slice(g * PAD + t * 4, g * PAD + t * 4 + 4)
            near_cm[at, :] = cm_of(TILE_SETS[0][t], slice(g * 4, g * 4 + 4), slice(None))
    for k in range(4):
        for g in range(GROUPS):
            for t in range(4):
                at = slice(k * NEAR + g * PAD + t * 4, k * NEAR + g * PAD + t * 4 + 4)
                call_f[at, :] = cm_of(TILE_SETS[k][t], slice(g * 4, g * 4 + 4), slice(0, FRAMES))
    high, low = split(call_f[...])
    c_high[...] = high
    c_low[...] = low

    frame = lax.broadcasted_iota(I32, (NEAR, FRAMES), 1)
    weighted = jnp.where((frame >= window[0]) & (frame < window[1]), near_cm[:, :FRAMES], 0.0)
    w_high, w_low = split(weighted)
    w_both = jnp.concatenate([w_high, w_low], axis=0)
    q4 = nt(w_both, w_both)
    q = q4[:NEAR, :NEAR] + q4[:NEAR, NEAR:] + q4[NEAR:, :NEAR] + q4[NEAR:, NEAR:]
    a_near = near_cm[:, FRAMES : FRAMES + 1].astype(I32)
    b_near = near_cm[:, FRAMES + 1 : FRAMES + 2].astype(I32)
    live_near = near_cm[:, FRAMES + 2 : FRAMES + 3]
    eye = lax.broadcasted_iota(I32, (NEAR, NEAR), 0) == lax.broadcasted_iota(I32, (NEAR, NEAR), 1)
    mass = jnp.sum(jnp.where(eye, q, 0.0), axis=1, keepdims=True)
    inverse = 1.0 / jnp.where(live_near > 0, mass, 1.0)
    q_high, q_low = split(jnp.where(eye, 0.0, q) * inverse)
    q3 = jnp.concatenate([q_high, q_high, q_low], axis=1)
    load0 = jnp.sum(weighted * back_time[0:1, :], axis=1, keepdims=True)
    load1 = jnp.sum(weighted * back_time[1:2, :], axis=1, keepdims=True)

    tile_at = (lax.broadcasted_iota(I32, (NEAR, 1), 0) >> 2) & 3
    above = tile_at < 2
    aside = (tile_at & 1) == 0
    y_low = jnp.where(above, 0, a_near)
    y_high = jnp.where(live_near > 0, jnp.where(above, a_near, SIDE), 0)
    x_low = jnp.where(aside, 0, b_near)
    x_high = jnp.where(aside, b_near, SIDE)

    def covered(rows_at, begin, width):
        spot = lax.broadcasted_iota(I32, (1, width), 1) + begin
        y = spot >> 6
        x = spot & 63
        return (
            (y >= y_low[rows_at]) & (y < y_high[rows_at]) & (x >= x_low[rows_at]) & (x < x_high[rows_at])
        )

    load_movie.wait()
    width = 1024
    for begin in range(0, PIX, width):
        at = slice(begin, begin + width)
        pull = nt(w_high, movie[at, :])
        pull = pull - load0 * back[0:1, at].astype(F32) - load1 * back[1:2, at].astype(F32)
        target[:, at] = jnp.where(covered(slice(None), begin, width), pull * inverse, -BIG)

    arrived(remote(code, r_code.at[2], r_send.at[2], r_recv.at[2], LEFT), there(LEFT))
    start(remote(r_code.at[2], r_code.at[0], r_send.at[0], r_recv.at[0], DOWN), there(DOWN) & there(LEFT))
    arrived(remote(code, r_code.at[1], r_send.at[1], r_recv.at[1], UP), there(UP))
    arrived(remote(code, r_code.at[0], r_send.at[0], r_recv.at[0], UL), there(UL))
    for t in (0, 1, 2, 3):
        coded = (r_code[t] if t < 3 else code[...]).astype(I32).astype(F32)
        if t in (0, 2):
            coded = half_turn(coded, False)
        for g in range(GROUPS):
            canvas[g * PAD + t * 4 : g * PAD + t * 4 + 4, :] = coded[g * 4 : g * 4 + 4, :]
    for g in range(GROUPS):
        rows_at = slice(g * PAD, g * PAD + PAD)
        value = jnp.where(covered(rows_at, 0, PIX), (canvas[rows_at, :] + 32768.0) * (1.0 / 65535.0), 0.0)
        high, low = split(value)
        x3[g * PAD : g * PAD + PAD, :] = high
        x3[NEAR + g * PAD : NEAR + g * PAD + PAD, :] = low
        x3[2 * NEAR + g * PAD : 2 * NEAR + g * PAD + PAD, :] = high

    both = x3[: 2 * NEAR, :]
    gram = nt(both, both)
    overlap = gram[:NEAR, :NEAR] + gram[:NEAR, NEAR:] + gram[NEAR:, :NEAR] + gram[NEAR:, NEAR:]
    loading = nt(both, back[...])
    loading = loading[:NEAR] + loading[NEAR:]
    drive = mm(x3[:NEAR, :], movie[...])
    drive = drive - loading[:, 0:1] * back_time[0:1, :] - loading[:, 1:2] * back_time[1:2, :]
    shares[:, :FRAMES] = drive
    shares[:, FRAMES : FRAMES + NEAR] = overlap
    shares[:, FRAMES + NEAR :] = jnp.zeros((NEAR, 128 - NEAR), F32)
    for t in range(4):
        for g in range(GROUPS):
            share_out[t, g * 4 : g * 4 + 4, :] = shares[g * PAD + t * 4 : g * PAD + t * 4 + 4, :]

    def share_copy(t, d):
        return remote(share_out.at[t], r_share.at[t], s_send.at[t], s_recv.at[t], d)

    for t, d in ((0, UL), (2, LEFT), (1, UP)):
        start(share_copy(t, d), there(d))

    for g in range(GROUPS):
        rows_at = slice(g * PAD, g * PAD + PAD)
        value = jnp.maximum(target[rows_at, :] - mm(q3[rows_at, :], x3[...]), 0.0)
        canvas[rows_at, :] = jnp.floor(jnp.sqrt(value * (1.0 / TOP)) * 65535.0 + 0.5) - 32768.0
        if g < GROUPS - 1:
            high, low = split(value)
            x3[g * PAD : g * PAD + PAD, :] = high
            x3[NEAR + g * PAD : NEAR + g * PAD + PAD, :] = low
            x3[2 * NEAR + g * PAD : 2 * NEAR + g * PAD + PAD, :] = high

    def gather_tile(t):
        for g in range(GROUPS):
            temp[g * 4 : g * 4 + 4, :] = canvas[g * PAD + t * 4 : g * PAD + t * 4 + 4, :]
        return temp[...]

    for t in range(2):
        piece_up[t] = gather_tile(t).astype(I32).astype(I16)

    def piece_copy(t, d):
        return remote(piece_up.at[t], r_piece.at[t], p_send.at[t], p_recv.at[t], d)

    for t in range(2):
        start(piece_copy(t, UP), there(UP))

    for t, d in ((2, RIGHT), (1, DOWN), (0, DR)):
        arrived(share_copy(t, d), there(d))
    parts = [share_out[3], r_share[2], r_share[1], r_share[0]]
    drive = parts[0][:, :FRAMES] + parts[1][:, :FRAMES] + parts[2][:, :FRAMES] + parts[3][:, :FRAMES]
    near_lane = lax.broadcasted_iota(I32, (PAD, NEAR), 1)
    near_row = lax.broadcasted_iota(I32, (PAD, NEAR), 0)
    lane_row = ((near_lane >> 4) << 2) + (near_lane & 3)
    lane_tile = (near_lane >> 2) & 3
    weight = jnp.zeros((PAD, 1), F32)
    others = []
    for k in range(4):
        v = parts[k][:, FRAMES : FRAMES + NEAR]
        mine = (lane_tile == SELF_AT[k]) & (lane_row == near_row)
        weight = weight + jnp.sum(jnp.where(mine, v, 0.0), axis=1, keepdims=True)
        others.append(jnp.where(mine, 0.0, v))
    scale = 1.0 / jnp.where(live_own > 0, weight, 1.0)
    v_high, v_low = split(jnp.concatenate(others, axis=1) * scale)
    v_both = jnp.concatenate([v_high, v_low], axis=0)
    goal = drive * scale
    own = cm[:, :FRAMES]
    row_group = lax.broadcasted_iota(I32, (PAD, FRAMES), 0) >> 2

    def wave_copy(g, d, slot):
        return remote(wave.at[g], r_wave.at[g, slot], t_send.at[g, slot], t_recv.at[g, slot], d)

    for g in range(GROUPS):
        if g > 0:
            for d in range(8):
                arrived(wave_copy(g - 1, d, d), there(d))
            for k in range(4):
                for t in range(4):
                    tile = TILE_SETS[k][t]
                    new = wave[g - 1] if tile == OWN else r_wave[g - 1, tile]
                    at = slice(k * NEAR + (g - 1) * PAD + t * 4, k * NEAR + (g - 1) * PAD + t * 4 + 4)
                    call_f[at, :128] = new[:4, :]
                    call_f[at, 128:] = new[4:, :]
                at = slice(k * NEAR + (g - 1) * PAD, k * NEAR + g * PAD)
                high, low = split(call_f[at, :])
                c_high[at, :] = high
                c_low[at, :] = low
        product = mm(v_both, c_high[...])
        coupled = product[:PAD] + product[PAD:] + mm(v_high, c_low[...])
        chosen = (row_group == g) & (live_own > 0)
        own = jnp.where(chosen, jnp.maximum(goal - coupled, 0.0), own)
        if g < GROUPS - 1:
            wave[g, :4, :] = own[g * 4 : g * 4 + 4, :128]
            wave[g, 4:, :] = own[g * 4 : g * 4 + 4, 128:]
            for d in (UR, DR, UL, DL, RIGHT, LEFT, UP, DOWN):
                start(wave_copy(g, d, 7 - d), there(d))
        if g == 0:
            for t in range(2):
                arrived(piece_copy(t, DOWN), there(DOWN))
            spot = lax.broadcasted_iota(I32, (PAD, PIX), 1)
            a_left = r_cm[LEFT, :, FRAMES : FRAMES + 1].astype(I32)
            below = (spot >> 6) < a_left
            merged[...] = jnp.where(below, r_piece[0].astype(I32), gather_tile(2).astype(I32)).astype(I16)
            start(remote(merged, r_merged, m_send, m_recv, LEFT), there(LEFT))

    back_own = jnp.dot(unpick16, own, precision=lax.Precision.HIGHEST, preferred_element_type=F32)
    out_traces[...] = jnp.where(alive_sub[:SLOTS, 0:1], back_own[:SLOTS, :], temporal[...])

    arrived(remote(merged, r_merged, m_send, m_recv, RIGHT), there(RIGHT))
    y = spot >> 6
    x = spot & 63
    a_int = a_own.astype(I32)
    b_int = b_own.astype(I32)
    far = half_turn(r_merged[...].astype(I32).astype(F32), True)
    near = jnp.where(y < a_int, r_piece[1].astype(I32).astype(F32), gather_tile(3))
    pad_f[...] = jnp.where(x < b_int, far, near) + 32768.0
    for half in range(2):
        part = slice(half * 8, half * 8 + 8)
        pad_f[part, :] = turn(pad_f[part, :], shift_own[part], False)
    whole = pad_f[...]
    upper = jnp.floor(whole * (1.0 / 256.0))
    hl[:PAD, :] = upper.astype(BF16)
    hl[PAD:, :] = (whole - upper * 256.0).astype(BF16)
    unpick_hl = jnp.concatenate([unpick16 * 256.0, unpick16], axis=1).astype(BF16)
    root = mm(unpick_hl, hl[...])[:SLOTS, :] * (1.0 / 65535.0)
    out_shapes[...] = root * root * TOP

    for copy, ok in pending:
        @pl.when(ok)
        def _(copy=copy):
            copy.wait_send()


def on_device(rows, cols, movie, footprints, anchors, groups, counts, temporal, back_spatial, back_temporal, window):
    vmem = pl.BlockSpec(memory_space=pltpu.VMEM)
    smem = pl.BlockSpec(memory_space=pltpu.SMEM)
    dma = pltpu.SemaphoreType.DMA
    shapes, traces = pl.pallas_call(
        functools.partial(kernel, rows, cols),
        out_shape=(
            jax.ShapeDtypeStruct((SLOTS, PIX), F32),
            jax.ShapeDtypeStruct((SLOTS, FRAMES), F32),
        ),
        in_specs=[smem] * 4 + [vmem] * 4 + [pl.BlockSpec(memory_space=pl.ANY)],
        out_specs=(vmem, vmem),
        scratch_shapes=[
            pltpu.VMEM((PIX, FRAMES), BF16),
            pltpu.VMEM((PAD, PIX), F32),
            pltpu.VMEM((2 * PAD, PIX), BF16),
            pltpu.VMEM((PAD, PIX), I16),
            pltpu.VMEM((3, PAD, PIX), I16),
            pltpu.VMEM((PAD, FRAMES + 128), F32),
            pltpu.VMEM((8, PAD, FRAMES + 128), F32),
            pltpu.VMEM((NEAR, FRAMES + 128), F32),
            pltpu.VMEM((NEAR, PIX), F32),
            pltpu.VMEM((NEAR, PIX), F32),
            pltpu.VMEM((3 * NEAR, PIX), BF16),
            pltpu.VMEM((NEAR, FRAMES + 128), F32),
            pltpu.VMEM((4, PAD, FRAMES + 128), F32),
            pltpu.VMEM((3, PAD, FRAMES + 128), F32),
            pltpu.VMEM((3, 8, 128), F32),
            pltpu.VMEM((3, 8, 8, 128), F32),
            pltpu.VMEM((4 * NEAR, FRAMES), F32),
            pltpu.VMEM((4 * NEAR, FRAMES), BF16),
            pltpu.VMEM((4 * NEAR, FRAMES), BF16),
            pltpu.VMEM((PAD, PIX), F32),
            pltpu.VMEM((2, PAD, PIX), I16),
            pltpu.VMEM((2, PAD, PIX), I16),
            pltpu.VMEM((PAD, PIX), I16),
            pltpu.VMEM((PAD, PIX), I16),
            dma,
            dma((8,)),
            dma((8,)),
            dma((3,)),
            dma((3,)),
            dma((3,)),
            dma((3,)),
            dma((3, 8)),
            dma((3, 8)),
            dma((2,)),
            dma((2,)),
            dma,
            dma,
        ],
        compiler_params=pltpu.CompilerParams(collective_id=0, has_side_effects=True, vmem_limit_bytes=48 << 20),
    )(
        anchors,
        groups,
        counts,
        window,
        footprints.reshape(SLOTS, PIX),
        temporal.reshape(SLOTS, FRAMES),
        back_spatial.reshape(2, PIX),
        back_temporal,
        movie.reshape(PIX, FRAMES),
    )
    return shapes[None, None], traces[None, None]


def solution(mesh):
    return jax.shard_map(
        functools.partial(on_device, mesh.shape["row"], mesh.shape["col"]),
        mesh=mesh,
        in_specs=(
            P("row", "col", None),
            P("row", "col", None, None),
            P("row", "col", None, None),
            P("row", "col", None),
            P("row", "col"),
            P("row", "col", None, None),
            P(None, "row", "col"),
            P(),
            P(),
        ),
        out_specs=(P("row", "col", None, None), P("row", "col", None, None)),
        check_vma=False,
    )
```

```python
import functools

import jax
import jax.numpy as jnp
from jax import lax
from jax.experimental import pallas as pl
from jax.experimental.pallas import tpu as pltpu
from jax.sharding import PartitionSpec as P

MESH = pl.DeviceIdType.MESH
F32 = jnp.float32
BF16 = jnp.bfloat16
I32 = jnp.int32
I16 = jnp.int16

SIDE = 64
PIX = SIDE * SIDE
FRAMES = 256
SLOTS = 12
GROUPS = 4
PAD = 16
NEAR = 4 * PAD
BIG = 1e30
TOP = 8.0

DIRS = ((-1, -1), (-1, 0), (-1, 1), (0, -1), (0, 1), (1, -1), (1, 0), (1, 1))
UL, UP, UR, LEFT, RIGHT, DL, DOWN, DR = range(8)
OWN = 8
TILE_SETS = (
    (UL, UP, LEFT, OWN),
    (UP, UR, OWN, RIGHT),
    (LEFT, OWN, DL, DOWN),
    (OWN, RIGHT, DOWN, DR),
)
SELF_AT = (3, 2, 1, 0)


def nt(a, b):
    return lax.dot_general(a, b, (((1,), (1,)), ((), ())), preferred_element_type=F32)


def mm(a, b):
    return jnp.dot(a, b, preferred_element_type=F32)


def split(x):
    high = x.astype(BF16)
    return high, (x - high.astype(F32)).astype(BF16)


def turn(x, shift, forward):
    for bit in range(12):
        step = 1 << bit
        chosen = ((shift >> bit) & 1) == 1
        by = step if forward else PIX - step
        if by % 128 == 0:
            moved = jnp.concatenate([x[:, PIX - by :], x[:, : PIX - by]], axis=1)
        else:
            moved = pltpu.roll(x, by, 1)
        x = jnp.where(chosen, moved, x)
    return x


def half_turn(x, forward):
    return pltpu.roll(x, SIDE if forward else PIX - SIDE, 1)


def kernel(
    rows, cols,
    anchors_in, groups_in, counts_in, window_in, footprints_in, temporal_in, back_in, back_time_in, movie_in,
    out_shapes, out_traces,
    anchors, groups, counts, window, footprints, temporal, back_raw, back_time, movie, back_even, back, pad_f, hl, code, r_code, cm, r_cm, near_cm, target, canvas, x3,
    shares, share_out, r_share, wave, r_wave, call_f, c_high, c_low, temp,
    piece_up, r_piece, merged, r_merged,
    load_sem, cm_send, cm_recv, r_send, r_recv, s_send, s_recv, t_send, t_recv, p_send, p_recv, m_send, m_recv,
):
    r = lax.axis_index("row")
    c = lax.axis_index("col")

    def there(d):
        down, right = DIRS[d]
        ok = None
        for at, step, count in ((r, down, rows), (c, right, cols)):
            if step:
                one = at + step >= 0 if step < 0 else at + step < count
                ok = one if ok is None else ok & one
        return ok

    def place(d):
        return (r + DIRS[d][0], c + DIRS[d][1])

    barrier = pltpu.get_barrier_semaphore()

    loads = [
        pltpu.make_async_copy(source, target_ref, load_sem.at[at])
        for at, (source, target_ref) in enumerate(
            (
                (groups_in, groups),
                (anchors_in, anchors),
                (counts_in, counts),
                (window_in, window),
                (temporal_in, temporal),
                (footprints_in, footprints),
                (back_time_in, back_time),
                (back_in, back_raw),
                (movie_in, movie),
            )
        )
    ]
    for load in loads:
        load.start()

    r_cm[...] = jnp.zeros_like(r_cm)
    r_share[...] = jnp.zeros_like(r_share)
    r_wave[...] = jnp.zeros_like(r_wave)

    expected = 0
    for d in range(8):
        ok = there(d)

        @pl.when(ok)
        def _(d=d):
            pl.semaphore_signal(barrier, inc=1, device_id=place(d), device_id_type=MESH)

        expected = expected + ok.astype(I32)

    for load in loads[:5]:
        load.wait()
    sub = lax.broadcasted_iota(I32, (PAD, 128), 0)
    lane = lax.broadcasted_iota(I32, (PAD, 128), 1)
    g_sub = jnp.full((PAD, 128), -1, I32)
    g_lane = jnp.full((PAD, 128), -1, I32)
    a_lane = jnp.zeros((PAD, 128), I32)
    b_lane = jnp.zeros((PAD, 128), I32)
    count = counts[0, 0]
    for m in range(SLOTS):
        g_sub = jnp.where(sub == m, groups[0, m], g_sub)
        g_lane = jnp.where(lane == m, groups[0, m], g_lane)
        a_lane = jnp.where(lane == m, anchors[0, m], a_lane)
        b_lane = jnp.where(lane == m, anchors[1, m], b_lane)
    alive_lane = lane < count
    alive_sub = sub < count
    a_lane = jnp.where(alive_lane, a_lane, 0)
    b_lane = jnp.where(alive_lane, b_lane, 0)
    same = g_sub == g_lane
    before_lane = jnp.sum(jnp.where(same & (sub < lane), 1.0, 0.0), axis=0, keepdims=True)
    before_sub = jnp.sum(jnp.where(same & (lane < sub), 1.0, 0.0), axis=1, keepdims=True)
    pos_lane = g_lane.astype(F32) * 4.0 + before_lane
    pos_sub = g_sub.astype(F32) * 4.0 + before_sub
    pick = jnp.where((sub.astype(F32) == pos_lane) & (lane < SLOTS), 1.0, 0.0)
    unpick = jnp.where((lane.astype(F32) == pos_sub) & (sub < SLOTS), 1.0, 0.0)
    a_own = jnp.sum(pick * a_lane.astype(F32), axis=1, keepdims=True)
    b_own = jnp.sum(pick * b_lane.astype(F32), axis=1, keepdims=True)
    live_own = jnp.sum(pick * jnp.where(alive_lane, 1.0, 0.0), axis=1, keepdims=True)
    shift_own = (a_own * float(SIDE) + b_own).astype(I32)
    pick16 = pick[:, :PAD]
    unpick16 = unpick[:, :PAD]

    pad_f[SLOTS:PAD, :] = jnp.zeros((PAD - SLOTS, PIX), F32)
    for half in range(2):
        pad_f[:SLOTS, half * 128 : half * 128 + 128] = temporal[pl.ds(half, SLOTS, stride=2), :]
    old_traces = pad_f[:SLOTS, :FRAMES]
    cm[:, :FRAMES] = jnp.dot(pick16, pad_f[:, :FRAMES], precision=lax.Precision.HIGHEST, preferred_element_type=F32)
    cm[:, FRAMES:] = jnp.where(lane == 0, a_own, jnp.where(lane == 1, b_own, jnp.where(lane == 2, live_own, 0.0)))

    loads[5].wait()
    for q in range(PIX // 128):
        pad_f[:SLOTS, q * 128 : q * 128 + 128] = footprints[pl.ds(q, SLOTS, stride=32), :]
    whole = jnp.floor(pad_f[...] * 65535.0 + 0.5)
    upper = jnp.floor(whole * (1.0 / 256.0))
    hl[:PAD, :] = upper.astype(BF16)
    hl[PAD:, :] = (whole - upper * 256.0).astype(BF16)
    pick_hl = jnp.concatenate([pick16 * 256.0, pick16], axis=1).astype(BF16)
    pad_f[...] = mm(pick_hl, hl[...])
    for half in range(2):
        part = slice(half * 8, half * 8 + 8)
        pad_f[part, :] = turn(pad_f[part, :], shift_own[part], True)
    code[...] = (pad_f[...] - 32768.0).astype(I32).astype(I16)

    loads[6].wait()
    loads[7].wait()
    for i in range(2):
        back_even[i * SIDE : i * SIDE + SIDE, :SIDE] = back_raw[i].astype(F32)
    even = back_even[pl.ds(0, SIDE, stride=2), :SIDE]
    odd = back_even[pl.ds(1, SIDE, stride=2), :SIDE]
    back_even[:SIDE, :] = jnp.concatenate([even, odd], axis=1)
    for q in range(PIX // 128):
        back[:2, q * 128 : q * 128 + 128] = back_even[pl.ds(q, 2, stride=32), :]
    back[2:, :] = jnp.zeros((6, PIX), F32)

    pl.semaphore_wait(barrier, expected)

    def remote(src, dst, send, recv, d):
        return pltpu.make_async_remote_copy(
            src_ref=src, dst_ref=dst, send_sem=send, recv_sem=recv, device_id=place(d), device_id_type=MESH
        )

    pending = []

    def start(copy, ok):
        @pl.when(ok)
        def _():
            copy.start()

        pending.append((copy, ok))

    def arrived(copy, ok):
        @pl.when(ok)
        def _():
            copy.wait_recv()

    def cm_copy(src, slot, d):
        return remote(src, r_cm.at[slot], cm_send.at[slot], cm_recv.at[slot], d)

    for d in (RIGHT, LEFT, DOWN, UP):
        start(cm_copy(cm, 7 - d, d), there(d))
    start(remote(code, r_code.at[2], r_send.at[2], r_recv.at[2], RIGHT), there(RIGHT))
    start(remote(code, r_code.at[1], r_send.at[1], r_recv.at[1], DOWN), there(DOWN))

    arrived(cm_copy(cm, LEFT, LEFT), there(LEFT))
    start(cm_copy(r_cm.at[LEFT], DL, UP), there(UP) & there(LEFT))
    start(cm_copy(r_cm.at[LEFT], UL, DOWN), there(DOWN) & there(LEFT))
    arrived(cm_copy(cm, RIGHT, RIGHT), there(RIGHT))
    start(cm_copy(r_cm.at[RIGHT], DR, UP), there(UP) & there(RIGHT))
    start(cm_copy(r_cm.at[RIGHT], UR, DOWN), there(DOWN) & there(RIGHT))
    for d in (UP, UL, DOWN, UR, DL, DR):
        arrived(cm_copy(cm, d, d), there(d))

    def cm_of(tile, rows_at, lanes_at):
        if tile == OWN:
            return cm[rows_at, lanes_at]
        return r_cm[tile, rows_at, lanes_at]

    for g in range(GROUPS):
        for t in range(4):
            at = slice(g * PAD + t * 4, g * PAD + t * 4 + 4)
            near_cm[at, :] = cm_of(TILE_SETS[0][t], slice(g * 4, g * 4 + 4), slice(None))
    for k in range(4):
        for g in range(GROUPS):
            for t in range(4):
                at = slice(k * NEAR + g * PAD + t * 4, k * NEAR + g * PAD + t * 4 + 4)
                call_f[at, :] = cm_of(TILE_SETS[k][t], slice(g * 4, g * 4 + 4), slice(0, FRAMES))
    high, low = split(call_f[...])
    c_high[...] = high
    c_low[...] = low

    frame = lax.broadcasted_iota(I32, (NEAR, FRAMES), 1)
    weighted = jnp.where((frame >= window[0]) & (frame < window[1]), near_cm[:, :FRAMES], 0.0)
    w_high, w_low = split(weighted)
    w_both = jnp.concatenate([w_high, w_low], axis=0)
    q4 = nt(w_both, w_both)
    q = q4[:NEAR, :NEAR] + q4[:NEAR, NEAR:] + q4[NEAR:, :NEAR] + q4[NEAR:, NEAR:]
    a_near = near_cm[:, FRAMES : FRAMES + 1].astype(I32)
    b_near = near_cm[:, FRAMES + 1 : FRAMES + 2].astype(I32)
    live_near = near_cm[:, FRAMES + 2 : FRAMES + 3]
    eye = lax.broadcasted_iota(I32, (NEAR, NEAR), 0) == lax.broadcasted_iota(I32, (NEAR, NEAR), 1)
    mass = jnp.sum(jnp.where(eye, q, 0.0), axis=1, keepdims=True)
    inverse = 1.0 / jnp.where(live_near > 0, mass, 1.0)
    q_high, q_low = split(jnp.where(eye, 0.0, q) * inverse)
    q3 = jnp.concatenate([q_high, q_high, q_low], axis=1)
    load0 = jnp.sum(weighted * back_time[0:1, :], axis=1, keepdims=True)
    load1 = jnp.sum(weighted * back_time[1:2, :], axis=1, keepdims=True)

    tile_at = (lax.broadcasted_iota(I32, (NEAR, 1), 0) >> 2) & 3
    above = tile_at < 2
    aside = (tile_at & 1) == 0
    y_low = jnp.where(above, 0, a_near)
    y_high = jnp.where(live_near > 0, jnp.where(above, a_near, SIDE), 0)
    x_low = jnp.where(aside, 0, b_near)
    x_high = jnp.where(aside, b_near, SIDE)

    def covered(rows_at, begin, width):
        spot = lax.broadcasted_iota(I32, (1, width), 1) + begin
        y = spot >> 6
        x = spot & 63
        return (
            (y >= y_low[rows_at]) & (y < y_high[rows_at]) & (x >= x_low[rows_at]) & (x < x_high[rows_at])
        )

    loads[8].wait()
    width = 1024
    for begin in range(0, PIX, width):
        at = slice(begin, begin + width)
        pull = nt(w_high, movie[at, :])
        pull = pull - load0 * back[0:1, at] - load1 * back[1:2, at]
        target[:, at] = jnp.where(covered(slice(None), begin, width), pull * inverse, -BIG)

    arrived(remote(code, r_code.at[2], r_send.at[2], r_recv.at[2], LEFT), there(LEFT))
    start(remote(r_code.at[2], r_code.at[0], r_send.at[0], r_recv.at[0], DOWN), there(DOWN) & there(LEFT))
    arrived(remote(code, r_code.at[1], r_send.at[1], r_recv.at[1], UP), there(UP))
    arrived(remote(code, r_code.at[0], r_send.at[0], r_recv.at[0], UL), there(UL))
    for t in (0, 1, 2, 3):
        coded = (r_code[t] if t < 3 else code[...]).astype(I32).astype(F32)
        if t in (0, 2):
            coded = half_turn(coded, False)
        for g in range(GROUPS):
            canvas[g * PAD + t * 4 : g * PAD + t * 4 + 4, :] = coded[g * 4 : g * 4 + 4, :]
    for g in range(GROUPS):
        rows_at = slice(g * PAD, g * PAD + PAD)
        value = jnp.where(covered(rows_at, 0, PIX), (canvas[rows_at, :] + 32768.0) * (1.0 / 65535.0), 0.0)
        high, low = split(value)
        x3[g * PAD : g * PAD + PAD, :] = high
        x3[NEAR + g * PAD : NEAR + g * PAD + PAD, :] = low
        x3[2 * NEAR + g * PAD : 2 * NEAR + g * PAD + PAD, :] = high

    both = x3[: 2 * NEAR, :]
    gram = nt(both, both)
    overlap = gram[:NEAR, :NEAR] + gram[:NEAR, NEAR:] + gram[NEAR:, :NEAR] + gram[NEAR:, NEAR:]
    loading = nt(both, back[...].astype(BF16))
    loading = loading[:NEAR] + loading[NEAR:]
    drive = mm(x3[:NEAR, :], movie[...])
    drive = drive - loading[:, 0:1] * back_time[0:1, :] - loading[:, 1:2] * back_time[1:2, :]
    shares[:, :FRAMES] = drive
    shares[:, FRAMES : FRAMES + NEAR] = overlap
    shares[:, FRAMES + NEAR :] = jnp.zeros((NEAR, 128 - NEAR), F32)
    for t in range(4):
        for g in range(GROUPS):
            share_out[t, g * 4 : g * 4 + 4, :] = shares[g * PAD + t * 4 : g * PAD + t * 4 + 4, :]

    def share_copy(t, d):
        return remote(share_out.at[t], r_share.at[t], s_send.at[t], s_recv.at[t], d)

    for t, d in ((0, UL), (2, LEFT), (1, UP)):
        start(share_copy(t, d), there(d))

    for g in range(GROUPS):
        rows_at = slice(g * PAD, g * PAD + PAD)
        value = jnp.maximum(target[rows_at, :] - mm(q3[rows_at, :], x3[...]), 0.0)
        canvas[rows_at, :] = jnp.floor(jnp.sqrt(value * (1.0 / TOP)) * 65535.0 + 0.5) - 32768.0
        if g < GROUPS - 1:
            high, low = split(value)
            x3[g * PAD : g * PAD + PAD, :] = high
            x3[NEAR + g * PAD : NEAR + g * PAD + PAD, :] = low
            x3[2 * NEAR + g * PAD : 2 * NEAR + g * PAD + PAD, :] = high

    def gather_tile(t):
        for g in range(GROUPS):
            temp[g * 4 : g * 4 + 4, :] = canvas[g * PAD + t * 4 : g * PAD + t * 4 + 4, :]
        return temp[...]

    for t in range(2):
        piece_up[t] = gather_tile(t).astype(I32).astype(I16)

    def piece_copy(t, d):
        return remote(piece_up.at[t], r_piece.at[t], p_send.at[t], p_recv.at[t], d)

    for t in range(2):
        start(piece_copy(t, UP), there(UP))

    for t, d in ((2, RIGHT), (1, DOWN), (0, DR)):
        arrived(share_copy(t, d), there(d))
    parts = [share_out[3], r_share[2], r_share[1], r_share[0]]
    drive = parts[0][:, :FRAMES] + parts[1][:, :FRAMES] + parts[2][:, :FRAMES] + parts[3][:, :FRAMES]
    near_lane = lax.broadcasted_iota(I32, (PAD, NEAR), 1)
    near_row = lax.broadcasted_iota(I32, (PAD, NEAR), 0)
    lane_row = ((near_lane >> 4) << 2) + (near_lane & 3)
    lane_tile = (near_lane >> 2) & 3
    weight = jnp.zeros((PAD, 1), F32)
    others = []
    for k in range(4):
        v = parts[k][:, FRAMES : FRAMES + NEAR]
        mine = (lane_tile == SELF_AT[k]) & (lane_row == near_row)
        weight = weight + jnp.sum(jnp.where(mine, v, 0.0), axis=1, keepdims=True)
        others.append(jnp.where(mine, 0.0, v))
    scale = 1.0 / jnp.where(live_own > 0, weight, 1.0)
    v_high, v_low = split(jnp.concatenate(others, axis=1) * scale)
    v_both = jnp.concatenate([v_high, v_low], axis=0)
    goal = drive * scale
    own = cm[:, :FRAMES]
    row_group = lax.broadcasted_iota(I32, (PAD, FRAMES), 0) >> 2

    def wave_copy(g, d, slot):
        return remote(wave.at[g], r_wave.at[g, slot], t_send.at[g, slot], t_recv.at[g, slot], d)

    for g in range(GROUPS):
        if g > 0:
            for d in range(8):
                arrived(wave_copy(g - 1, d, d), there(d))
            for k in range(4):
                for t in range(4):
                    tile = TILE_SETS[k][t]
                    new = wave[g - 1] if tile == OWN else r_wave[g - 1, tile]
                    at = slice(k * NEAR + (g - 1) * PAD + t * 4, k * NEAR + (g - 1) * PAD + t * 4 + 4)
                    call_f[at, :128] = new[:4, :]
                    call_f[at, 128:] = new[4:, :]
                at = slice(k * NEAR + (g - 1) * PAD, k * NEAR + g * PAD)
                high, low = split(call_f[at, :])
                c_high[at, :] = high
                c_low[at, :] = low
        product = mm(v_both, c_high[...])
        coupled = product[:PAD] + product[PAD:] + mm(v_high, c_low[...])
        chosen = (row_group == g) & (live_own > 0)
        own = jnp.where(chosen, jnp.maximum(goal - coupled, 0.0), own)
        if g < GROUPS - 1:
            wave[g, :4, :] = own[g * 4 : g * 4 + 4, :128]
            wave[g, 4:, :] = own[g * 4 : g * 4 + 4, 128:]
            for d in (UR, DR, UL, DL, RIGHT, LEFT, UP, DOWN):
                start(wave_copy(g, d, 7 - d), there(d))
        if g == 0:
            for t in range(2):
                arrived(piece_copy(t, DOWN), there(DOWN))
            spot = lax.broadcasted_iota(I32, (PAD, PIX), 1)
            a_left = r_cm[LEFT, :, FRAMES : FRAMES + 1].astype(I32)
            below = (spot >> 6) < a_left
            merged[...] = jnp.where(below, r_piece[0].astype(I32), gather_tile(2).astype(I32)).astype(I16)
            start(remote(merged, r_merged, m_send, m_recv, LEFT), there(LEFT))

    back_own = jnp.dot(unpick16, own, precision=lax.Precision.HIGHEST, preferred_element_type=F32)
    new_traces = jnp.where(alive_sub[:SLOTS, 0:1], back_own[:SLOTS, :], old_traces)
    for half in range(2):
        out_traces[pl.ds(half, SLOTS, stride=2), :] = new_traces[:, half * 128 : half * 128 + 128]

    arrived(remote(merged, r_merged, m_send, m_recv, RIGHT), there(RIGHT))
    y = spot >> 6
    x = spot & 63
    a_int = a_own.astype(I32)
    b_int = b_own.astype(I32)
    far = half_turn(r_merged[...].astype(I32).astype(F32), True)
    near = jnp.where(y < a_int, r_piece[1].astype(I32).astype(F32), gather_tile(3))
    pad_f[...] = jnp.where(x < b_int, far, near) + 32768.0
    for half in range(2):
        part = slice(half * 8, half * 8 + 8)
        pad_f[part, :] = turn(pad_f[part, :], shift_own[part], False)
    whole = pad_f[...]
    upper = jnp.floor(whole * (1.0 / 256.0))
    hl[:PAD, :] = upper.astype(BF16)
    hl[PAD:, :] = (whole - upper * 256.0).astype(BF16)
    unpick_hl = jnp.concatenate([unpick16 * 256.0, unpick16], axis=1).astype(BF16)
    root = mm(unpick_hl, hl[...])[:SLOTS, :] * (1.0 / 65535.0)
    pad_f[:SLOTS, :] = root * root * TOP
    for q in range(PIX // 128):
        out_shapes[pl.ds(q, SLOTS, stride=32), :] = pad_f[:SLOTS, q * 128 : q * 128 + 128]

    for copy, ok in pending:
        @pl.when(ok)
        def _(copy=copy):
            copy.wait_send()


def on_device(rows, cols, movie, footprints, anchors, groups, counts, temporal, back_spatial, back_temporal, window):
    vmem = pl.BlockSpec(memory_space=pltpu.VMEM)
    dma = pltpu.SemaphoreType.DMA
    shapes, traces = pl.pallas_call(
        functools.partial(kernel, rows, cols),
        out_shape=(
            jax.ShapeDtypeStruct((SLOTS * PIX // 128, 128), F32),
            jax.ShapeDtypeStruct((SLOTS * FRAMES // 128, 128), F32),
        ),
        in_specs=[pl.BlockSpec(memory_space=pl.ANY)] * 9,
        out_specs=(vmem, vmem),
        scratch_shapes=[
            pltpu.SMEM((2, SLOTS), I32),
            pltpu.SMEM((1, SLOTS), I32),
            pltpu.SMEM((1, 1), I32),
            pltpu.SMEM((2,), I32),
            pltpu.VMEM((SLOTS * PIX // 128, 128), F32),
            pltpu.VMEM((SLOTS * FRAMES // 128, 128), F32),
            pltpu.VMEM((2, SIDE, SIDE), BF16),
            pltpu.VMEM((2, FRAMES), F32),
            pltpu.VMEM((PIX, FRAMES), BF16),
            pltpu.VMEM((2 * SIDE, 2 * SIDE), F32),
            pltpu.VMEM((8, PIX), F32),
            pltpu.VMEM((PAD, PIX), F32),
            pltpu.VMEM((2 * PAD, PIX), BF16),
            pltpu.VMEM((PAD, PIX), I16),
            pltpu.VMEM((3, PAD, PIX), I16),
            pltpu.VMEM((PAD, FRAMES + 128), F32),
            pltpu.VMEM((8, PAD, FRAMES + 128), F32),
            pltpu.VMEM((NEAR, FRAMES + 128), F32),
            pltpu.VMEM((NEAR, PIX), F32),
            pltpu.VMEM((NEAR, PIX), F32),
            pltpu.VMEM((3 * NEAR, PIX), BF16),
            pltpu.VMEM((NEAR, FRAMES + 128), F32),
            pltpu.VMEM((4, PAD, FRAMES + 128), F32),
            pltpu.VMEM((3, PAD, FRAMES + 128), F32),
            pltpu.VMEM((3, 8, 128), F32),
            pltpu.VMEM((3, 8, 8, 128), F32),
            pltpu.VMEM((4 * NEAR, FRAMES), F32),
            pltpu.VMEM((4 * NEAR, FRAMES), BF16),
            pltpu.VMEM((4 * NEAR, FRAMES), BF16),
            pltpu.VMEM((PAD, PIX), F32),
            pltpu.VMEM((2, PAD, PIX), I16),
            pltpu.VMEM((2, PAD, PIX), I16),
            pltpu.VMEM((PAD, PIX), I16),
            pltpu.VMEM((PAD, PIX), I16),
            dma((9,)),
            dma((8,)),
            dma((8,)),
            dma((3,)),
            dma((3,)),
            dma((3,)),
            dma((3,)),
            dma((3, 8)),
            dma((3, 8)),
            dma((2,)),
            dma((2,)),
            dma,
            dma,
        ],
        compiler_params=pltpu.CompilerParams(collective_id=0, has_side_effects=True),
    )(
        anchors.reshape(SLOTS, 2).T,
        groups.reshape(1, SLOTS),
        counts,
        window,
        footprints.reshape(SLOTS * PIX // 128, 128),
        temporal.reshape(SLOTS * FRAMES // 128, 128),
        back_spatial,
        back_temporal,
        movie.reshape(PIX, FRAMES),
    )
    return shapes.reshape(1, 1, SLOTS, PIX), traces.reshape(1, 1, SLOTS, FRAMES)


def solution(mesh):
    return jax.shard_map(
        functools.partial(on_device, mesh.shape["row"], mesh.shape["col"]),
        mesh=mesh,
        in_specs=(
            P("row", "col", None),
            P("row", "col", None, None),
            P("row", "col", None, None),
            P("row", "col", None),
            P("row", "col"),
            P("row", "col", None, None),
            P(None, "row", "col"),
            P(),
            P(),
        ),
        out_specs=(P("row", "col", None, None), P("row", "col", None, None)),
        check_vma=False,
    )
```

```python
import functools

import jax
import jax.numpy as jnp
from jax import lax
from jax.experimental import pallas as pl
from jax.experimental.pallas import tpu as pltpu
from jax.sharding import PartitionSpec as P

MESH = pl.DeviceIdType.MESH
F32 = jnp.float32
BF16 = jnp.bfloat16
I32 = jnp.int32
I16 = jnp.int16

SIDE = 64
PIX = SIDE * SIDE
FRAMES = 256
SLOTS = 12
GROUPS = 4
PAD = 16
NEAR = 4 * PAD
BIG = 1e30
TOP = 8.0

DIRS = ((-1, -1), (-1, 0), (-1, 1), (0, -1), (0, 1), (1, -1), (1, 0), (1, 1))
UL, UP, UR, LEFT, RIGHT, DL, DOWN, DR = range(8)
OWN = 8
TILE_SETS = (
    (UL, UP, LEFT, OWN),
    (UP, UR, OWN, RIGHT),
    (LEFT, OWN, DL, DOWN),
    (OWN, RIGHT, DOWN, DR),
)
HALVES = 2


def nt(a, b):
    return lax.dot_general(a, b, (((1,), (1,)), ((), ())), preferred_element_type=F32)


def mm(a, b):
    return jnp.dot(a, b, preferred_element_type=F32)


def split(x):
    high = x.astype(BF16)
    return high, (x - high.astype(F32)).astype(BF16)


def turn(x, shift, forward):
    for bit in range(12):
        step = 1 << bit
        chosen = ((shift >> bit) & 1) == 1
        by = step if forward else PIX - step
        if by % 128 == 0:
            moved = jnp.concatenate([x[:, PIX - by :], x[:, : PIX - by]], axis=1)
        else:
            moved = pltpu.roll(x, by, 1)
        x = jnp.where(chosen, moved, x)
    return x


def half_turn(x, forward):
    return pltpu.roll(x, SIDE if forward else PIX - SIDE, 1)


def kernel(
    rows, cols,
    counts, anchors_in, groups_in, window_in, footprints_in, temporal_in, back_in, back_time_in, movie_in,
    out_shapes, out_traces,
    anchors, groups, window, footprints, temporal, back_raw, back_time, movie, back_even, back, pad_f, hl, code, r_code, cm, r_cm, near_cm, target, canvas, x3,
    shares, share_out, r_share, wave, r_wave, call_f, c_high, c_low, temp,
    r_mate, mate_cm, mate_goal, mate_v, mate_wave, r_far, mate_f, mate_high, mate_low,
    piece_up, r_piece, merged, r_merged,
    load_sem, cm_send, cm_recv, r_send, r_recv, s_send, s_recv, t_send, t_recv, p_send, p_recv, m_send, m_recv,
    mate_send, mate_recv, mw_send, far_send, far_recv,
):
    r = lax.axis_index("row")
    c = lax.axis_index("col")

    def there(d):
        down, right = DIRS[d]
        ok = None
        for at, step, count in ((r, down, rows), (c, right, cols)):
            if step:
                one = at + step >= 0 if step < 0 else at + step < count
                ok = one if ok is None else ok & one
        return ok

    def place(d):
        return (r + DIRS[d][0], c + DIRS[d][1])

    west = c == cols // 2 - 1
    east = c == cols // 2
    beside_west = c == cols // 2 - 2
    beside_east = c == cols // 2 + 1

    def row_ok(step):
        return (r + step >= 0) & (r + step < rows)

    barrier = pltpu.get_barrier_semaphore()

    loads = [
        pltpu.make_async_copy(source, target_ref, load_sem.at[at])
        for at, (source, target_ref) in enumerate(
            (
                (groups_in, groups),
                (anchors_in, anchors),
                (window_in, window),
                (temporal_in, temporal),
                (footprints_in, footprints),
                (back_time_in, back_time),
                (back_in, back_raw),
                (movie_in, movie),
            )
        )
    ]
    for load in loads:
        load.start()

    r_cm[...] = jnp.zeros_like(r_cm)
    r_share[...] = jnp.zeros_like(r_share)
    r_wave[...] = jnp.zeros_like(r_wave)
    r_mate[...] = jnp.zeros_like(r_mate)
    r_far[...] = jnp.zeros_like(r_far)
    call_f[...] = jnp.zeros_like(call_f)
    c_high[...] = jnp.zeros_like(c_high)
    c_low[...] = jnp.zeros_like(c_low)
    mate_f[...] = jnp.zeros_like(mate_f)
    mate_high[...] = jnp.zeros_like(mate_high)
    mate_low[...] = jnp.zeros_like(mate_low)

    expected = 0
    for d in range(8):
        ok = there(d)

        @pl.when(ok)
        def _(d=d):
            pl.semaphore_signal(barrier, inc=1, device_id=place(d), device_id_type=MESH)

        expected = expected + ok.astype(I32)
    for down in (-1, 0, 1):
        for right, role in ((2, beside_west | west), (-2, beside_east | east)):
            ok = role & row_ok(down)

            @pl.when(ok)
            def _(down=down, right=right):
                pl.semaphore_signal(barrier, inc=1, device_id=(r + down, c + right), device_id_type=MESH)

            expected = expected + ok.astype(I32)

    for load in loads[:4]:
        load.wait()
    sub = lax.broadcasted_iota(I32, (PAD, 128), 0)
    lane = lax.broadcasted_iota(I32, (PAD, 128), 1)
    g_sub = jnp.full((PAD, 128), -1, I32)
    g_lane = jnp.full((PAD, 128), -1, I32)
    a_lane = jnp.zeros((PAD, 128), I32)
    b_lane = jnp.zeros((PAD, 128), I32)
    count = counts[0, 0]
    for m in range(SLOTS):
        g_sub = jnp.where(sub == m, groups[0, m], g_sub)
        g_lane = jnp.where(lane == m, groups[0, m], g_lane)
        a_lane = jnp.where(lane == m, anchors[0, m], a_lane)
        b_lane = jnp.where(lane == m, anchors[1, m], b_lane)
    alive_lane = lane < count
    alive_sub = sub < count
    a_lane = jnp.where(alive_lane, a_lane, 0)
    b_lane = jnp.where(alive_lane, b_lane, 0)
    same = g_sub == g_lane
    before_lane = jnp.sum(jnp.where(same & (sub < lane), 1.0, 0.0), axis=0, keepdims=True)
    before_sub = jnp.sum(jnp.where(same & (lane < sub), 1.0, 0.0), axis=1, keepdims=True)
    pos_lane = g_lane.astype(F32) * 4.0 + before_lane
    pos_sub = g_sub.astype(F32) * 4.0 + before_sub
    pick = jnp.where((sub.astype(F32) == pos_lane) & (lane < SLOTS), 1.0, 0.0)
    unpick = jnp.where((lane.astype(F32) == pos_sub) & (sub < SLOTS), 1.0, 0.0)
    a_own = jnp.sum(pick * a_lane.astype(F32), axis=1, keepdims=True)
    b_own = jnp.sum(pick * b_lane.astype(F32), axis=1, keepdims=True)
    live_own = jnp.sum(pick * jnp.where(alive_lane, 1.0, 0.0), axis=1, keepdims=True)
    shift_own = (a_own * float(SIDE) + b_own).astype(I32)
    pick16 = pick[:, :PAD]
    unpick16 = unpick[:, :PAD]

    pad_f[SLOTS:PAD, :] = jnp.zeros((PAD - SLOTS, PIX), F32)
    for half in range(2):
        pad_f[:SLOTS, half * 128 : half * 128 + 128] = temporal[pl.ds(half, SLOTS, stride=2), :]
    old_traces = pad_f[:SLOTS, :FRAMES]
    cm[:, :FRAMES] = jnp.dot(pick16, pad_f[:, :FRAMES], precision=lax.Precision.HIGHEST, preferred_element_type=F32)
    cm[:, FRAMES:] = jnp.where(lane == 0, a_own, jnp.where(lane == 1, b_own, jnp.where(lane == 2, live_own, 0.0)))

    loads[4].wait()
    for q in range(PIX // 128):
        pad_f[:SLOTS, q * 128 : q * 128 + 128] = footprints[pl.ds(q, SLOTS, stride=32), :]
    whole = jnp.floor(pad_f[...] * 65535.0 + 0.5)
    upper = jnp.floor(whole * (1.0 / 256.0))
    hl[:PAD, :] = upper.astype(BF16)
    hl[PAD:, :] = (whole - upper * 256.0).astype(BF16)
    pick_hl = jnp.concatenate([pick16 * 256.0, pick16], axis=1).astype(BF16)
    pad_f[...] = mm(pick_hl, hl[...])
    for half in range(2):
        part = slice(half * 8, half * 8 + 8)
        pad_f[part, :] = turn(pad_f[part, :], shift_own[part], True)
    code[...] = (pad_f[...] - 32768.0).astype(I32).astype(I16)

    loads[5].wait()
    loads[6].wait()
    for i in range(2):
        back_even[i * SIDE : i * SIDE + SIDE, :SIDE] = back_raw[i].astype(F32)
    even = back_even[pl.ds(0, SIDE, stride=2), :SIDE]
    odd = back_even[pl.ds(1, SIDE, stride=2), :SIDE]
    back_even[:SIDE, :] = jnp.concatenate([even, odd], axis=1)
    for q in range(PIX // 128):
        back[:2, q * 128 : q * 128 + 128] = back_even[pl.ds(q, 2, stride=32), :]
    back[2:, :] = jnp.zeros((6, PIX), F32)

    pl.semaphore_wait(barrier, expected)

    def remote(src, dst, send, recv, d):
        target_id = place(d) if isinstance(d, int) else (r + d[0], c + d[1])
        return pltpu.make_async_remote_copy(
            src_ref=src, dst_ref=dst, send_sem=send, recv_sem=recv, device_id=target_id, device_id_type=MESH
        )

    pending = []

    def start(copy, ok):
        @pl.when(ok)
        def _():
            copy.start()

        pending.append((copy, ok))

    def arrived(copy, ok):
        @pl.when(ok)
        def _():
            copy.wait_recv()

    def cm_copy(src, slot, d):
        return remote(src, r_cm.at[slot], cm_send.at[slot], cm_recv.at[slot], d)

    for d in (RIGHT, LEFT, DOWN, UP):
        start(cm_copy(cm, 7 - d, d), there(d))

    def code_copy(source, slot, part, d):
        at = pl.ds(part * (PIX // HALVES), PIX // HALVES)
        source = code.at[:, at] if source is None else r_code.at[source, :, at]
        return remote(source, r_code.at[slot, :, at], r_send.at[slot, part], r_recv.at[slot, part], d)

    for part in range(HALVES):
        start(code_copy(None, 2, part, RIGHT), there(RIGHT))
    for part in range(HALVES):
        start(code_copy(None, 1, part, DOWN), there(DOWN))

    arrived(cm_copy(cm, LEFT, LEFT), there(LEFT))
    start(cm_copy(r_cm.at[LEFT], DL, UP), there(UP) & there(LEFT))
    start(cm_copy(r_cm.at[LEFT], UL, DOWN), there(DOWN) & there(LEFT))
    arrived(cm_copy(cm, RIGHT, RIGHT), there(RIGHT))
    start(cm_copy(r_cm.at[RIGHT], DR, UP), there(UP) & there(RIGHT))
    start(cm_copy(r_cm.at[RIGHT], UR, DOWN), there(DOWN) & there(RIGHT))
    for d in (UP, UL, DOWN, UR, DL, DR):
        arrived(cm_copy(cm, d, d), there(d))

    def cm_of(tile, rows_at, lanes_at):
        if tile == OWN:
            return cm[rows_at, lanes_at]
        return r_cm[tile, rows_at, lanes_at]

    for g in range(GROUPS):
        for t in range(4):
            at = slice(g * PAD + t * 4, g * PAD + t * 4 + 4)
            near_cm[at, :] = cm_of(TILE_SETS[0][t], slice(g * 4, g * 4 + 4), slice(None))
    near_high, near_low = split(near_cm[:, :FRAMES])

    frame = lax.broadcasted_iota(I32, (NEAR, FRAMES), 1)
    weighted = jnp.where((frame >= window[0]) & (frame < window[1]), near_cm[:, :FRAMES], 0.0)
    w_high, w_low = split(weighted)
    w_both = jnp.concatenate([w_high, w_low], axis=0)
    q4 = nt(w_both, w_both)
    q = q4[:NEAR, :NEAR] + q4[:NEAR, NEAR:] + q4[NEAR:, :NEAR] + q4[NEAR:, NEAR:]
    a_near = near_cm[:, FRAMES : FRAMES + 1].astype(I32)
    b_near = near_cm[:, FRAMES + 1 : FRAMES + 2].astype(I32)
    live_near = near_cm[:, FRAMES + 2 : FRAMES + 3]
    eye = lax.broadcasted_iota(I32, (NEAR, NEAR), 0) == lax.broadcasted_iota(I32, (NEAR, NEAR), 1)
    mass = jnp.sum(jnp.where(eye, q, 0.0), axis=1, keepdims=True)
    inverse = 1.0 / jnp.where(live_near > 0, mass, 1.0)
    q_high, q_low = split(jnp.where(eye, 0.0, q) * inverse)
    q3 = jnp.concatenate([q_high, q_high, q_low], axis=1)
    load0 = jnp.sum(weighted * back_time[0:1, :], axis=1, keepdims=True)
    load1 = jnp.sum(weighted * back_time[1:2, :], axis=1, keepdims=True)

    tile_at = (lax.broadcasted_iota(I32, (NEAR, 1), 0) >> 2) & 3
    above = tile_at < 2
    aside = (tile_at & 1) == 0
    y_low = jnp.where(above, 0, a_near)
    y_high = jnp.where(live_near > 0, jnp.where(above, a_near, SIDE), 0)
    x_low = jnp.where(aside, 0, b_near)
    x_high = jnp.where(aside, b_near, SIDE)

    def covered(rows_at, begin, width):
        spot = lax.broadcasted_iota(I32, (1, width), 1) + begin
        y = spot >> 6
        x = spot & 63
        return (
            (y >= y_low[rows_at]) & (y < y_high[rows_at]) & (x >= x_low[rows_at]) & (x < x_high[rows_at])
        )

    loads[7].wait()
    width = 1024
    for begin in range(0, PIX, width):
        at = slice(begin, begin + width)
        pull = nt(w_high, movie[at, :])
        pull = pull - load0 * back[0:1, at] - load1 * back[1:2, at]
        target[:, at] = jnp.where(covered(slice(None), begin, width), pull * inverse, -BIG)

    for part in range(HALVES):
        arrived(code_copy(None, 2, part, LEFT), there(LEFT))
        start(code_copy(2, 0, part, DOWN), there(DOWN) & there(LEFT))
    for part in range(HALVES):
        arrived(code_copy(None, 1, part, UP), there(UP))
    for part in range(HALVES):
        arrived(code_copy(None, 0, part, UL), there(UL))
    for t in (0, 1, 2, 3):
        coded = (r_code[t] if t < 3 else code[...]).astype(I32).astype(F32)
        if t in (0, 2):
            coded = half_turn(coded, False)
        for g in range(GROUPS):
            canvas[g * PAD + t * 4 : g * PAD + t * 4 + 4, :] = coded[g * 4 : g * 4 + 4, :]
    for g in range(GROUPS):
        rows_at = slice(g * PAD, g * PAD + PAD)
        value = jnp.where(covered(rows_at, 0, PIX), (canvas[rows_at, :] + 32768.0) * (1.0 / 65535.0), 0.0)
        high, low = split(value)
        x3[g * PAD : g * PAD + PAD, :] = high
        x3[NEAR + g * PAD : NEAR + g * PAD + PAD, :] = low
        x3[2 * NEAR + g * PAD : 2 * NEAR + g * PAD + PAD, :] = high

    both = x3[: 2 * NEAR, :]
    gram = nt(both, both)
    overlap = gram[:NEAR, :NEAR] + gram[:NEAR, NEAR:] + gram[NEAR:, :NEAR] + gram[NEAR:, NEAR:]
    loading = nt(both, back[...].astype(BF16))
    loading = loading[:NEAR] + loading[NEAR:]
    drive = mm(x3[:NEAR, :], movie[...])
    drive = drive - loading[:, 0:1] * back_time[0:1, :] - loading[:, 1:2] * back_time[1:2, :]
    self_overlap = jnp.sum(jnp.where(eye, overlap, 0.0), axis=1, keepdims=True)
    overlap = jnp.where(eye, 0.0, overlap)
    o_high, o_low = split(overlap)
    product = mm(jnp.concatenate([o_high, o_low], axis=0), near_high)
    shares[:, :FRAMES] = drive - (product[:NEAR] + product[NEAR:] + mm(o_high, near_low))
    shares[:, FRAMES : FRAMES + NEAR] = overlap
    shares[:, FRAMES + NEAR :] = jnp.broadcast_to(self_overlap, (NEAR, 128 - NEAR))
    for t in range(4):
        for g in range(GROUPS):
            share_out[t, g * 4 : g * 4 + 4, :] = shares[g * PAD + t * 4 : g * PAD + t * 4 + 4, :]

    def share_copy(t, d):
        return remote(share_out.at[t], r_share.at[t], s_send.at[t], s_recv.at[t], d)

    for t, d in ((0, UL), (2, LEFT), (1, UP)):
        start(share_copy(t, d), there(d))

    def mate_share(t, k, d):
        return remote(share_out.at[t], r_mate.at[k], mate_send.at[t], mate_recv.at[k], d)

    start(mate_share(3, 0, (0, 1)), west)
    start(mate_share(1, 2, (-1, 1)), west & row_ok(-1))
    start(mate_share(3, 0, (0, -1)), east)
    start(mate_share(1, 2, (-1, -1)), east & row_ok(-1))
    start(mate_share(0, 3, (-1, 0)), east & row_ok(-1))
    start(mate_share(2, 1, (0, -2)), beside_east)
    start(mate_share(0, 3, (-1, -2)), beside_east & row_ok(-1))

    for g in range(GROUPS):
        rows_at = slice(g * PAD, g * PAD + PAD)
        value = jnp.maximum(target[rows_at, :] - mm(q3[rows_at, :], x3[...]), 0.0)
        canvas[rows_at, :] = jnp.floor(jnp.sqrt(value * (1.0 / TOP)) * 65535.0 + 0.5) - 32768.0
        if g < GROUPS - 1:
            high, low = split(value)
            x3[g * PAD : g * PAD + PAD, :] = high
            x3[NEAR + g * PAD : NEAR + g * PAD + PAD, :] = low
            x3[2 * NEAR + g * PAD : 2 * NEAR + g * PAD + PAD, :] = high

    def gather_tile(t):
        for g in range(GROUPS):
            temp[g * 4 : g * 4 + 4, :] = canvas[g * PAD + t * 4 : g * PAD + t * 4 + 4, :]
        return temp[...]

    for t in range(2):
        piece_up[t] = gather_tile(t).astype(I32).astype(I16)

    def piece_copy(t, d):
        return remote(piece_up.at[t], r_piece.at[t], p_send.at[t], p_recv.at[t], d)

    for t in range(2):
        start(piece_copy(t, UP), there(UP))

    for t, d in ((2, RIGHT), (1, DOWN), (0, DR)):
        arrived(share_copy(t, d), there(d))

    def joined(parts, live):
        total = parts[0] + parts[1] + parts[2] + parts[3]
        scale = 1.0 / jnp.where(live > 0, total[:, FRAMES + NEAR : FRAMES + NEAR + 1], 1.0)
        v = jnp.concatenate([part[:, FRAMES : FRAMES + NEAR] for part in parts], axis=1) * scale
        return total[:, :FRAMES] * scale, jnp.concatenate(split(v), axis=0)

    goal, v_both = joined([share_out[3], r_share[2], r_share[1], r_share[0]], live_own)
    own = cm[:, :FRAMES]
    row_group = lax.broadcasted_iota(I32, (PAD, FRAMES), 0) >> 2

    def changes(sources, g, full, high_ref, low_ref):
        for k in range(4):
            for t in range(4):
                new = sources[TILE_SETS[k][t]]
                at = slice(k * NEAR + g * PAD + t * 4, k * NEAR + g * PAD + t * 4 + 4)
                full[at, :128] = new[:4, :]
                full[at, 128:] = new[4:, :]
            at = slice(k * NEAR + g * PAD, k * NEAR + g * PAD + PAD)
            high, low = split(full[at, :])
            high_ref[at, :] = high
            low_ref[at, :] = low

    def updated(g, aim, v_two, high_ref, low_ref, old, live):
        left_over = aim
        if g > 0:
            product = mm(v_two, high_ref[...])
            left_over = aim - (product[:PAD] + product[PAD:] + mm(v_two[:PAD], low_ref[...]))
        chosen = (row_group == g) & (live > 0)
        return jnp.where(chosen, jnp.maximum(left_over, 0.0), old)

    def pack(ref, g, new, old):
        change = new - old
        ref[g, :4, :] = change[g * 4 : g * 4 + 4, :128]
        ref[g, 4:, :] = change[g * 4 : g * 4 + 4, 128:]

    def wave_copy(g, d, slot):
        return remote(wave.at[g], r_wave.at[g, slot], t_send.at[g, slot], t_recv.at[g, slot], d)

    def wave_ok(d):
        ok = there(d)
        if DIRS[d][1] > 0:
            ok = ok & jnp.logical_not(west)
        if DIRS[d][1] < 0:
            ok = ok & jnp.logical_not(east)
        return ok

    def mate_copy(g, at, d, slot):
        return remote(mate_wave.at[g], r_wave.at[g, slot], mw_send.at[g, at], t_recv.at[g, slot], d)

    def far_copy(g, down, right):
        return remote(wave.at[g], r_far.at[g, 1 - down], far_send.at[g, 1 - down], far_recv.at[g, 1 - down], (down, right))

    sides = (
        (west, RIGHT, UR, DR, {UL: UP, LEFT: OWN, DL: DOWN, UP: UR, OWN: RIGHT, DOWN: DR}, (UR, RIGHT, DR)),
        (east, LEFT, UL, DL, {UR: UP, RIGHT: OWN, DR: DOWN, UP: UL, OWN: LEFT, DOWN: DL}, (UL, LEFT, DL)),
    )

    def start_mate(g):
        for role, mate, over, under, _, _ in sides:
            @pl.when(role)
            def _(mate=mate):
                r_wave[g, mate] = mate_wave[g]

            start(mate_copy(g, 0, UP, under), role & there(UP))
            start(mate_copy(g, 1, DOWN, over), role & there(DOWN))

    for g in range(GROUPS):
        if g > 0:
            for d in range(8):
                arrived(wave_copy(g - 1, d, d), wave_ok(d))
            for role, mate, over, under, _, _ in sides:
                arrived(mate_copy(g - 1, 0, UP, over), role & there(UP))
                arrived(mate_copy(g - 1, 1, DOWN, under), role & there(DOWN))
            changes([r_wave[g - 1, d] for d in range(8)] + [wave[g - 1]], g - 1, call_f, c_high, c_low)
        new = updated(g, goal, v_both, c_high, c_low, own, live_own)
        if g < GROUPS - 1:
            pack(wave, g, new, own)
            for d in (UR, DR, UL, DL, RIGHT, LEFT, UP, DOWN):
                start(wave_copy(g, d, 7 - d), wave_ok(d))
            if g < 2:
                for down in (-1, 0, 1):
                    start(far_copy(g, down, 2), beside_west & row_ok(down))
                    start(far_copy(g, down, -2), beside_east & row_ok(down))
        own = new
        if g == 0:
            for t in range(2):
                arrived(piece_copy(t, DOWN), there(DOWN))
            spot = lax.broadcasted_iota(I32, (PAD, PIX), 1)
            a_left = r_cm[LEFT, :, FRAMES : FRAMES + 1].astype(I32)
            below = (spot >> 6) < a_left
            merged[...] = jnp.where(below, r_piece[0].astype(I32), gather_tile(2).astype(I32)).astype(I16)
            start(remote(merged, r_merged, m_send, m_recv, LEFT), there(LEFT))

            arrived(mate_share(3, 0, (0, 1)), west)
            arrived(mate_share(1, 2, (1, 1)), west & row_ok(1))
            arrived(mate_share(2, 1, (0, 2)), west)
            arrived(mate_share(0, 3, (1, 2)), west & row_ok(1))
            arrived(mate_share(3, 0, (0, -1)), east)
            arrived(mate_share(1, 2, (1, -1)), east & row_ok(1))
            arrived(mate_share(0, 3, (1, 0)), east & row_ok(1))

            @pl.when(west)
            def _():
                mate_cm[...] = r_cm[RIGHT]

            @pl.when(east)
            def _():
                mate_cm[...] = r_cm[LEFT]
                r_mate[1] = share_out[2]

            @pl.when(west | east)
            def _():
                live = mate_cm[:, FRAMES + 2 : FRAMES + 3]
                mate_goal[...], mate_v[...] = joined([r_mate[k] for k in range(4)], live)
                old = mate_cm[:, :FRAMES]
                pack(mate_wave, 0, updated(0, mate_goal[...], None, None, None, old, live), old)

            start_mate(0)
        elif g < GROUPS - 1:
            for down in (-1, 0, 1):
                arrived(far_copy(g - 1, -down, 2), west & row_ok(down))
                arrived(far_copy(g - 1, -down, -2), east & row_ok(down))
            for role, mate, over, under, where_at, far_at in sides:
                @pl.when(role)
                def _(where_at=where_at, far_at=far_at):
                    sources = {}
                    for tile, at in where_at.items():
                        sources[tile] = wave[g - 1] if at == OWN else r_wave[g - 1, at]
                    for down, tile in enumerate(far_at):
                        sources[tile] = r_far[g - 1, down]
                    changes(sources, g - 1, mate_f, mate_high, mate_low)
                    old = mate_cm[:, :FRAMES]
                    live = mate_cm[:, FRAMES + 2 : FRAMES + 3]
                    pack(mate_wave, g, updated(g, mate_goal[...], mate_v[...], mate_high, mate_low, old, live), old)

            start_mate(g)

    back_own = jnp.dot(unpick16, own, precision=lax.Precision.HIGHEST, preferred_element_type=F32)
    new_traces = jnp.where(alive_sub[:SLOTS, 0:1], back_own[:SLOTS, :], old_traces)
    for half in range(2):
        out_traces[pl.ds(half, SLOTS, stride=2), :] = new_traces[:, half * 128 : half * 128 + 128]

    arrived(remote(merged, r_merged, m_send, m_recv, RIGHT), there(RIGHT))
    y = spot >> 6
    x = spot & 63
    a_int = a_own.astype(I32)
    b_int = b_own.astype(I32)
    far = half_turn(r_merged[...].astype(I32).astype(F32), True)
    near = jnp.where(y < a_int, r_piece[1].astype(I32).astype(F32), gather_tile(3))
    pad_f[...] = jnp.where(x < b_int, far, near) + 32768.0
    for half in range(2):
        part = slice(half * 8, half * 8 + 8)
        pad_f[part, :] = turn(pad_f[part, :], shift_own[part], False)
    whole = pad_f[...]
    upper = jnp.floor(whole * (1.0 / 256.0))
    hl[:PAD, :] = upper.astype(BF16)
    hl[PAD:, :] = (whole - upper * 256.0).astype(BF16)
    unpick_hl = jnp.concatenate([unpick16 * 256.0, unpick16], axis=1).astype(BF16)
    root = mm(unpick_hl, hl[...])[:SLOTS, :] * (1.0 / 65535.0)
    pad_f[:SLOTS, :] = root * root * TOP
    for q in range(PIX // 128):
        out_shapes[pl.ds(q, SLOTS, stride=32), :] = pad_f[:SLOTS, q * 128 : q * 128 + 128]

    for copy, ok in pending:
        @pl.when(ok)
        def _(copy=copy):
            copy.wait_send()


def on_device(rows, cols, movie, footprints, anchors, groups, counts, temporal, back_spatial, back_temporal, window):
    vmem = pl.BlockSpec(memory_space=pltpu.VMEM)
    dma = pltpu.SemaphoreType.DMA
    shapes, traces = pl.pallas_call(
        functools.partial(kernel, rows, cols),
        out_shape=(
            jax.ShapeDtypeStruct((SLOTS * PIX // 128, 128), F32),
            jax.ShapeDtypeStruct((SLOTS * FRAMES // 128, 128), F32),
        ),
        in_specs=[pl.BlockSpec(memory_space=pltpu.SMEM)] + [pl.BlockSpec(memory_space=pltpu.HBM)] * 8,
        out_specs=(vmem, vmem),
        scratch_shapes=[
            pltpu.SMEM((2, SLOTS), I32),
            pltpu.SMEM((1, SLOTS), I32),
            pltpu.SMEM((2,), I32),
            pltpu.VMEM((SLOTS * PIX // 128, 128), F32),
            pltpu.VMEM((SLOTS * FRAMES // 128, 128), F32),
            pltpu.VMEM((2, SIDE, SIDE), BF16),
            pltpu.VMEM((2, FRAMES), F32),
            pltpu.VMEM((PIX, FRAMES), BF16),
            pltpu.VMEM((2 * SIDE, 2 * SIDE), F32),
            pltpu.VMEM((8, PIX), F32),
            pltpu.VMEM((PAD, PIX), F32),
            pltpu.VMEM((2 * PAD, PIX), BF16),
            pltpu.VMEM((PAD, PIX), I16),
            pltpu.VMEM((3, PAD, PIX), I16),
            pltpu.VMEM((PAD, FRAMES + 128), F32),
            pltpu.VMEM((8, PAD, FRAMES + 128), F32),
            pltpu.VMEM((NEAR, FRAMES + 128), F32),
            pltpu.VMEM((NEAR, PIX), F32),
            pltpu.VMEM((NEAR, PIX), F32),
            pltpu.VMEM((3 * NEAR, PIX), BF16),
            pltpu.VMEM((NEAR, FRAMES + 128), F32),
            pltpu.VMEM((4, PAD, FRAMES + 128), F32),
            pltpu.VMEM((3, PAD, FRAMES + 128), F32),
            pltpu.VMEM((3, 8, 128), F32),
            pltpu.VMEM((3, 8, 8, 128), F32),
            pltpu.VMEM((4 * NEAR, FRAMES), F32),
            pltpu.VMEM((4 * NEAR, FRAMES), BF16),
            pltpu.VMEM((4 * NEAR, FRAMES), BF16),
            pltpu.VMEM((PAD, PIX), F32),
            pltpu.VMEM((4, PAD, FRAMES + 128), F32),
            pltpu.VMEM((PAD, FRAMES + 128), F32),
            pltpu.VMEM((PAD, FRAMES), F32),
            pltpu.VMEM((2 * PAD, 4 * NEAR), BF16),
            pltpu.VMEM((3, 8, 128), F32),
            pltpu.VMEM((2, 3, 8, 128), F32),
            pltpu.VMEM((4 * NEAR, FRAMES), F32),
            pltpu.VMEM((4 * NEAR, FRAMES), BF16),
            pltpu.VMEM((4 * NEAR, FRAMES), BF16),
            pltpu.VMEM((2, PAD, PIX), I16),
            pltpu.VMEM((2, PAD, PIX), I16),
            pltpu.VMEM((PAD, PIX), I16),
            pltpu.VMEM((PAD, PIX), I16),
            dma((8,)),
            dma((8,)),
            dma((8,)),
            dma((3, HALVES)),
            dma((3, HALVES)),
            dma((3,)),
            dma((3,)),
            dma((3, 8)),
            dma((3, 8)),
            dma((2,)),
            dma((2,)),
            dma,
            dma,
            dma((4,)),
            dma((4,)),
            dma((3, 2)),
            dma((2, 3)),
            dma((2, 3)),
        ],
        compiler_params=pltpu.CompilerParams(collective_id=0, has_side_effects=True, vmem_limit_bytes=32 << 20),
    )(
        counts,
        *(
            pltpu.with_memory_space_constraint(x, pltpu.HBM)
            for x in (
                anchors.reshape(SLOTS, 2).T,
                groups.reshape(1, SLOTS),
                window,
                footprints.reshape(SLOTS * PIX // 128, 128),
                temporal.reshape(SLOTS * FRAMES // 128, 128),
                back_spatial,
                back_temporal,
                movie.reshape(PIX, FRAMES),
            )
        )
    )
    return shapes.reshape(1, 1, SLOTS, PIX), traces.reshape(1, 1, SLOTS, FRAMES)


def solution(mesh):
    return jax.shard_map(
        functools.partial(on_device, mesh.shape["row"], mesh.shape["col"]),
        mesh=mesh,
        in_specs=(
            P("row", "col", None),
            P("row", "col", None, None),
            P("row", "col", None, None),
            P("row", "col", None),
            P("row", "col"),
            P("row", "col", None, None),
            P(None, "row", "col"),
            P(),
            P(),
        ),
        out_specs=(P("row", "col", None, None), P("row", "col", None, None)),
        check_vma=False,
    )
```

```python
import functools

import jax
import jax.numpy as jnp
from jax import lax
from jax.experimental import pallas as pl
from jax.experimental.pallas import tpu as pltpu
from jax.sharding import PartitionSpec as P

MESH = pl.DeviceIdType.MESH
F32 = jnp.float32
BF16 = jnp.bfloat16
I32 = jnp.int32
I16 = jnp.int16

SIDE = 64
PIX = SIDE * SIDE
FRAMES = 256
SLOTS = 12
GROUPS = 4
PAD = 16
NEAR = 4 * PAD
BIG = 1e30
DENSE = 4 * SLOTS
WIDE = PIX // 4
TOP = 8.0

DIRS = ((-1, -1), (-1, 0), (-1, 1), (0, -1), (0, 1), (1, -1), (1, 0), (1, 1))
UL, UP, UR, LEFT, RIGHT, DL, DOWN, DR = range(8)
OWN = 8
TILE_SETS = (
    (UL, UP, LEFT, OWN),
    (UP, UR, OWN, RIGHT),
    (LEFT, OWN, DL, DOWN),
    (OWN, RIGHT, DOWN, DR),
)
PARTS = 4


def nt(a, b):
    return lax.dot_general(a, b, (((1,), (1,)), ((), ())), preferred_element_type=F32)


def mm(a, b):
    return jnp.dot(a, b, preferred_element_type=F32)


def split(x):
    high = x.astype(BF16)
    return high, (x - high.astype(F32)).astype(BF16)


def turn(x, shift, forward):
    for bit in range(12):
        step = 1 << bit
        chosen = ((shift >> bit) & 1) == 1
        by = step if forward else PIX - step
        if by % 128 == 0:
            moved = jnp.concatenate([x[:, PIX - by :], x[:, : PIX - by]], axis=1)
        else:
            moved = pltpu.roll(x, by, 1)
        x = jnp.where(chosen, moved, x)
    return x


def half_turn(x, forward):
    return pltpu.roll(x, SIDE if forward else PIX - SIDE, 1)


def kernel(
    rows, cols,
    counts, anchors_in, groups_in, window_in, footprints_in, temporal_in, back_in, back_time_in, movie_in,
    out_shapes, out_traces,
    anchors, groups, window, footprints, temporal, back_raw, back_time, movie, back_even, back, pad_f, hl, code, code_right, r_code, cm, r_cm, near_cm, target, canvas, x3,
    shares, share_out, r_share, wave, r_wave, call_f, c_high, c_low, temp, dense, labels, far_f, near_f,
    r_mate, mate_cm, mate_goal, mate_v, mate_wave, r_far, mate_f, mate_high, mate_low,
    joint, r_joint, outer, r_outer, outer_wave, outer_f, outer_high, outer_low,
    piece_up, r_piece, merged, r_merged,
    load_sem, cm_send, cm_recv, r_send, r_recv, s_send, s_recv, t_send, t_recv, p_send, p_recv, m_send, m_recv,
    mate_send, mate_recv, mw_send, far_send, far_recv, joint_sem, outer_sem, ow_send,
):
    r = lax.axis_index("row")
    c = lax.axis_index("col")

    def there(d):
        down, right = DIRS[d]
        ok = None
        for at, step, count in ((r, down, rows), (c, right, cols)):
            if step:
                one = at + step >= 0 if step < 0 else at + step < count
                ok = one if ok is None else ok & one
        return ok

    def place(d):
        return (r + DIRS[d][0], c + DIRS[d][1])

    west = c == cols // 2 - 1
    east = c == cols // 2
    beside_west = c == cols // 2 - 2
    beside_east = c == cols // 2 + 1

    def row_ok(step):
        return (r + step >= 0) & (r + step < rows)

    barrier = pltpu.get_barrier_semaphore()

    loads = [
        pltpu.make_async_copy(source, target_ref, load_sem.at[at])
        for at, (source, target_ref) in enumerate(
            (
                (groups_in, groups),
                (anchors_in, anchors),
                (window_in, window),
                (temporal_in, temporal),
                (footprints_in, footprints),
                (back_time_in, back_time),
                (back_in, back_raw),
                (movie_in, movie),
            )
        )
    ]
    for load in loads:
        load.start()

    r_cm[...] = jnp.zeros_like(r_cm)
    r_share[...] = jnp.zeros_like(r_share)
    r_wave[...] = jnp.zeros_like(r_wave)
    r_mate[...] = jnp.zeros_like(r_mate)
    r_far[...] = jnp.zeros_like(r_far)
    call_f[...] = jnp.zeros_like(call_f)
    c_high[...] = jnp.zeros_like(c_high)
    c_low[...] = jnp.zeros_like(c_low)
    far_f[...] = jnp.zeros_like(far_f)
    near_f[...] = jnp.zeros_like(near_f)
    mate_f[...] = jnp.zeros_like(mate_f)
    mate_high[...] = jnp.zeros_like(mate_high)
    mate_low[...] = jnp.zeros_like(mate_low)
    outer_f[...] = jnp.zeros_like(outer_f)
    outer_high[...] = jnp.zeros_like(outer_high)
    outer_low[...] = jnp.zeros_like(outer_low)

    expected = 0
    for d in range(8):
        ok = there(d)

        @pl.when(ok)
        def _(d=d):
            pl.semaphore_signal(barrier, inc=1, device_id=place(d), device_id_type=MESH)

        expected = expected + ok.astype(I32)
    for down in (-1, 0, 1):
        for right, role in ((2, beside_west | west), (-2, beside_east | east)):
            ok = role & row_ok(down)

            @pl.when(ok)
            def _(down=down, right=right):
                pl.semaphore_signal(barrier, inc=1, device_id=(r + down, c + right), device_id_type=MESH)

            expected = expected + ok.astype(I32)

    for load in loads[:4]:
        load.wait()
    sub = lax.broadcasted_iota(I32, (PAD, 128), 0)
    lane = lax.broadcasted_iota(I32, (PAD, 128), 1)
    g_sub = jnp.full((PAD, 128), -1, I32)
    g_lane = jnp.full((PAD, 128), -1, I32)
    a_lane = jnp.zeros((PAD, 128), I32)
    b_lane = jnp.zeros((PAD, 128), I32)
    count = counts[0, 0]
    for m in range(SLOTS):
        g_sub = jnp.where(sub == m, groups[0, m], g_sub)
        g_lane = jnp.where(lane == m, groups[0, m], g_lane)
        a_lane = jnp.where(lane == m, anchors[0, m], a_lane)
        b_lane = jnp.where(lane == m, anchors[1, m], b_lane)
    alive_lane = lane < count
    alive_sub = sub < count
    a_lane = jnp.where(alive_lane, a_lane, 0)
    b_lane = jnp.where(alive_lane, b_lane, 0)
    same = g_sub == g_lane
    before_lane = jnp.sum(jnp.where(same & (sub < lane), 1.0, 0.0), axis=0, keepdims=True)
    before_sub = jnp.sum(jnp.where(same & (lane < sub), 1.0, 0.0), axis=1, keepdims=True)
    pos_lane = g_lane.astype(F32) * 4.0 + before_lane
    pos_sub = g_sub.astype(F32) * 4.0 + before_sub
    pick = jnp.where((sub.astype(F32) == pos_lane) & (lane < SLOTS), 1.0, 0.0)
    unpick = jnp.where((lane.astype(F32) == pos_sub) & (sub < SLOTS), 1.0, 0.0)
    a_own = jnp.sum(pick * a_lane.astype(F32), axis=1, keepdims=True)
    b_own = jnp.sum(pick * b_lane.astype(F32), axis=1, keepdims=True)
    live_own = jnp.sum(pick * jnp.where(alive_lane, 1.0, 0.0), axis=1, keepdims=True)
    shift_own = (a_own * float(SIDE) + b_own).astype(I32)
    pick16 = pick[:, :PAD]
    unpick16 = unpick[:, :PAD]

    pad_f[SLOTS:PAD, :] = jnp.zeros((PAD - SLOTS, PIX), F32)
    for half in range(2):
        pad_f[:SLOTS, half * 128 : half * 128 + 128] = temporal[pl.ds(half, SLOTS, stride=2), :]
    old_traces = pad_f[:SLOTS, :FRAMES]
    cm[:, :FRAMES] = jnp.dot(pick16, pad_f[:, :FRAMES], precision=lax.Precision.HIGHEST, preferred_element_type=F32)
    cm[:, FRAMES:] = jnp.where(lane == 0, a_own, jnp.where(lane == 1, b_own, jnp.where(lane == 2, live_own, 0.0)))

    loads[4].wait()
    for q in range(PIX // 128):
        pad_f[:SLOTS, q * 128 : q * 128 + 128] = footprints[pl.ds(q, SLOTS, stride=32), :]
    whole = jnp.floor(pad_f[...] * 65535.0 + 0.5)
    upper = jnp.floor(whole * (1.0 / 256.0))
    hl[:PAD, :] = upper.astype(BF16)
    hl[PAD:, :] = (whole - upper * 256.0).astype(BF16)
    pick_hl = jnp.concatenate([pick16 * 256.0, pick16], axis=1).astype(BF16)
    pad_f[...] = mm(pick_hl, hl[...])
    for half in range(2):
        part = slice(half * 8, half * 8 + 8)
        pad_f[part, :] = turn(pad_f[part, :], shift_own[part], True)

    def packed(ref, row_of):
        for q in range(4):
            for g in range(GROUPS):
                at = slice(q * SLOTS + g * 3, q * SLOTS + g * 3 + 3)
                dense[at, :] = ref[row_of(g) : row_of(g) + 3, q * WIDE : (q + 1) * WIDE]
        return dense[...].astype(I32).astype(I16)

    def unpacked(codes, ref, row_of):
        codes = codes.astype(I32).astype(F32)
        for q in range(4):
            for g in range(GROUPS):
                at = slice(q * SLOTS + g * 3, q * SLOTS + g * 3 + 3)
                ref[row_of(g) : row_of(g) + 3, q * WIDE : (q + 1) * WIDE] = codes[at, :]

    pad_f[...] = pad_f[...] - 32768.0
    code[...] = packed(pad_f, lambda g: g * 4)
    temp[...] = half_turn(pad_f[...], False)
    code_right[...] = packed(temp, lambda g: g * 4)

    loads[5].wait()
    loads[6].wait()
    for i in range(2):
        back_even[i * SIDE : i * SIDE + SIDE, :SIDE] = back_raw[i].astype(F32)
    even = back_even[pl.ds(0, SIDE, stride=2), :SIDE]
    odd = back_even[pl.ds(1, SIDE, stride=2), :SIDE]
    back_even[:SIDE, :] = jnp.concatenate([even, odd], axis=1)
    for q in range(PIX // 128):
        back[:2, q * 128 : q * 128 + 128] = back_even[pl.ds(q, 2, stride=32), :]
    back[2:, :] = jnp.zeros((6, PIX), F32)

    pl.semaphore_wait(barrier, expected)

    def remote(src, dst, send, recv, d):
        target_id = place(d) if isinstance(d, int) else (r + d[0], c + d[1])
        return pltpu.make_async_remote_copy(
            src_ref=src, dst_ref=dst, send_sem=send, recv_sem=recv, device_id=target_id, device_id_type=MESH
        )

    pending = []

    def start(copy, ok):
        @pl.when(ok)
        def _():
            copy.start()

        pending.append((copy, ok))

    def arrived(copy, ok):
        @pl.when(ok)
        def _():
            copy.wait_recv()

    def cm_copy(src, slot, d):
        return remote(src, r_cm.at[slot], cm_send.at[slot], cm_recv.at[slot], d)

    def code_copy(source, slot, part, d):
        at = pl.ds(part * (WIDE // PARTS), WIDE // PARTS)
        if source is None:
            source = code_right.at[:, at] if slot == 2 else code.at[:, at]
        else:
            source = r_code.at[source, :, at]
        return remote(source, r_code.at[slot, :, at], r_send.at[slot, part], r_recv.at[slot, part], d)

    start(cm_copy(cm, LEFT, RIGHT), there(RIGHT))
    for part in range(PARTS):
        start(code_copy(None, 2, part, RIGHT), there(RIGHT))
    start(cm_copy(cm, UP, DOWN), there(DOWN))
    for part in range(PARTS):
        start(code_copy(None, 1, part, DOWN), there(DOWN))
    start(cm_copy(cm, RIGHT, LEFT), east)

    arrived(cm_copy(cm, LEFT, LEFT), there(LEFT))
    start(cm_copy(r_cm.at[LEFT], UL, DOWN), there(DOWN) & there(LEFT))
    for part in range(PARTS):
        arrived(code_copy(None, 2, part, LEFT), there(LEFT))
        start(code_copy(2, 0, part, DOWN), there(DOWN) & there(LEFT))
    arrived(cm_copy(cm, UP, UP), there(UP))
    arrived(cm_copy(cm, UL, UL), there(UL))

    def cm_of(tile, rows_at, lanes_at):
        if tile == OWN:
            return cm[rows_at, lanes_at]
        return r_cm[tile, rows_at, lanes_at]

    for g in range(GROUPS):
        for t in range(4):
            at = slice(g * PAD + t * 4, g * PAD + t * 4 + 4)
            near_cm[at, :] = cm_of(TILE_SETS[0][t], slice(g * 4, g * 4 + 4), slice(None))
    near_high, near_low = split(near_cm[:, :FRAMES])

    frame = lax.broadcasted_iota(I32, (NEAR, FRAMES), 1)
    weighted = jnp.where((frame >= window[0]) & (frame < window[1]), near_cm[:, :FRAMES], 0.0)
    w_high, w_low = split(weighted)
    w_both = jnp.concatenate([w_high, w_low], axis=0)
    q4 = nt(w_both, w_both)
    q = q4[:NEAR, :NEAR] + q4[:NEAR, NEAR:] + q4[NEAR:, :NEAR] + q4[NEAR:, NEAR:]
    a_near = near_cm[:, FRAMES : FRAMES + 1].astype(I32)
    b_near = near_cm[:, FRAMES + 1 : FRAMES + 2].astype(I32)
    live_near = near_cm[:, FRAMES + 2 : FRAMES + 3]
    eye = lax.broadcasted_iota(I32, (NEAR, NEAR), 0) == lax.broadcasted_iota(I32, (NEAR, NEAR), 1)
    mass = jnp.sum(jnp.where(eye, q, 0.0), axis=1, keepdims=True)
    inverse = 1.0 / jnp.where(live_near > 0, mass, 1.0)
    q_high, q_low = split(jnp.where(eye, 0.0, q) * inverse)
    q3 = jnp.concatenate([q_high, q_high, q_low], axis=1)
    load0 = jnp.sum(weighted * back_time[0:1, :], axis=1, keepdims=True)
    load1 = jnp.sum(weighted * back_time[1:2, :], axis=1, keepdims=True)

    tile_at = (lax.broadcasted_iota(I32, (NEAR, 1), 0) >> 2) & 3
    above = tile_at < 2
    aside = (tile_at & 1) == 0
    y_low = jnp.where(above, 0, a_near)
    y_high = jnp.where(live_near > 0, jnp.where(above, a_near, SIDE), 0)
    x_low = jnp.where(aside, 0, b_near)
    x_high = jnp.where(aside, b_near, SIDE)

    def covered(rows_at, begin, width):
        spot = lax.broadcasted_iota(I32, (1, width), 1) + begin
        y = spot >> 6
        x = spot & 63
        return (
            (y >= y_low[rows_at]) & (y < y_high[rows_at]) & (x >= x_low[rows_at]) & (x < x_high[rows_at])
        )

    loads[7].wait()
    width = 1024
    for begin in range(0, PIX, width):
        at = slice(begin, begin + width)
        pull = nt(w_high, movie[at, :])
        pull = pull - load0 * back[0:1, at] - load1 * back[1:2, at]
        target[:, at] = jnp.where(covered(slice(None), begin, width), pull * inverse, -BIG)

    for part in range(PARTS):
        arrived(code_copy(None, 1, part, UP), there(UP))
    for part in range(PARTS):
        arrived(code_copy(None, 0, part, UL), there(UL))
    for t in range(3):
        unpacked(r_code[t], canvas, lambda g: g * PAD + t * 4)
    for g in range(GROUPS):
        canvas[g * PAD + 12 : g * PAD + 16, :] = pad_f[g * 4 : g * 4 + 4, :]
    for g in range(GROUPS):
        rows_at = slice(g * PAD, g * PAD + PAD)
        value = jnp.where(covered(rows_at, 0, PIX), (canvas[rows_at, :] + 32768.0) * (1.0 / 65535.0), 0.0)
        high, low = split(value)
        x3[g * PAD : g * PAD + PAD, :] = high
        x3[NEAR + g * PAD : NEAR + g * PAD + PAD, :] = low
        x3[2 * NEAR + g * PAD : 2 * NEAR + g * PAD + PAD, :] = high

    both = x3[: 2 * NEAR, :]
    gram = nt(both, both)
    overlap = gram[:NEAR, :NEAR] + gram[:NEAR, NEAR:] + gram[NEAR:, :NEAR] + gram[NEAR:, NEAR:]
    loading = nt(both, back[...].astype(BF16))
    loading = loading[:NEAR] + loading[NEAR:]
    drive = mm(x3[:NEAR, :], movie[...])
    drive = drive - loading[:, 0:1] * back_time[0:1, :] - loading[:, 1:2] * back_time[1:2, :]
    self_overlap = jnp.sum(jnp.where(eye, overlap, 0.0), axis=1, keepdims=True)
    overlap = jnp.where(eye, 0.0, overlap)
    o_high, o_low = split(overlap)
    product = mm(jnp.concatenate([o_high, o_low], axis=0), near_high)
    shares[:, :FRAMES] = drive - (product[:NEAR] + product[NEAR:] + mm(o_high, near_low))
    shares[:, FRAMES : FRAMES + NEAR] = overlap
    shares[:, FRAMES + NEAR :] = jnp.broadcast_to(self_overlap, (NEAR, 128 - NEAR))
    for t in range(4):
        for g in range(GROUPS):
            share_out[t, g * 4 : g * 4 + 4, :] = shares[g * PAD + t * 4 : g * PAD + t * 4 + 4, :]

    def share_copy(t, d):
        return remote(share_out.at[t], r_share.at[t], s_send.at[t], s_recv.at[t], d)

    for t, d in ((2, LEFT), (0, UL), (1, UP)):
        start(share_copy(t, d), there(d))

    def mate_share(t, k, d):
        return remote(share_out.at[t], r_mate.at[k], mate_send.at[t], mate_recv.at[k], d)

    start(mate_share(3, 0, (0, 1)), west)
    start(mate_share(1, 2, (-1, 1)), west & row_ok(-1))
    start(mate_share(0, 3, (-1, 0)), east & row_ok(-1))

    for g in range(GROUPS):
        rows_at = slice(g * PAD, g * PAD + PAD)
        value = jnp.maximum(target[rows_at, :] - mm(q3[rows_at, :], x3[...]), 0.0)
        canvas[rows_at, :] = jnp.floor(jnp.sqrt(value * (1.0 / TOP)) * 65535.0 + 0.5) - 32768.0
        if g < GROUPS - 1:
            high, low = split(value)
            x3[g * PAD : g * PAD + PAD, :] = high
            x3[NEAR + g * PAD : NEAR + g * PAD + PAD, :] = low
            x3[2 * NEAR + g * PAD : 2 * NEAR + g * PAD + PAD, :] = high

    for t in range(2):
        piece_up[t] = packed(canvas, lambda g: g * PAD + t * 4)

    def piece_copy(t, d):
        return remote(piece_up.at[t], r_piece.at[t], p_send.at[t], p_recv.at[t], d)

    for t, d in ((2, RIGHT), (1, DOWN), (0, DR)):
        arrived(share_copy(t, d), there(d))

    def joined(parts, live):
        total = parts[0] + parts[1] + parts[2] + parts[3]
        scale = 1.0 / jnp.where(live > 0, total[:, FRAMES + NEAR : FRAMES + NEAR + 1], 1.0)
        v = jnp.concatenate([part[:, FRAMES : FRAMES + NEAR] for part in parts], axis=1) * scale
        return total[:, :FRAMES] * scale, v

    def stacked(v):
        return jnp.concatenate(split(v), axis=0)

    goal, v_own = joined([share_out[3], r_share[2], r_share[1], r_share[0]], live_own)
    v_both = stacked(v_own)
    own = cm[:, :FRAMES]
    row_group = lax.broadcasted_iota(I32, (PAD, FRAMES), 0) >> 2

    def changes(sources, g, full, high_ref, low_ref):
        for k in range(4):
            for t in range(4):
                if TILE_SETS[k][t] not in sources:
                    continue
                new = sources[TILE_SETS[k][t]]
                at = slice(k * NEAR + g * PAD + t * 4, k * NEAR + g * PAD + t * 4 + 4)
                full[at, :128] = new[:4, :]
                full[at, 128:] = new[4:, :]
            at = slice(k * NEAR + g * PAD, k * NEAR + g * PAD + PAD)
            high, low = split(full[at, :])
            high_ref[at, :] = high
            low_ref[at, :] = low

    def remaining(aim, v_two, high_ref, low_ref):
        product = mm(v_two, high_ref[...])
        return aim - (product[:PAD] + product[PAD:] + mm(v_two[:PAD], low_ref[...]))

    def updated(g, left_over, old, live):
        chosen = (row_group == g) & (live > 0)
        return jnp.where(chosen, jnp.maximum(left_over, 0.0), old)

    def pack(ref, g, new, old):
        change = new - old
        ref[g, :4, :] = change[g * 4 : g * 4 + 4, :128]
        ref[g, 4:, :] = change[g * 4 : g * 4 + 4, 128:]

    def wave_copy(g, d, slot):
        return remote(wave.at[g], r_wave.at[g, slot], t_send.at[g, slot], t_recv.at[g, slot], d)

    def sends(g, d):
        ok = there(d)
        if DIRS[d][1] > 0:
            ok = ok & jnp.logical_not(west)
        if DIRS[d][1] < 0 and g > 0:
            ok = ok & jnp.logical_not(east)
        return ok

    def gets(g, d):
        ok = there(d)
        if DIRS[d][1] > 0 and g > 0:
            ok = ok & jnp.logical_not(west)
        if DIRS[d][1] < 0:
            ok = ok & jnp.logical_not(east)
        return ok

    def mate_copy(g, at, d, slot):
        return remote(mate_wave.at[g], r_wave.at[g, slot], mw_send.at[g, at], t_recv.at[g, slot], d)

    def far_copy(g, down, right):
        return remote(wave.at[g], r_far.at[g, 1 - down], far_send.at[g, 1 - down], far_recv.at[g, 1 - down], (down, right))

    def outer_copy(at, d):
        return remote(outer_wave, r_far.at[1, 2 - at], ow_send.at[at // 2], far_recv.at[1, 2 - at], d)

    joint_copy = remote(joint, r_joint, joint_sem.at[0], joint_sem.at[1], LEFT)
    outer_sum = remote(outer, r_outer, outer_sem.at[0], outer_sem.at[1], (0, 2))

    sides = (
        (west, 1, RIGHT, UR, DR, {UL: UP, LEFT: OWN, DL: DOWN, UP: UR, OWN: RIGHT, DOWN: DR}, (UR, RIGHT, DR)),
        (east, 0, LEFT, UL, DL, {UR: UP, RIGHT: OWN, DR: DOWN, UP: UL, OWN: LEFT, DOWN: DL}, (UL, LEFT, DL)),
    )

    def start_mate(g):
        for role, first, mate, over, under, _, _ in sides:
            if g < first:
                continue

            @pl.when(role)
            def _(mate=mate):
                r_wave[g, mate] = mate_wave[g]

            start(mate_copy(g, 0, UP, under), role & there(UP))
            start(mate_copy(g, 1, DOWN, over), role & there(DOWN))

    for g in range(GROUPS):
        left_over = goal
        if g > 0:
            for d in (UP, DOWN, LEFT, UL, DL):
                arrived(wave_copy(g - 1, d, d), gets(g - 1, d))
            if g == 1:
                @pl.when(beside_west)
                def _():
                    sources = {d: r_wave[0, d] for d in (UP, DOWN, LEFT, UL, DL)}
                    sources[OWN] = wave[0]
                    changes(sources, 0, mate_f, mate_high, mate_low)
                    aim = jnp.where(live_own > 0, remaining(goal, v_both, mate_high, mate_low), own)
                    for at, value in enumerate((aim, own, v_own)):
                        outer[at, :4, :] = value[4:8, :128]
                        outer[at, 4:, :] = value[4:8, 128:]

                start(outer_sum, beside_west)
            for d in (RIGHT, UR, DR):
                arrived(wave_copy(g - 1, d, d), gets(g - 1, d))
            for role, first, mate, over, under, _, _ in sides:
                if g - 1 >= first:
                    arrived(mate_copy(g - 1, 0, UP, over), role & there(UP))
                    arrived(mate_copy(g - 1, 1, DOWN, under), role & there(DOWN))
            changes({**{d: r_wave[g - 1, d] for d in range(8)}, OWN: wave[g - 1]}, g - 1, call_f, c_high, c_low)
            left_over = remaining(goal, v_both, c_high, c_low)
        new = updated(g, left_over, own, live_own)
        if g < GROUPS - 1:
            pack(wave, g, new, own)
            for d in (UL, DL, LEFT, UR, DR, RIGHT, UP, DOWN):
                start(wave_copy(g, d, 7 - d), sends(g, d))
            if g < 2:
                for down in (-1, 0, 1):
                    if g == 0:
                        start(far_copy(g, down, 2), beside_west & row_ok(down))
                    start(far_copy(g, down, -2), beside_east & row_ok(down))
        own = new
        if g == 0:
            @pl.when(east)
            def _():
                joint[:, :FRAMES] = goal
                joint[:, FRAMES:] = v_own

            start(joint_copy, east)

            for t in range(2):
                start(piece_copy(t, UP), there(UP))

            arrived(mate_share(3, 0, (0, -1)), east)
            arrived(mate_share(1, 2, (1, -1)), east & row_ok(1))
            arrived(mate_share(0, 3, (1, 0)), east & row_ok(1))

            @pl.when(east)
            def _():
                mate_cm[...] = r_cm[LEFT]
                r_mate[1] = share_out[2]
                live = mate_cm[:, FRAMES + 2 : FRAMES + 3]
                mate_goal[...], v_mate = joined([r_mate[k] for k in range(4)], live)
                mate_v[...] = stacked(v_mate)
                old = mate_cm[:, :FRAMES]
                pack(mate_wave, 0, updated(0, mate_goal[...], old, live), old)

            start_mate(0)

            for q in range(4):
                for k in range(GROUPS):
                    at = slice(q * SLOTS + k * 3, q * SLOTS + k * 3 + 3)
                    labels[at, :] = r_cm[LEFT, k * 4 : k * 4 + 3, FRAMES:]
            a_left = labels[:, 0:1].astype(I32)
            row = lax.broadcasted_iota(I32, (DENSE, WIDE), 0)
            quarter = (row >= SLOTS).astype(I32) + (row >= 2 * SLOTS).astype(I32) + (row >= 3 * SLOTS).astype(I32)
            below = quarter * 16 + (lax.broadcasted_iota(I32, (DENSE, WIDE), 1) >> 6) < a_left
            left_codes = packed(canvas, lambda k: k * PAD + 8).astype(I32)
            for t in range(2):
                arrived(piece_copy(t, DOWN), there(DOWN))
            merged[...] = jnp.where(below, r_piece[0].astype(I32), left_codes).astype(I16)
            start(remote(merged, r_merged, m_send, m_recv, LEFT), there(LEFT))
        elif g < GROUPS - 1:
            if g == 1:
                arrived(cm_copy(cm, RIGHT, RIGHT), west)
                arrived(joint_copy, west)

                @pl.when(west)
                def _():
                    mate_cm[...] = r_cm[RIGHT]
                    mate_goal[...] = r_joint[:, :FRAMES]
                    mate_v[...] = stacked(r_joint[:, FRAMES:])

            for down in (-1, 0, 1):
                arrived(far_copy(g - 1, -down, -2), west & row_ok(down))
                if g == 1:
                    arrived(far_copy(g - 1, -down, 2), east & row_ok(down))
                elif down:
                    arrived(outer_copy(1 - down, (down, 0)), east & row_ok(down))
            for role, first, mate, over, under, where_at, far_at in sides:
                @pl.when(role)
                def _(where_at=where_at, far_at=far_at):
                    sources = {}
                    for tile, at in where_at.items():
                        sources[tile] = wave[g - 1] if at == OWN else r_wave[g - 1, at]
                    for down, tile in enumerate(far_at):
                        sources[tile] = r_far[g - 1, down]
                    changes(sources, g - 1, mate_f, mate_high, mate_low)
                    old = mate_cm[:, :FRAMES]
                    live = mate_cm[:, FRAMES + 2 : FRAMES + 3]
                    rest = remaining(mate_goal[...], mate_v[...], mate_high, mate_low)
                    pack(mate_wave, g, updated(g, rest, old, live), old)

            start_mate(g)
            if g == 1:
                arrived(outer_sum, east)

                @pl.when(east)
                def _():
                    changes({UR: r_wave[0, UL], RIGHT: r_wave[0, LEFT], DR: r_wave[0, DL]}, 0, outer_f, outer_high, outer_low)
                    zero = jnp.zeros((4, FRAMES), F32)
                    aim, old, v = (
                        jnp.concatenate(
                            [zero, jnp.concatenate([r_outer[at, :4, :], r_outer[at, 4:, :]], axis=1), zero, zero], axis=0
                        )
                        for at in range(3)
                    )
                    value = jnp.maximum(remaining(aim, stacked(v), outer_high, outer_low), 0.0)
                    pack2 = value - old
                    outer_wave[:4, :] = pack2[4:8, :128]
                    outer_wave[4:, :] = pack2[4:8, 128:]
                    r_far[1, 1] = outer_wave[...]

                start(outer_copy(0, UP), east & there(UP))
                start(outer_copy(2, DOWN), east & there(DOWN))

    back_own = jnp.dot(unpick16, own, precision=lax.Precision.HIGHEST, preferred_element_type=F32)
    new_traces = jnp.where(alive_sub[:SLOTS, 0:1], back_own[:SLOTS, :], old_traces)
    for half in range(2):
        out_traces[pl.ds(half, SLOTS, stride=2), :] = new_traces[:, half * 128 : half * 128 + 128]

    arrived(remote(merged, r_merged, m_send, m_recv, RIGHT), there(RIGHT))
    spot = lax.broadcasted_iota(I32, (PAD, PIX), 1)
    y = spot >> 6
    x = spot & 63
    a_int = a_own.astype(I32)
    b_int = b_own.astype(I32)
    unpacked(r_merged[...], far_f, lambda g: g * 4)
    unpacked(r_piece[1], near_f, lambda g: g * 4)
    for g in range(GROUPS):
        temp[g * 4 : g * 4 + 4, :] = canvas[g * PAD + 12 : g * PAD + 16, :]
    near = jnp.where(y < a_int, near_f[...], temp[...])
    pad_f[...] = jnp.where(x < b_int, half_turn(far_f[...], True), near) + 32768.0
    for half in range(2):
        part = slice(half * 8, half * 8 + 8)
        pad_f[part, :] = turn(pad_f[part, :], shift_own[part], False)
    whole = pad_f[...]
    upper = jnp.floor(whole * (1.0 / 256.0))
    hl[:PAD, :] = upper.astype(BF16)
    hl[PAD:, :] = (whole - upper * 256.0).astype(BF16)
    unpick_hl = jnp.concatenate([unpick16 * 256.0, unpick16], axis=1).astype(BF16)
    root = mm(unpick_hl, hl[...])[:SLOTS, :] * (1.0 / 65535.0)
    pad_f[:SLOTS, :] = root * root * TOP
    for q in range(PIX // 128):
        out_shapes[pl.ds(q, SLOTS, stride=32), :] = pad_f[:SLOTS, q * 128 : q * 128 + 128]

    for copy, ok in pending:
        @pl.when(ok)
        def _(copy=copy):
            copy.wait_send()


def on_device(rows, cols, movie, footprints, anchors, groups, counts, temporal, back_spatial, back_temporal, window):
    vmem = pl.BlockSpec(memory_space=pltpu.VMEM)
    dma = pltpu.SemaphoreType.DMA
    shapes, traces = pl.pallas_call(
        functools.partial(kernel, rows, cols),
        out_shape=(
            jax.ShapeDtypeStruct((SLOTS * PIX // 128, 128), F32),
            jax.ShapeDtypeStruct((SLOTS * FRAMES // 128, 128), F32),
        ),
        in_specs=[pl.BlockSpec(memory_space=pltpu.SMEM)] + [pl.BlockSpec(memory_space=pltpu.HBM)] * 8,
        out_specs=(vmem, vmem),
        scratch_shapes=[
            pltpu.SMEM((2, SLOTS), I32),
            pltpu.SMEM((1, SLOTS), I32),
            pltpu.SMEM((2,), I32),
            pltpu.VMEM((SLOTS * PIX // 128, 128), F32),
            pltpu.VMEM((SLOTS * FRAMES // 128, 128), F32),
            pltpu.VMEM((2, SIDE, SIDE), BF16),
            pltpu.VMEM((2, FRAMES), F32),
            pltpu.VMEM((PIX, FRAMES), BF16),
            pltpu.VMEM((2 * SIDE, 2 * SIDE), F32),
            pltpu.VMEM((8, PIX), F32),
            pltpu.VMEM((PAD, PIX), F32),
            pltpu.VMEM((2 * PAD, PIX), BF16),
            pltpu.VMEM((DENSE, WIDE), I16),
            pltpu.VMEM((DENSE, WIDE), I16),
            pltpu.VMEM((3, DENSE, WIDE), I16),
            pltpu.VMEM((PAD, FRAMES + 128), F32),
            pltpu.VMEM((8, PAD, FRAMES + 128), F32),
            pltpu.VMEM((NEAR, FRAMES + 128), F32),
            pltpu.VMEM((NEAR, PIX), F32),
            pltpu.VMEM((NEAR, PIX), F32),
            pltpu.VMEM((3 * NEAR, PIX), BF16),
            pltpu.VMEM((NEAR, FRAMES + 128), F32),
            pltpu.VMEM((4, PAD, FRAMES + 128), F32),
            pltpu.VMEM((3, PAD, FRAMES + 128), F32),
            pltpu.VMEM((3, 8, 128), F32),
            pltpu.VMEM((3, 8, 8, 128), F32),
            pltpu.VMEM((4 * NEAR, FRAMES), F32),
            pltpu.VMEM((4 * NEAR, FRAMES), BF16),
            pltpu.VMEM((4 * NEAR, FRAMES), BF16),
            pltpu.VMEM((PAD, PIX), F32),
            pltpu.VMEM((DENSE, WIDE), F32),
            pltpu.VMEM((DENSE, 128), F32),
            pltpu.VMEM((PAD, PIX), F32),
            pltpu.VMEM((PAD, PIX), F32),
            pltpu.VMEM((4, PAD, FRAMES + 128), F32),
            pltpu.VMEM((PAD, FRAMES + 128), F32),
            pltpu.VMEM((PAD, FRAMES), F32),
            pltpu.VMEM((2 * PAD, 4 * NEAR), BF16),
            pltpu.VMEM((3, 8, 128), F32),
            pltpu.VMEM((2, 3, 8, 128), F32),
            pltpu.VMEM((4 * NEAR, FRAMES), F32),
            pltpu.VMEM((4 * NEAR, FRAMES), BF16),
            pltpu.VMEM((4 * NEAR, FRAMES), BF16),
            pltpu.VMEM((PAD, 2 * FRAMES), F32),
            pltpu.VMEM((PAD, 2 * FRAMES), F32),
            pltpu.VMEM((3, 8, 128), F32),
            pltpu.VMEM((3, 8, 128), F32),
            pltpu.VMEM((8, 128), F32),
            pltpu.VMEM((4 * NEAR, FRAMES), F32),
            pltpu.VMEM((4 * NEAR, FRAMES), BF16),
            pltpu.VMEM((4 * NEAR, FRAMES), BF16),
            pltpu.VMEM((2, DENSE, WIDE), I16),
            pltpu.VMEM((2, DENSE, WIDE), I16),
            pltpu.VMEM((DENSE, WIDE), I16),
            pltpu.VMEM((DENSE, WIDE), I16),
            dma((8,)),
            dma((8,)),
            dma((8,)),
            dma((3, PARTS)),
            dma((3, PARTS)),
            dma((3,)),
            dma((3,)),
            dma((3, 8)),
            dma((3, 8)),
            dma((2,)),
            dma((2,)),
            dma,
            dma,
            dma((4,)),
            dma((4,)),
            dma((3, 2)),
            dma((2, 3)),
            dma((2, 3)),
            dma((2,)),
            dma((2,)),
            dma((2,)),
        ],
        compiler_params=pltpu.CompilerParams(collective_id=0, has_side_effects=True, vmem_limit_bytes=32 << 20),
    )(
        counts,
        *(
            pltpu.with_memory_space_constraint(x, pltpu.HBM)
            for x in (
                anchors.reshape(SLOTS, 2).T,
                groups.reshape(1, SLOTS),
                window,
                footprints.reshape(SLOTS * PIX // 128, 128),
                temporal.reshape(SLOTS * FRAMES // 128, 128),
                back_spatial,
                back_temporal,
                movie.reshape(PIX, FRAMES),
            )
        )
    )
    return shapes.reshape(1, 1, SLOTS, PIX), traces.reshape(1, 1, SLOTS, FRAMES)


def solution(mesh):
    return jax.shard_map(
        functools.partial(on_device, mesh.shape["row"], mesh.shape["col"]),
        mesh=mesh,
        in_specs=(
            P("row", "col", None),
            P("row", "col", None, None),
            P("row", "col", None, None),
            P("row", "col", None),
            P("row", "col"),
            P("row", "col", None, None),
            P(None, "row", "col"),
            P(),
            P(),
        ),
        out_specs=(P("row", "col", None, None), P("row", "col", None, None)),
        check_vma=False,
    )
```

```python
import functools

import jax
import jax.numpy as jnp
from jax import lax
from jax.experimental import pallas as pl
from jax.experimental.pallas import tpu as pltpu
from jax.sharding import PartitionSpec as P

MESH = pl.DeviceIdType.MESH
F32 = jnp.float32
BF16 = jnp.bfloat16
I32 = jnp.int32
I16 = jnp.int16

SIDE = 64
PIX = SIDE * SIDE
FRAMES = 256
SLOTS = 12
GROUPS = 4
PAD = 16
NEAR = 4 * PAD
BIG = 1e30
DENSE = 4 * SLOTS
WIDE = PIX // 4
TOP = 8.0

DIRS = ((-1, -1), (-1, 0), (-1, 1), (0, -1), (0, 1), (1, -1), (1, 0), (1, 1))
UL, UP, UR, LEFT, RIGHT, DL, DOWN, DR = range(8)
OWN = 8
TILE_SETS = (
    (UL, UP, LEFT, OWN),
    (UP, UR, OWN, RIGHT),
    (LEFT, OWN, DL, DOWN),
    (OWN, RIGHT, DOWN, DR),
)
PARTS = 4


def nt(a, b):
    return lax.dot_general(a, b, (((1,), (1,)), ((), ())), preferred_element_type=F32)


def mm(a, b):
    return jnp.dot(a, b, preferred_element_type=F32)


def split(x):
    high = x.astype(BF16)
    return high, (x - high.astype(F32)).astype(BF16)


def turn(x, shift, forward):
    for bit in range(12):
        step = 1 << bit
        chosen = ((shift >> bit) & 1) == 1
        by = step if forward else PIX - step
        if by % 128 == 0:
            moved = jnp.concatenate([x[:, PIX - by :], x[:, : PIX - by]], axis=1)
        else:
            moved = pltpu.roll(x, by, 1)
        x = jnp.where(chosen, moved, x)
    return x


def half_turn(x, forward):
    return pltpu.roll(x, SIDE if forward else PIX - SIDE, 1)


def kernel(
    rows, cols,
    counts, anchors_in, groups_in, window_in, footprints_in, temporal_in, back_in, back_time_in, movie_in,
    out_shapes, out_traces,
    anchors, groups, window, footprints, temporal, back_raw, back_time, movie, back_even, back, pad_f, hl, code, code_right, r_code, cm, r_cm, near_cm, target, canvas, x3,
    shares, share_out, r_share, wave, r_wave, call_f, c_high, c_low, temp, dense, labels, far_f, near_f,
    r_mate, mate_cm, mate_goal, mate_v, mate_wave, r_far, mate_f, mate_high, mate_low,
    joint, r_joint, outer, r_outer, outer_wave, outer_f, outer_high, outer_low,
    piece_up, r_piece, merged, r_merged,
    load_sem, cm_send, cm_recv, r_send, r_recv, s_send, s_recv, t_send, t_recv, p_send, p_recv, m_send, m_recv,
    mate_send, mate_recv, mw_send, far_send, far_recv, joint_sem, outer_sem, ow_send,
):
    r = lax.axis_index("row")
    c = lax.axis_index("col")

    def there(d):
        down, right = DIRS[d]
        ok = None
        for at, step, count in ((r, down, rows), (c, right, cols)):
            if step:
                one = at + step >= 0 if step < 0 else at + step < count
                ok = one if ok is None else ok & one
        return ok

    def place(d):
        return (r + DIRS[d][0], c + DIRS[d][1])

    west = c == cols // 2 - 1
    east = c == cols // 2
    beside_west = c == cols // 2 - 2
    beside_east = c == cols // 2 + 1

    def row_ok(step):
        return (r + step >= 0) & (r + step < rows)

    barrier = pltpu.get_barrier_semaphore()

    loads = [
        pltpu.make_async_copy(source, target_ref, load_sem.at[at])
        for at, (source, target_ref) in enumerate(
            (
                (groups_in, groups),
                (anchors_in, anchors),
                (window_in, window),
                (temporal_in, temporal),
                (footprints_in, footprints),
                (back_time_in, back_time),
                (back_in, back_raw),
                (movie_in, movie),
            )
        )
    ]
    for load in loads:
        load.start()

    r_cm[...] = jnp.zeros_like(r_cm)
    r_share[...] = jnp.zeros_like(r_share)
    r_wave[...] = jnp.zeros_like(r_wave)
    r_mate[...] = jnp.zeros_like(r_mate)
    r_far[...] = jnp.zeros_like(r_far)
    call_f[...] = jnp.zeros_like(call_f)
    c_high[...] = jnp.zeros_like(c_high)
    c_low[...] = jnp.zeros_like(c_low)
    far_f[...] = jnp.zeros_like(far_f)
    near_f[...] = jnp.zeros_like(near_f)
    mate_f[...] = jnp.zeros_like(mate_f)
    mate_high[...] = jnp.zeros_like(mate_high)
    mate_low[...] = jnp.zeros_like(mate_low)
    outer_f[...] = jnp.zeros_like(outer_f)
    outer_high[...] = jnp.zeros_like(outer_high)
    outer_low[...] = jnp.zeros_like(outer_low)

    expected = 0
    for d in range(8):
        ok = there(d)

        @pl.when(ok)
        def _(d=d):
            pl.semaphore_signal(barrier, inc=1, device_id=place(d), device_id_type=MESH)

        expected = expected + ok.astype(I32)
    for down in (-1, 0, 1):
        for right, role in ((2, beside_west | west), (-2, beside_east | east)):
            ok = role & row_ok(down)

            @pl.when(ok)
            def _(down=down, right=right):
                pl.semaphore_signal(barrier, inc=1, device_id=(r + down, c + right), device_id_type=MESH)

            expected = expected + ok.astype(I32)

    for load in loads[:4]:
        load.wait()
    sub = lax.broadcasted_iota(I32, (PAD, 128), 0)
    lane = lax.broadcasted_iota(I32, (PAD, 128), 1)
    g_sub = jnp.full((PAD, 128), -1, I32)
    g_lane = jnp.full((PAD, 128), -1, I32)
    a_lane = jnp.zeros((PAD, 128), I32)
    b_lane = jnp.zeros((PAD, 128), I32)
    count = counts[0, 0]
    for m in range(SLOTS):
        g_sub = jnp.where(sub == m, groups[0, m], g_sub)
        g_lane = jnp.where(lane == m, groups[0, m], g_lane)
        a_lane = jnp.where(lane == m, anchors[0, m], a_lane)
        b_lane = jnp.where(lane == m, anchors[1, m], b_lane)
    alive_lane = lane < count
    alive_sub = sub < count
    a_lane = jnp.where(alive_lane, a_lane, 0)
    b_lane = jnp.where(alive_lane, b_lane, 0)
    same = g_sub == g_lane
    before_lane = jnp.sum(jnp.where(same & (sub < lane), 1.0, 0.0), axis=0, keepdims=True)
    before_sub = jnp.sum(jnp.where(same & (lane < sub), 1.0, 0.0), axis=1, keepdims=True)
    pos_lane = g_lane.astype(F32) * 4.0 + before_lane
    pos_sub = g_sub.astype(F32) * 4.0 + before_sub
    pick = jnp.where((sub.astype(F32) == pos_lane) & (lane < SLOTS), 1.0, 0.0)
    unpick = jnp.where((lane.astype(F32) == pos_sub) & (sub < SLOTS), 1.0, 0.0)
    a_own = jnp.sum(pick * a_lane.astype(F32), axis=1, keepdims=True)
    b_own = jnp.sum(pick * b_lane.astype(F32), axis=1, keepdims=True)
    live_own = jnp.sum(pick * jnp.where(alive_lane, 1.0, 0.0), axis=1, keepdims=True)
    shift_own = (a_own * float(SIDE) + b_own).astype(I32)
    pick16 = pick[:, :PAD]
    unpick16 = unpick[:, :PAD]

    pad_f[SLOTS:PAD, :] = jnp.zeros((PAD - SLOTS, PIX), F32)
    for half in range(2):
        pad_f[:SLOTS, half * 128 : half * 128 + 128] = temporal[pl.ds(half, SLOTS, stride=2), :]
    old_traces = pad_f[:SLOTS, :FRAMES]
    cm[:, :FRAMES] = jnp.dot(pick16, pad_f[:, :FRAMES], precision=lax.Precision.HIGHEST, preferred_element_type=F32)
    cm[:, FRAMES:] = jnp.where(lane == 0, a_own, jnp.where(lane == 1, b_own, jnp.where(lane == 2, live_own, 0.0)))

    loads[4].wait()
    for q in range(PIX // 128):
        pad_f[:SLOTS, q * 128 : q * 128 + 128] = footprints[pl.ds(q, SLOTS, stride=32), :]
    whole = jnp.floor(pad_f[...] * 65535.0 + 0.5)
    upper = jnp.floor(whole * (1.0 / 256.0))
    hl[:PAD, :] = upper.astype(BF16)
    hl[PAD:, :] = (whole - upper * 256.0).astype(BF16)
    pick_hl = jnp.concatenate([pick16 * 256.0, pick16], axis=1).astype(BF16)
    pad_f[...] = mm(pick_hl, hl[...])
    for half in range(2):
        part = slice(half * 8, half * 8 + 8)
        pad_f[part, :] = turn(pad_f[part, :], shift_own[part], True)

    def packed(ref, row_of):
        for q in range(4):
            for g in range(GROUPS):
                at = slice(q * SLOTS + g * 3, q * SLOTS + g * 3 + 3)
                dense[at, :] = ref[row_of(g) : row_of(g) + 3, q * WIDE : (q + 1) * WIDE]
        return dense[...].astype(I32).astype(I16)

    def unpacked(codes, ref, row_of):
        codes = codes.astype(I32).astype(F32)
        for q in range(4):
            for g in range(GROUPS):
                at = slice(q * SLOTS + g * 3, q * SLOTS + g * 3 + 3)
                ref[row_of(g) : row_of(g) + 3, q * WIDE : (q + 1) * WIDE] = codes[at, :]

    pad_f[...] = pad_f[...] - 32768.0
    code[...] = packed(pad_f, lambda g: g * 4)
    temp[...] = half_turn(pad_f[...], False)
    code_right[...] = packed(temp, lambda g: g * 4)

    loads[5].wait()
    loads[6].wait()
    for i in range(2):
        back_even[i * SIDE : i * SIDE + SIDE, :SIDE] = back_raw[i].astype(F32)
    even = back_even[pl.ds(0, SIDE, stride=2), :SIDE]
    odd = back_even[pl.ds(1, SIDE, stride=2), :SIDE]
    back_even[:SIDE, :] = jnp.concatenate([even, odd], axis=1)
    for q in range(PIX // 128):
        back[:2, q * 128 : q * 128 + 128] = back_even[pl.ds(q, 2, stride=32), :]
    back[2:, :] = jnp.zeros((6, PIX), F32)

    pl.semaphore_wait(barrier, expected)

    def remote(src, dst, send, recv, d):
        target_id = place(d) if isinstance(d, int) else (r + d[0], c + d[1])
        return pltpu.make_async_remote_copy(
            src_ref=src, dst_ref=dst, send_sem=send, recv_sem=recv, device_id=target_id, device_id_type=MESH
        )

    pending = []

    def start(copy, ok):
        @pl.when(ok)
        def _():
            copy.start()

        pending.append((copy, ok))

    def arrived(copy, ok):
        @pl.when(ok)
        def _():
            copy.wait_recv()

    def cm_copy(src, slot, d):
        return remote(src, r_cm.at[slot], cm_send.at[slot], cm_recv.at[slot], d)

    def code_copy(source, slot, part, d):
        at = pl.ds(part * (WIDE // PARTS), WIDE // PARTS)
        if source is None:
            source = code_right.at[:, at] if slot == 2 else code.at[:, at]
        else:
            source = r_code.at[source, :, at]
        return remote(source, r_code.at[slot, :, at], r_send.at[slot, part], r_recv.at[slot, part], d)

    start(cm_copy(cm, LEFT, RIGHT), there(RIGHT))
    for part in range(PARTS):
        start(code_copy(None, 2, part, RIGHT), there(RIGHT))
    start(cm_copy(cm, UP, DOWN), there(DOWN))
    for part in range(PARTS):
        start(code_copy(None, 1, part, DOWN), there(DOWN))
    start(cm_copy(cm, RIGHT, LEFT), east)

    arrived(cm_copy(cm, LEFT, LEFT), there(LEFT))
    start(cm_copy(r_cm.at[LEFT], UL, DOWN), there(DOWN) & there(LEFT))
    for part in range(PARTS):
        arrived(code_copy(None, 2, part, LEFT), there(LEFT))
        start(code_copy(2, 0, part, DOWN), there(DOWN) & there(LEFT))
    arrived(cm_copy(cm, UP, UP), there(UP))
    arrived(cm_copy(cm, UL, UL), there(UL))

    def cm_of(tile, rows_at, lanes_at):
        if tile == OWN:
            return cm[rows_at, lanes_at]
        return r_cm[tile, rows_at, lanes_at]

    for g in range(GROUPS):
        for t in range(4):
            at = slice(g * PAD + t * 4, g * PAD + t * 4 + 4)
            near_cm[at, :] = cm_of(TILE_SETS[0][t], slice(g * 4, g * 4 + 4), slice(None))
    near_high, near_low = split(near_cm[:, :FRAMES])

    frame = lax.broadcasted_iota(I32, (NEAR, FRAMES), 1)
    weighted = jnp.where((frame >= window[0]) & (frame < window[1]), near_cm[:, :FRAMES], 0.0)
    w_high, w_low = split(weighted)
    w_both = jnp.concatenate([w_high, w_low], axis=0)
    q4 = nt(w_both, w_both)
    q = q4[:NEAR, :NEAR] + q4[:NEAR, NEAR:] + q4[NEAR:, :NEAR] + q4[NEAR:, NEAR:]
    a_near = near_cm[:, FRAMES : FRAMES + 1].astype(I32)
    b_near = near_cm[:, FRAMES + 1 : FRAMES + 2].astype(I32)
    live_near = near_cm[:, FRAMES + 2 : FRAMES + 3]
    eye = lax.broadcasted_iota(I32, (NEAR, NEAR), 0) == lax.broadcasted_iota(I32, (NEAR, NEAR), 1)
    mass = jnp.sum(jnp.where(eye, q, 0.0), axis=1, keepdims=True)
    inverse = 1.0 / jnp.where(live_near > 0, mass, 1.0)
    q_high, q_low = split(jnp.where(eye, 0.0, q) * inverse)
    q3 = jnp.concatenate([q_high, q_high, q_low], axis=1)
    load0 = jnp.sum(weighted * back_time[0:1, :], axis=1, keepdims=True)
    load1 = jnp.sum(weighted * back_time[1:2, :], axis=1, keepdims=True)

    tile_at = (lax.broadcasted_iota(I32, (NEAR, 1), 0) >> 2) & 3
    above = tile_at < 2
    aside = (tile_at & 1) == 0
    y_low = jnp.where(above, 0, a_near)
    y_high = jnp.where(live_near > 0, jnp.where(above, a_near, SIDE), 0)
    x_low = jnp.where(aside, 0, b_near)
    x_high = jnp.where(aside, b_near, SIDE)

    def covered(rows_at, begin, width):
        spot = lax.broadcasted_iota(I32, (1, width), 1) + begin
        y = spot >> 6
        x = spot & 63
        return (
            (y >= y_low[rows_at]) & (y < y_high[rows_at]) & (x >= x_low[rows_at]) & (x < x_high[rows_at])
        )

    loads[7].wait()
    width = 1024
    for begin in range(0, PIX, width):
        at = slice(begin, begin + width)
        pull = nt(w_high, movie[at, :])
        pull = pull - load0 * back[0:1, at] - load1 * back[1:2, at]
        target[:, at] = jnp.where(covered(slice(None), begin, width), pull * inverse, -BIG)

    for part in range(PARTS):
        arrived(code_copy(None, 1, part, UP), there(UP))
    for part in range(PARTS):
        arrived(code_copy(None, 0, part, UL), there(UL))
    for t in range(3):
        unpacked(r_code[t], canvas, lambda g: g * PAD + t * 4)
    for g in range(GROUPS):
        canvas[g * PAD + 12 : g * PAD + 16, :] = pad_f[g * 4 : g * 4 + 4, :]
    for g in range(GROUPS):
        rows_at = slice(g * PAD, g * PAD + PAD)
        value = jnp.where(covered(rows_at, 0, PIX), (canvas[rows_at, :] + 32768.0) * (1.0 / 65535.0), 0.0)
        high, low = split(value)
        x3[g * PAD : g * PAD + PAD, :] = high
        x3[NEAR + g * PAD : NEAR + g * PAD + PAD, :] = low
        x3[2 * NEAR + g * PAD : 2 * NEAR + g * PAD + PAD, :] = high

    both = x3[: 2 * NEAR, :]
    gram = nt(both, both)
    overlap = gram[:NEAR, :NEAR] + gram[:NEAR, NEAR:] + gram[NEAR:, :NEAR] + gram[NEAR:, NEAR:]
    loading = nt(both, back[...].astype(BF16))
    loading = loading[:NEAR] + loading[NEAR:]
    drive = mm(x3[:NEAR, :], movie[...])
    drive = drive - loading[:, 0:1] * back_time[0:1, :] - loading[:, 1:2] * back_time[1:2, :]
    self_overlap = jnp.sum(jnp.where(eye, overlap, 0.0), axis=1, keepdims=True)
    overlap = jnp.where(eye, 0.0, overlap)
    o_high, o_low = split(overlap)
    product = mm(jnp.concatenate([o_high, o_low], axis=0), near_high)
    shares[:, :FRAMES] = drive - (product[:NEAR] + product[NEAR:] + mm(o_high, near_low))
    shares[:, FRAMES : FRAMES + NEAR] = overlap
    shares[:, FRAMES + NEAR :] = jnp.broadcast_to(self_overlap, (NEAR, 128 - NEAR))
    for t in range(4):
        for g in range(GROUPS):
            share_out[t, g * 4 : g * 4 + 4, :] = shares[g * PAD + t * 4 : g * PAD + t * 4 + 4, :]

    def share_copy(t, d):
        return remote(share_out.at[t], r_share.at[t], s_send.at[t], s_recv.at[t], d)

    for t, d in ((2, LEFT), (0, UL), (1, UP)):
        start(share_copy(t, d), there(d))

    def mate_share(t, k, d):
        return remote(share_out.at[t], r_mate.at[k], mate_send.at[t], mate_recv.at[k], d)

    start(mate_share(3, 0, (0, 1)), west)
    start(mate_share(1, 2, (-1, 1)), west & row_ok(-1))
    start(mate_share(0, 3, (-1, 0)), east & row_ok(-1))

    for g in range(GROUPS):
        rows_at = slice(g * PAD, g * PAD + PAD)
        value = jnp.maximum(target[rows_at, :] - mm(q3[rows_at, :], x3[...]), 0.0)
        canvas[rows_at, :] = jnp.floor(jnp.sqrt(value * (1.0 / TOP)) * 65535.0 + 0.5) - 32768.0
        if g < GROUPS - 1:
            high, low = split(value)
            x3[g * PAD : g * PAD + PAD, :] = high
            x3[NEAR + g * PAD : NEAR + g * PAD + PAD, :] = low
            x3[2 * NEAR + g * PAD : 2 * NEAR + g * PAD + PAD, :] = high

    for t in range(2):
        piece_up[t] = packed(canvas, lambda g: g * PAD + t * 4)

    def piece_copy(t, d):
        return remote(piece_up.at[t], r_piece.at[t], p_send.at[t], p_recv.at[t], d)

    for t in range(2):
        start(piece_copy(t, UP), there(UP) & (c < cols // 2))

    for t, d in ((2, RIGHT), (1, DOWN), (0, DR)):
        arrived(share_copy(t, d), there(d))

    def joined(parts, live):
        total = parts[0] + parts[1] + parts[2] + parts[3]
        scale = 1.0 / jnp.where(live > 0, total[:, FRAMES + NEAR : FRAMES + NEAR + 1], 1.0)
        v = jnp.concatenate([part[:, FRAMES : FRAMES + NEAR] for part in parts], axis=1) * scale
        return total[:, :FRAMES] * scale, v

    def stacked(v):
        return jnp.concatenate(split(v), axis=0)

    goal, v_own = joined([share_out[3], r_share[2], r_share[1], r_share[0]], live_own)
    v_both = stacked(v_own)
    own = cm[:, :FRAMES]
    row_group = lax.broadcasted_iota(I32, (PAD, FRAMES), 0) >> 2

    def changes(sources, g, full, high_ref, low_ref):
        for k in range(4):
            for t in range(4):
                if TILE_SETS[k][t] not in sources:
                    continue
                new = sources[TILE_SETS[k][t]]
                at = slice(k * NEAR + g * PAD + t * 4, k * NEAR + g * PAD + t * 4 + 4)
                full[at, :128] = new[:4, :]
                full[at, 128:] = new[4:, :]
            at = slice(k * NEAR + g * PAD, k * NEAR + g * PAD + PAD)
            high, low = split(full[at, :])
            high_ref[at, :] = high
            low_ref[at, :] = low

    def remaining(aim, v_two, high_ref, low_ref):
        product = mm(v_two, high_ref[...])
        return aim - (product[:PAD] + product[PAD:] + mm(v_two[:PAD], low_ref[...]))

    def updated(g, left_over, old, live):
        chosen = (row_group == g) & (live > 0)
        return jnp.where(chosen, jnp.maximum(left_over, 0.0), old)

    def pack(ref, g, new, old):
        change = new - old
        ref[g, :4, :] = change[g * 4 : g * 4 + 4, :128]
        ref[g, 4:, :] = change[g * 4 : g * 4 + 4, 128:]

    def wave_copy(g, d, slot):
        return remote(wave.at[g], r_wave.at[g, slot], t_send.at[g, slot], t_recv.at[g, slot], d)

    def sends(g, d):
        ok = there(d)
        if DIRS[d][1] > 0:
            ok = ok & jnp.logical_not(west)
        if DIRS[d][1] < 0 and g > 0:
            ok = ok & jnp.logical_not(east)
        return ok

    def gets(g, d):
        ok = there(d)
        if DIRS[d][1] > 0 and g > 0:
            ok = ok & jnp.logical_not(west)
        if DIRS[d][1] < 0:
            ok = ok & jnp.logical_not(east)
        return ok

    def mate_copy(g, at, d, slot):
        return remote(mate_wave.at[g], r_wave.at[g, slot], mw_send.at[g, at], t_recv.at[g, slot], d)

    def far_copy(g, down, right):
        return remote(wave.at[g], r_far.at[g, 1 - down], far_send.at[g, 1 - down], far_recv.at[g, 1 - down], (down, right))

    def outer_copy(at, d):
        return remote(outer_wave, r_far.at[1, 2 - at], ow_send.at[at // 2], far_recv.at[1, 2 - at], d)

    joint_copy = remote(joint, r_joint, joint_sem.at[0], joint_sem.at[1], LEFT)
    outer_sum = remote(outer, r_outer, outer_sem.at[0], outer_sem.at[1], (0, 2))

    sides = (
        (west, 1, RIGHT, UR, DR, {UL: UP, LEFT: OWN, DL: DOWN, UP: UR, OWN: RIGHT, DOWN: DR}, (UR, RIGHT, DR)),
        (east, 0, LEFT, UL, DL, {UR: UP, RIGHT: OWN, DR: DOWN, UP: UL, OWN: LEFT, DOWN: DL}, (UL, LEFT, DL)),
    )

    def start_mate(g):
        for role, first, mate, over, under, _, _ in sides:
            if g < first:
                continue

            @pl.when(role)
            def _(mate=mate):
                r_wave[g, mate] = mate_wave[g]

            start(mate_copy(g, 0, UP, under), role & there(UP))
            start(mate_copy(g, 1, DOWN, over), role & there(DOWN))

    for g in range(GROUPS):
        left_over = goal
        if g == GROUPS - 1:
            arrived(remote(merged, r_merged, m_send, m_recv, RIGHT), there(RIGHT))
            spot = lax.broadcasted_iota(I32, (PAD, PIX), 1)
            y = spot >> 6
            x = spot & 63
            a_int = a_own.astype(I32)
            b_int = b_own.astype(I32)
            unpacked(r_merged[...], far_f, lambda k: k * 4)
            unpacked(r_piece[1], near_f, lambda k: k * 4)
            for k in range(GROUPS):
                temp[k * 4 : k * 4 + 4, :] = canvas[k * PAD + 12 : k * PAD + 16, :]
            near = jnp.where(y < a_int, near_f[...], temp[...])
            pad_f[...] = jnp.where(x < b_int, half_turn(far_f[...], True), near) + 32768.0
            for half in range(2):
                part = slice(half * 8, half * 8 + 8)
                pad_f[part, :] = turn(pad_f[part, :], shift_own[part], False)
            whole = pad_f[...]
            upper = jnp.floor(whole * (1.0 / 256.0))
            hl[:PAD, :] = upper.astype(BF16)
            hl[PAD:, :] = (whole - upper * 256.0).astype(BF16)
            unpick_hl = jnp.concatenate([unpick16 * 256.0, unpick16], axis=1).astype(BF16)
            root = mm(unpick_hl, hl[...])[:SLOTS, :] * (1.0 / 65535.0)
            pad_f[:SLOTS, :] = root * root * TOP
            for q in range(PIX // 128):
                out_shapes[pl.ds(q, SLOTS, stride=32), :] = pad_f[:SLOTS, q * 128 : q * 128 + 128]

        if g > 0:
            for d in (UP, DOWN, LEFT, UL, DL):
                arrived(wave_copy(g - 1, d, d), gets(g - 1, d))
            if g == 1:
                @pl.when(beside_west)
                def _():
                    sources = {d: r_wave[0, d] for d in (UP, DOWN, LEFT, UL, DL)}
                    sources[OWN] = wave[0]
                    changes(sources, 0, mate_f, mate_high, mate_low)
                    aim = jnp.where(live_own > 0, remaining(goal, v_both, mate_high, mate_low), own)
                    for at, value in enumerate((aim, own, v_own)):
                        outer[at, :4, :] = value[4:8, :128]
                        outer[at, 4:, :] = value[4:8, 128:]

                start(outer_sum, beside_west)
            for d in (RIGHT, UR, DR):
                arrived(wave_copy(g - 1, d, d), gets(g - 1, d))
            for role, first, mate, over, under, _, _ in sides:
                if g - 1 >= first:
                    arrived(mate_copy(g - 1, 0, UP, over), role & there(UP))
                    arrived(mate_copy(g - 1, 1, DOWN, under), role & there(DOWN))
            changes({**{d: r_wave[g - 1, d] for d in range(8)}, OWN: wave[g - 1]}, g - 1, call_f, c_high, c_low)
            left_over = remaining(goal, v_both, c_high, c_low)
        new = updated(g, left_over, own, live_own)
        if g < GROUPS - 1:
            pack(wave, g, new, own)
            for d in (UL, DL, LEFT, UR, DR, RIGHT, UP, DOWN):
                start(wave_copy(g, d, 7 - d), sends(g, d))
            if g < 2:
                for down in (-1, 0, 1):
                    if g == 0:
                        start(far_copy(g, down, 2), beside_west & row_ok(down))
                    start(far_copy(g, down, -2), beside_east & row_ok(down))
        own = new
        if g == 0:
            @pl.when(east)
            def _():
                joint[:, :FRAMES] = goal
                joint[:, FRAMES:] = v_own

            start(joint_copy, east)

            for t in range(2):
                start(piece_copy(t, UP), there(UP) & (c >= cols // 2))

            arrived(mate_share(3, 0, (0, -1)), east)
            arrived(mate_share(1, 2, (1, -1)), east & row_ok(1))
            arrived(mate_share(0, 3, (1, 0)), east & row_ok(1))

            @pl.when(east)
            def _():
                mate_cm[...] = r_cm[LEFT]
                r_mate[1] = share_out[2]
                live = mate_cm[:, FRAMES + 2 : FRAMES + 3]
                mate_goal[...], v_mate = joined([r_mate[k] for k in range(4)], live)
                mate_v[...] = stacked(v_mate)
                old = mate_cm[:, :FRAMES]
                pack(mate_wave, 0, updated(0, mate_goal[...], old, live), old)

            start_mate(0)

            for q in range(4):
                for k in range(GROUPS):
                    at = slice(q * SLOTS + k * 3, q * SLOTS + k * 3 + 3)
                    labels[at, :] = r_cm[LEFT, k * 4 : k * 4 + 3, FRAMES:]
            a_left = labels[:, 0:1].astype(I32)
            row = lax.broadcasted_iota(I32, (DENSE, WIDE), 0)
            quarter = (row >= SLOTS).astype(I32) + (row >= 2 * SLOTS).astype(I32) + (row >= 3 * SLOTS).astype(I32)
            below = quarter * 16 + (lax.broadcasted_iota(I32, (DENSE, WIDE), 1) >> 6) < a_left
            left_codes = packed(canvas, lambda k: k * PAD + 8).astype(I32)
            for t in range(2):
                arrived(piece_copy(t, DOWN), there(DOWN))
            merged[...] = jnp.where(below, r_piece[0].astype(I32), left_codes).astype(I16)
            start(remote(merged, r_merged, m_send, m_recv, LEFT), there(LEFT))
        elif g < GROUPS - 1:
            if g == 1:
                arrived(cm_copy(cm, RIGHT, RIGHT), west)
                arrived(joint_copy, west)

                @pl.when(west)
                def _():
                    mate_cm[...] = r_cm[RIGHT]
                    mate_goal[...] = r_joint[:, :FRAMES]
                    mate_v[...] = stacked(r_joint[:, FRAMES:])

            for down in (-1, 0, 1):
                arrived(far_copy(g - 1, -down, -2), west & row_ok(down))
                if g == 1:
                    arrived(far_copy(g - 1, -down, 2), east & row_ok(down))
                elif down:
                    arrived(outer_copy(1 - down, (down, 0)), east & row_ok(down))
            for role, first, mate, over, under, where_at, far_at in sides:
                @pl.when(role)
                def _(where_at=where_at, far_at=far_at):
                    sources = {}
                    for tile, at in where_at.items():
                        sources[tile] = wave[g - 1] if at == OWN else r_wave[g - 1, at]
                    for down, tile in enumerate(far_at):
                        sources[tile] = r_far[g - 1, down]
                    changes(sources, g - 1, mate_f, mate_high, mate_low)
                    old = mate_cm[:, :FRAMES]
                    live = mate_cm[:, FRAMES + 2 : FRAMES + 3]
                    rest = remaining(mate_goal[...], mate_v[...], mate_high, mate_low)
                    pack(mate_wave, g, updated(g, rest, old, live), old)

            start_mate(g)
            if g == 1:
                arrived(outer_sum, east)

                @pl.when(east)
                def _():
                    changes({UR: r_wave[0, UL], RIGHT: r_wave[0, LEFT], DR: r_wave[0, DL]}, 0, outer_f, outer_high, outer_low)
                    zero = jnp.zeros((4, FRAMES), F32)
                    aim, old, v = (
                        jnp.concatenate(
                            [zero, jnp.concatenate([r_outer[at, :4, :], r_outer[at, 4:, :]], axis=1), zero, zero], axis=0
                        )
                        for at in range(3)
                    )
                    value = jnp.maximum(remaining(aim, stacked(v), outer_high, outer_low), 0.0)
                    pack2 = value - old
                    outer_wave[:4, :] = pack2[4:8, :128]
                    outer_wave[4:, :] = pack2[4:8, 128:]
                    r_far[1, 1] = outer_wave[...]

                start(outer_copy(0, UP), east & there(UP))
                start(outer_copy(2, DOWN), east & there(DOWN))

    back_own = jnp.dot(unpick16, own, precision=lax.Precision.HIGHEST, preferred_element_type=F32)
    new_traces = jnp.where(alive_sub[:SLOTS, 0:1], back_own[:SLOTS, :], old_traces)
    for half in range(2):
        out_traces[pl.ds(half, SLOTS, stride=2), :] = new_traces[:, half * 128 : half * 128 + 128]

    for copy, ok in pending:
        @pl.when(ok)
        def _(copy=copy):
            copy.wait_send()


def on_device(rows, cols, movie, footprints, anchors, groups, counts, temporal, back_spatial, back_temporal, window):
    vmem = pl.BlockSpec(memory_space=pltpu.VMEM)
    dma = pltpu.SemaphoreType.DMA
    shapes, traces = pl.pallas_call(
        functools.partial(kernel, rows, cols),
        out_shape=(
            jax.ShapeDtypeStruct((SLOTS * PIX // 128, 128), F32),
            jax.ShapeDtypeStruct((SLOTS * FRAMES // 128, 128), F32),
        ),
        in_specs=[pl.BlockSpec(memory_space=pltpu.SMEM)] + [pl.BlockSpec(memory_space=pltpu.HBM)] * 8,
        out_specs=(vmem, vmem),
        scratch_shapes=[
            pltpu.SMEM((2, SLOTS), I32),
            pltpu.SMEM((1, SLOTS), I32),
            pltpu.SMEM((2,), I32),
            pltpu.VMEM((SLOTS * PIX // 128, 128), F32),
            pltpu.VMEM((SLOTS * FRAMES // 128, 128), F32),
            pltpu.VMEM((2, SIDE, SIDE), BF16),
            pltpu.VMEM((2, FRAMES), F32),
            pltpu.VMEM((PIX, FRAMES), BF16),
            pltpu.VMEM((2 * SIDE, 2 * SIDE), F32),
            pltpu.VMEM((8, PIX), F32),
            pltpu.VMEM((PAD, PIX), F32),
            pltpu.VMEM((2 * PAD, PIX), BF16),
            pltpu.VMEM((DENSE, WIDE), I16),
            pltpu.VMEM((DENSE, WIDE), I16),
            pltpu.VMEM((3, DENSE, WIDE), I16),
            pltpu.VMEM((PAD, FRAMES + 128), F32),
            pltpu.VMEM((8, PAD, FRAMES + 128), F32),
            pltpu.VMEM((NEAR, FRAMES + 128), F32),
            pltpu.VMEM((NEAR, PIX), F32),
            pltpu.VMEM((NEAR, PIX), F32),
            pltpu.VMEM((3 * NEAR, PIX), BF16),
            pltpu.VMEM((NEAR, FRAMES + 128), F32),
            pltpu.VMEM((4, PAD, FRAMES + 128), F32),
            pltpu.VMEM((3, PAD, FRAMES + 128), F32),
            pltpu.VMEM((3, 8, 128), F32),
            pltpu.VMEM((3, 8, 8, 128), F32),
            pltpu.VMEM((4 * NEAR, FRAMES), F32),
            pltpu.VMEM((4 * NEAR, FRAMES), BF16),
            pltpu.VMEM((4 * NEAR, FRAMES), BF16),
            pltpu.VMEM((PAD, PIX), F32),
            pltpu.VMEM((DENSE, WIDE), F32),
            pltpu.VMEM((DENSE, 128), F32),
            pltpu.VMEM((PAD, PIX), F32),
            pltpu.VMEM((PAD, PIX), F32),
            pltpu.VMEM((4, PAD, FRAMES + 128), F32),
            pltpu.VMEM((PAD, FRAMES + 128), F32),
            pltpu.VMEM((PAD, FRAMES), F32),
            pltpu.VMEM((2 * PAD, 4 * NEAR), BF16),
            pltpu.VMEM((3, 8, 128), F32),
            pltpu.VMEM((2, 3, 8, 128), F32),
            pltpu.VMEM((4 * NEAR, FRAMES), F32),
            pltpu.VMEM((4 * NEAR, FRAMES), BF16),
            pltpu.VMEM((4 * NEAR, FRAMES), BF16),
            pltpu.VMEM((PAD, 2 * FRAMES), F32),
            pltpu.VMEM((PAD, 2 * FRAMES), F32),
            pltpu.VMEM((3, 8, 128), F32),
            pltpu.VMEM((3, 8, 128), F32),
            pltpu.VMEM((8, 128), F32),
            pltpu.VMEM((4 * NEAR, FRAMES), F32),
            pltpu.VMEM((4 * NEAR, FRAMES), BF16),
            pltpu.VMEM((4 * NEAR, FRAMES), BF16),
            pltpu.VMEM((2, DENSE, WIDE), I16),
            pltpu.VMEM((2, DENSE, WIDE), I16),
            pltpu.VMEM((DENSE, WIDE), I16),
            pltpu.VMEM((DENSE, WIDE), I16),
            dma((8,)),
            dma((8,)),
            dma((8,)),
            dma((3, PARTS)),
            dma((3, PARTS)),
            dma((3,)),
            dma((3,)),
            dma((3, 8)),
            dma((3, 8)),
            dma((2,)),
            dma((2,)),
            dma,
            dma,
            dma((4,)),
            dma((4,)),
            dma((3, 2)),
            dma((2, 3)),
            dma((2, 3)),
            dma((2,)),
            dma((2,)),
            dma((2,)),
        ],
        compiler_params=pltpu.CompilerParams(collective_id=0, has_side_effects=True, vmem_limit_bytes=32 << 20),
    )(
        counts,
        *(
            pltpu.with_memory_space_constraint(x, pltpu.HBM)
            for x in (
                anchors.reshape(SLOTS, 2).T,
                groups.reshape(1, SLOTS),
                window,
                footprints.reshape(SLOTS * PIX // 128, 128),
                temporal.reshape(SLOTS * FRAMES // 128, 128),
                back_spatial,
                back_temporal,
                movie.reshape(PIX, FRAMES),
            )
        )
    )
    return shapes.reshape(1, 1, SLOTS, PIX), traces.reshape(1, 1, SLOTS, FRAMES)


def solution(mesh):
    return jax.shard_map(
        functools.partial(on_device, mesh.shape["row"], mesh.shape["col"]),
        mesh=mesh,
        in_specs=(
            P("row", "col", None),
            P("row", "col", None, None),
            P("row", "col", None, None),
            P("row", "col", None),
            P("row", "col"),
            P("row", "col", None, None),
            P(None, "row", "col"),
            P(),
            P(),
        ),
        out_specs=(P("row", "col", None, None), P("row", "col", None, None)),
        check_vma=False,
    )
```

```python
import functools

import jax
import jax.numpy as jnp
from jax import lax
from jax.experimental import pallas as pl
from jax.experimental.pallas import tpu as pltpu
from jax.sharding import PartitionSpec as P

MESH = pl.DeviceIdType.MESH
F32 = jnp.float32
BF16 = jnp.bfloat16
I32 = jnp.int32
I16 = jnp.int16

SIDE = 64
PIX = SIDE * SIDE
FRAMES = 256
SLOTS = 12
GROUPS = 4
PAD = 16
NEAR = 4 * PAD
BIG = 1e30
DENSE = 4 * SLOTS
WIDE = PIX // 4
TOP = 8.0

DIRS = ((-1, -1), (-1, 0), (-1, 1), (0, -1), (0, 1), (1, -1), (1, 0), (1, 1))
UL, UP, UR, LEFT, RIGHT, DL, DOWN, DR = range(8)
OWN = 8
TILE_SETS = (
    (UL, UP, LEFT, OWN),
    (UP, UR, OWN, RIGHT),
    (LEFT, OWN, DL, DOWN),
    (OWN, RIGHT, DOWN, DR),
)
PARTS = 4


def nt(a, b):
    return lax.dot_general(a, b, (((1,), (1,)), ((), ())), preferred_element_type=F32)


def mm(a, b):
    return jnp.dot(a, b, preferred_element_type=F32)


def split(x):
    high = x.astype(BF16)
    return high, (x - high.astype(F32)).astype(BF16)


def turn(x, shift, forward):
    for bit in range(12):
        step = 1 << bit
        chosen = ((shift >> bit) & 1) == 1
        by = step if forward else PIX - step
        if by % 128 == 0:
            moved = jnp.concatenate([x[:, PIX - by :], x[:, : PIX - by]], axis=1)
        else:
            moved = pltpu.roll(x, by, 1)
        x = jnp.where(chosen, moved, x)
    return x


def half_turn(x, forward):
    return pltpu.roll(x, SIDE if forward else PIX - SIDE, 1)


def kernel(
    rows, cols,
    counts, anchors_in, groups_in, window_in, footprints_in, temporal_in, back_in, back_time_in, movie_in,
    out_shapes, out_traces,
    anchors, groups, window, footprints, temporal, back_raw, back_time, movie, back_even, back, pad_f, hl, code, code_right, r_code, cm, r_cm, near_cm, target, canvas, x3,
    shares, share_out, r_share, wave, r_wave, call_f, c_high, c_low, temp, dense, labels, far_f, near_f,
    r_mate, mate_cm, mate_goal, mate_v, mate_wave, r_far, mate_f, mate_high, mate_low,
    joint, r_joint, outer, r_outer, outer_wave, outer_f, outer_high, outer_low,
    piece_up, r_piece, merged, r_merged,
    load_sem, cm_send, cm_recv, r_send, r_recv, s_send, s_recv, t_send, t_recv, p_send, p_recv, m_send, m_recv,
    mate_send, mate_recv, mw_send, far_send, far_recv, joint_sem, outer_sem, ow_send,
):
    r = lax.axis_index("row")
    c = lax.axis_index("col")

    def there(d):
        down, right = DIRS[d]
        ok = None
        for at, step, count in ((r, down, rows), (c, right, cols)):
            if step:
                one = at + step >= 0 if step < 0 else at + step < count
                ok = one if ok is None else ok & one
        return ok

    def place(d):
        return (r + DIRS[d][0], c + DIRS[d][1])

    west = c == cols // 2 - 1
    east = c == cols // 2
    beside_west = c == cols // 2 - 2
    beside_east = c == cols // 2 + 1

    def row_ok(step):
        return (r + step >= 0) & (r + step < rows)

    barrier = pltpu.get_barrier_semaphore()

    loads = [
        pltpu.make_async_copy(source, target_ref, load_sem.at[at])
        for at, (source, target_ref) in enumerate(
            (
                (groups_in, groups),
                (anchors_in, anchors),
                (window_in, window),
                (temporal_in, temporal),
                (footprints_in, footprints),
                (back_time_in, back_time),
                (back_in, back_raw),
                (movie_in, movie),
            )
        )
    ]
    for load in loads:
        load.start()

    expected = 0
    for d in range(8):
        ok = there(d)

        @pl.when(ok)
        def _(d=d):
            pl.semaphore_signal(barrier, inc=1, device_id=place(d), device_id_type=MESH)

        expected = expected + ok.astype(I32)
    for down in (-1, 0, 1):
        for right, receiver, sender in ((2, west, beside_east), (-2, east, beside_west)):
            @pl.when(receiver & row_ok(down))
            def _(down=down, right=right):
                pl.semaphore_signal(barrier, inc=1, device_id=(r + down, c + right), device_id_type=MESH)

            expected = expected + (sender & row_ok(down)).astype(I32)

    for d in range(8):
        @pl.when(jnp.logical_not(there(d)))
        def _(d=d):
            r_cm[d] = jnp.zeros((PAD, FRAMES + 128), F32)
            for g in range(3):
                r_wave[g, d] = jnp.zeros((8, 128), F32)

    for t, d in ((0, DR), (1, DOWN), (2, RIGHT)):
        @pl.when(jnp.logical_not(there(d)))
        def _(t=t):
            r_share[t] = jnp.zeros((PAD, FRAMES + 128), F32)

    @pl.when(jnp.logical_not(row_ok(1)))
    def _():
        r_mate[2] = jnp.zeros((PAD, FRAMES + 128), F32)
        r_mate[3] = jnp.zeros((PAD, FRAMES + 128), F32)

    for down in (-1, 1):
        @pl.when(jnp.logical_not(row_ok(down)))
        def _(down=down):
            for g in range(2):
                r_far[g, 1 + down] = jnp.zeros((8, 128), F32)

    for ref in (call_f, c_high, c_low, far_f, near_f, mate_f, mate_high, mate_low, outer_f, outer_high, outer_low):
        ref[...] = jnp.zeros_like(ref)

    for load in loads[:4]:
        load.wait()
    sub = lax.broadcasted_iota(I32, (PAD, 128), 0)
    lane = lax.broadcasted_iota(I32, (PAD, 128), 1)
    g_sub = jnp.full((PAD, 128), -1, I32)
    g_lane = jnp.full((PAD, 128), -1, I32)
    a_lane = jnp.zeros((PAD, 128), I32)
    b_lane = jnp.zeros((PAD, 128), I32)
    count = counts[0, 0]
    for m in range(SLOTS):
        g_sub = jnp.where(sub == m, groups[0, m], g_sub)
        g_lane = jnp.where(lane == m, groups[0, m], g_lane)
        a_lane = jnp.where(lane == m, anchors[0, m], a_lane)
        b_lane = jnp.where(lane == m, anchors[1, m], b_lane)
    alive_lane = lane < count
    alive_sub = sub < count
    a_lane = jnp.where(alive_lane, a_lane, 0)
    b_lane = jnp.where(alive_lane, b_lane, 0)
    same = g_sub == g_lane
    before_lane = jnp.sum(jnp.where(same & (sub < lane), 1.0, 0.0), axis=0, keepdims=True)
    before_sub = jnp.sum(jnp.where(same & (lane < sub), 1.0, 0.0), axis=1, keepdims=True)
    pos_lane = g_lane.astype(F32) * 4.0 + before_lane
    pos_sub = g_sub.astype(F32) * 4.0 + before_sub
    pick = jnp.where((sub.astype(F32) == pos_lane) & (lane < SLOTS), 1.0, 0.0)
    unpick = jnp.where((lane.astype(F32) == pos_sub) & (sub < SLOTS), 1.0, 0.0)
    a_own = jnp.sum(pick * a_lane.astype(F32), axis=1, keepdims=True)
    b_own = jnp.sum(pick * b_lane.astype(F32), axis=1, keepdims=True)
    live_own = jnp.sum(pick * jnp.where(alive_lane, 1.0, 0.0), axis=1, keepdims=True)
    shift_own = (a_own * float(SIDE) + b_own).astype(I32)
    pick16 = pick[:, :PAD]
    unpick16 = unpick[:, :PAD]

    pad_f[SLOTS:PAD, :] = jnp.zeros((PAD - SLOTS, PIX), F32)
    for half in range(2):
        pad_f[:SLOTS, half * 128 : half * 128 + 128] = temporal[pl.ds(half, SLOTS, stride=2), :]
    old_traces = pad_f[:SLOTS, :FRAMES]
    cm[:, :FRAMES] = jnp.dot(pick16, pad_f[:, :FRAMES], precision=lax.Precision.HIGHEST, preferred_element_type=F32)
    cm[:, FRAMES:] = jnp.where(lane == 0, a_own, jnp.where(lane == 1, b_own, jnp.where(lane == 2, live_own, 0.0)))

    loads[4].wait()
    for q in range(PIX // 128):
        pad_f[:SLOTS, q * 128 : q * 128 + 128] = footprints[pl.ds(q, SLOTS, stride=32), :]
    whole = jnp.floor(pad_f[...] * 65535.0 + 0.5)
    upper = jnp.floor(whole * (1.0 / 256.0))
    hl[:PAD, :] = upper.astype(BF16)
    hl[PAD:, :] = (whole - upper * 256.0).astype(BF16)
    pick_hl = jnp.concatenate([pick16 * 256.0, pick16], axis=1).astype(BF16)
    pad_f[...] = mm(pick_hl, hl[...])
    for half in range(2):
        part = slice(half * 8, half * 8 + 8)
        pad_f[part, :] = turn(pad_f[part, :], shift_own[part], True)

    def packed(ref, row_of):
        for q in range(4):
            for g in range(GROUPS):
                at = slice(q * SLOTS + g * 3, q * SLOTS + g * 3 + 3)
                dense[at, :] = ref[row_of(g) : row_of(g) + 3, q * WIDE : (q + 1) * WIDE]
        return dense[...].astype(I32).astype(I16)

    def unpacked(codes, ref, row_of):
        codes = codes.astype(I32).astype(F32)
        for q in range(4):
            for g in range(GROUPS):
                at = slice(q * SLOTS + g * 3, q * SLOTS + g * 3 + 3)
                ref[row_of(g) : row_of(g) + 3, q * WIDE : (q + 1) * WIDE] = codes[at, :]

    pad_f[...] = pad_f[...] - 32768.0
    code[...] = packed(pad_f, lambda g: g * 4)
    temp[...] = half_turn(pad_f[...], False)
    code_right[...] = packed(temp, lambda g: g * 4)

    loads[5].wait()
    loads[6].wait()
    for i in range(2):
        back_even[i * SIDE : i * SIDE + SIDE, :SIDE] = back_raw[i].astype(F32)
    even = back_even[pl.ds(0, SIDE, stride=2), :SIDE]
    odd = back_even[pl.ds(1, SIDE, stride=2), :SIDE]
    back_even[:SIDE, :] = jnp.concatenate([even, odd], axis=1)
    for q in range(PIX // 128):
        back[:2, q * 128 : q * 128 + 128] = back_even[pl.ds(q, 2, stride=32), :]
    back[2:, :] = jnp.zeros((14, PIX), F32)
    x3[3 * NEAR :, :] = back[...].astype(BF16)

    pl.semaphore_wait(barrier, expected)

    def remote(src, dst, send, recv, d):
        target_id = place(d) if isinstance(d, int) else (r + d[0], c + d[1])
        return pltpu.make_async_remote_copy(
            src_ref=src, dst_ref=dst, send_sem=send, recv_sem=recv, device_id=target_id, device_id_type=MESH
        )

    pending = []

    def start(copy, ok):
        @pl.when(ok)
        def _():
            copy.start()

        pending.append((copy, ok))

    def arrived(copy, ok):
        @pl.when(ok)
        def _():
            copy.wait_recv()

    def cm_copy(src, slot, d):
        return remote(src, r_cm.at[slot], cm_send.at[slot], cm_recv.at[slot], d)

    def code_copy(source, slot, part, d):
        at = pl.ds(part * (WIDE // PARTS), WIDE // PARTS)
        if source is None:
            source = code_right.at[:, at] if slot == 2 else code.at[:, at]
        else:
            source = r_code.at[source, :, at]
        return remote(source, r_code.at[slot, :, at], r_send.at[slot, part], r_recv.at[slot, part], d)

    start(cm_copy(cm, LEFT, RIGHT), there(RIGHT))
    for part in range(PARTS):
        start(code_copy(None, 2, part, RIGHT), there(RIGHT))
    start(cm_copy(cm, UP, DOWN), there(DOWN))
    for part in range(PARTS):
        start(code_copy(None, 1, part, DOWN), there(DOWN))
    start(cm_copy(cm, RIGHT, LEFT), east)

    arrived(cm_copy(cm, LEFT, LEFT), there(LEFT))
    start(cm_copy(r_cm.at[LEFT], UL, DOWN), there(DOWN) & there(LEFT))
    for part in range(PARTS):
        arrived(code_copy(None, 2, part, LEFT), there(LEFT))
        start(code_copy(2, 0, part, DOWN), there(DOWN) & there(LEFT))
    arrived(cm_copy(cm, UP, UP), there(UP))
    arrived(cm_copy(cm, UL, UL), there(UL))

    def cm_of(tile, rows_at, lanes_at):
        if tile == OWN:
            return cm[rows_at, lanes_at]
        return r_cm[tile, rows_at, lanes_at]

    for g in range(GROUPS):
        for t in range(4):
            at = slice(g * PAD + t * 4, g * PAD + t * 4 + 4)
            near_cm[at, :] = cm_of(TILE_SETS[0][t], slice(g * 4, g * 4 + 4), slice(None))
    near_high, near_low = split(near_cm[:, :FRAMES])

    frame = lax.broadcasted_iota(I32, (NEAR, FRAMES), 1)
    weighted = jnp.where((frame >= window[0]) & (frame < window[1]), near_cm[:, :FRAMES], 0.0)
    w_high, w_low = split(weighted)
    w_both = jnp.concatenate([w_high, w_low], axis=0)
    q4 = nt(w_both, w_both)
    q = q4[:NEAR, :NEAR] + q4[:NEAR, NEAR:] + q4[NEAR:, :NEAR] + q4[NEAR:, NEAR:]
    a_near = near_cm[:, FRAMES : FRAMES + 1].astype(I32)
    b_near = near_cm[:, FRAMES + 1 : FRAMES + 2].astype(I32)
    live_near = near_cm[:, FRAMES + 2 : FRAMES + 3]
    eye = lax.broadcasted_iota(I32, (NEAR, NEAR), 0) == lax.broadcasted_iota(I32, (NEAR, NEAR), 1)
    mass = jnp.sum(jnp.where(eye, q, 0.0), axis=1, keepdims=True)
    inverse = 1.0 / jnp.where(live_near > 0, mass, 1.0)
    q_high, q_low = split(jnp.where(eye, 0.0, q) * inverse)
    q3 = jnp.concatenate([q_high, q_high, q_low], axis=1)
    load0 = jnp.sum(weighted * back_time[0:1, :], axis=1, keepdims=True)
    load1 = jnp.sum(weighted * back_time[1:2, :], axis=1, keepdims=True)

    tile_at = (lax.broadcasted_iota(I32, (NEAR, 1), 0) >> 2) & 3
    above = tile_at < 2
    aside = (tile_at & 1) == 0
    y_low = jnp.where(above, 0, a_near)
    y_high = jnp.where(live_near > 0, jnp.where(above, a_near, SIDE), 0)
    x_low = jnp.where(aside, 0, b_near)
    x_high = jnp.where(aside, b_near, SIDE)

    def covered(rows_at, begin, width):
        spot = lax.broadcasted_iota(I32, (1, width), 1) + begin
        y = spot >> 6
        x = spot & 63
        return (
            (y >= y_low[rows_at]) & (y < y_high[rows_at]) & (x >= x_low[rows_at]) & (x < x_high[rows_at])
        )

    loads[7].wait()
    width = 1024
    for begin in range(0, PIX, width):
        at = slice(begin, begin + width)
        pull = nt(w_high, movie[at, :])
        pull = pull - load0 * back[0:1, at] - load1 * back[1:2, at]
        target[:, at] = jnp.where(covered(slice(None), begin, width), pull * inverse, -BIG)

    for part in range(PARTS):
        arrived(code_copy(None, 1, part, UP), there(UP))
    for part in range(PARTS):
        arrived(code_copy(None, 0, part, UL), there(UL))
    for t in range(3):
        unpacked(r_code[t], canvas, lambda g: g * PAD + t * 4)
    for g in range(GROUPS):
        canvas[g * PAD + 12 : g * PAD + 16, :] = pad_f[g * 4 : g * 4 + 4, :]
    for g in range(GROUPS):
        rows_at = slice(g * PAD, g * PAD + PAD)
        value = jnp.where(covered(rows_at, 0, PIX), (canvas[rows_at, :] + 32768.0) * (1.0 / 65535.0), 0.0)
        high, low = split(value)
        x3[g * PAD : g * PAD + PAD, :] = high
        x3[NEAR + g * PAD : NEAR + g * PAD + PAD, :] = low
        x3[2 * NEAR + g * PAD : 2 * NEAR + g * PAD + PAD, :] = high

    gram = nt(x3[: 2 * NEAR, :], x3[NEAR:, :])
    gram = gram[:NEAR] + gram[NEAR:]
    overlap = gram[:, :NEAR] + gram[:, NEAR : 2 * NEAR]
    loading = gram[:, 2 * NEAR : 2 * NEAR + 2]
    drive = mm(x3[:NEAR, :], movie[...])
    drive = drive - loading[:, 0:1] * back_time[0:1, :] - loading[:, 1:2] * back_time[1:2, :]
    self_overlap = jnp.sum(jnp.where(eye, overlap, 0.0), axis=1, keepdims=True)
    overlap = jnp.where(eye, 0.0, overlap)
    o_high, o_low = split(overlap)
    product = mm(jnp.concatenate([o_high, o_low], axis=0), near_high)
    shares[:, :FRAMES] = drive - (product[:NEAR] + product[NEAR:] + mm(o_high, near_low))
    shares[:, FRAMES : FRAMES + NEAR] = overlap
    shares[:, FRAMES + NEAR :] = jnp.broadcast_to(self_overlap, (NEAR, 128 - NEAR))
    for t in range(4):
        for g in range(GROUPS):
            share_out[t, g * 4 : g * 4 + 4, :] = shares[g * PAD + t * 4 : g * PAD + t * 4 + 4, :]

    def share_copy(t, d):
        return remote(share_out.at[t], r_share.at[t], s_send.at[t], s_recv.at[t], d)

    for t, d in ((2, LEFT), (0, UL), (1, UP)):
        start(share_copy(t, d), there(d))

    def mate_share(t, k, d):
        return remote(share_out.at[t], r_mate.at[k], mate_send.at[t], mate_recv.at[k], d)

    start(mate_share(3, 0, (0, 1)), west)
    start(mate_share(1, 2, (-1, 1)), west & row_ok(-1))
    start(mate_share(0, 3, (-1, 0)), east & row_ok(-1))

    for g in range(GROUPS):
        rows_at = slice(g * PAD, g * PAD + PAD)
        value = jnp.maximum(target[rows_at, :] - mm(q3[rows_at, :], x3[: 3 * NEAR, :]), 0.0)
        canvas[rows_at, :] = jnp.floor(jnp.sqrt(value * (1.0 / TOP)) * 65535.0 + 0.5) - 32768.0
        if g < GROUPS - 1:
            high, low = split(value)
            x3[g * PAD : g * PAD + PAD, :] = high
            x3[NEAR + g * PAD : NEAR + g * PAD + PAD, :] = low
            x3[2 * NEAR + g * PAD : 2 * NEAR + g * PAD + PAD, :] = high

    for t in range(2):
        piece_up[t] = packed(canvas, lambda g: g * PAD + t * 4)

    def piece_copy(t, d):
        return remote(piece_up.at[t], r_piece.at[t], p_send.at[t], p_recv.at[t], d)

    for t in range(2):
        start(piece_copy(t, UP), there(UP) & (c < cols // 2))

    for t, d in ((2, RIGHT), (1, DOWN), (0, DR)):
        arrived(share_copy(t, d), there(d))

    def joined(parts, live):
        total = parts[0] + parts[1] + parts[2] + parts[3]
        scale = 1.0 / jnp.where(live > 0, total[:, FRAMES + NEAR : FRAMES + NEAR + 1], 1.0)
        v = jnp.concatenate([part[:, FRAMES : FRAMES + NEAR] for part in parts], axis=1) * scale
        return total[:, :FRAMES] * scale, v

    def stacked(v):
        return jnp.concatenate(split(v), axis=0)

    goal, v_own = joined([share_out[3], r_share[2], r_share[1], r_share[0]], live_own)
    v_both = stacked(v_own)
    own = cm[:, :FRAMES]
    row_group = lax.broadcasted_iota(I32, (PAD, FRAMES), 0) >> 2

    def changes(sources, g, full, high_ref, low_ref):
        for k in range(4):
            for t in range(4):
                if TILE_SETS[k][t] not in sources:
                    continue
                new = sources[TILE_SETS[k][t]]
                at = slice(k * NEAR + g * PAD + t * 4, k * NEAR + g * PAD + t * 4 + 4)
                full[at, :128] = new[:4, :]
                full[at, 128:] = new[4:, :]
            at = slice(k * NEAR + g * PAD, k * NEAR + g * PAD + PAD)
            high, low = split(full[at, :])
            high_ref[at, :] = high
            low_ref[at, :] = low

    def remaining(aim, v_two, high_ref, low_ref):
        product = mm(v_two, high_ref[...])
        return aim - (product[:PAD] + product[PAD:] + mm(v_two[:PAD], low_ref[...]))

    def updated(g, left_over, old, live):
        chosen = (row_group == g) & (live > 0)
        return jnp.where(chosen, jnp.maximum(left_over, 0.0), old)

    def pack(ref, g, new, old):
        change = new - old
        ref[g, :4, :] = change[g * 4 : g * 4 + 4, :128]
        ref[g, 4:, :] = change[g * 4 : g * 4 + 4, 128:]

    def wave_copy(g, d, slot):
        return remote(wave.at[g], r_wave.at[g, slot], t_send.at[g, slot], t_recv.at[g, slot], d)

    def sends(g, d):
        ok = there(d)
        if DIRS[d][1] > 0:
            ok = ok & jnp.logical_not(west)
        if DIRS[d][1] < 0 and g > 0:
            ok = ok & jnp.logical_not(east)
        return ok

    def gets(g, d):
        ok = there(d)
        if DIRS[d][1] > 0 and g > 0:
            ok = ok & jnp.logical_not(west)
        if DIRS[d][1] < 0:
            ok = ok & jnp.logical_not(east)
        return ok

    def mate_copy(g, at, d, slot):
        return remote(mate_wave.at[g], r_wave.at[g, slot], mw_send.at[g, at], t_recv.at[g, slot], d)

    def far_copy(g, down, right):
        return remote(wave.at[g], r_far.at[g, 1 - down], far_send.at[g, 1 - down], far_recv.at[g, 1 - down], (down, right))

    def outer_copy(at, d):
        return remote(outer_wave, r_far.at[1, 2 - at], ow_send.at[at // 2], far_recv.at[1, 2 - at], d)

    joint_copy = remote(joint, r_joint, joint_sem.at[0], joint_sem.at[1], LEFT)
    outer_sum = remote(outer, r_outer, outer_sem.at[0], outer_sem.at[1], (0, 2))

    sides = (
        (west, 1, RIGHT, UR, DR, {UL: UP, LEFT: OWN, DL: DOWN, UP: UR, OWN: RIGHT, DOWN: DR}, (UR, RIGHT, DR)),
        (east, 0, LEFT, UL, DL, {UR: UP, RIGHT: OWN, DR: DOWN, UP: UL, OWN: LEFT, DOWN: DL}, (UL, LEFT, DL)),
    )

    def start_mate(g):
        for role, first, mate, over, under, _, _ in sides:
            if g < first:
                continue

            @pl.when(role)
            def _(mate=mate):
                r_wave[g, mate] = mate_wave[g]

            start(mate_copy(g, 0, UP, under), role & there(UP))
            start(mate_copy(g, 1, DOWN, over), role & there(DOWN))

    for g in range(GROUPS):
        left_over = goal
        if g == GROUPS - 1:
            arrived(remote(merged, r_merged, m_send, m_recv, RIGHT), there(RIGHT))
            spot = lax.broadcasted_iota(I32, (PAD, PIX), 1)
            y = spot >> 6
            x = spot & 63
            a_int = a_own.astype(I32)
            b_int = b_own.astype(I32)
            unpacked(r_merged[...], far_f, lambda k: k * 4)
            unpacked(r_piece[1], near_f, lambda k: k * 4)
            for k in range(GROUPS):
                temp[k * 4 : k * 4 + 4, :] = canvas[k * PAD + 12 : k * PAD + 16, :]
            near = jnp.where(y < a_int, near_f[...], temp[...])
            pad_f[...] = jnp.where(x < b_int, half_turn(far_f[...], True), near) + 32768.0
            for half in range(2):
                part = slice(half * 8, half * 8 + 8)
                pad_f[part, :] = turn(pad_f[part, :], shift_own[part], False)
            whole = pad_f[...]
            upper = jnp.floor(whole * (1.0 / 256.0))
            hl[:PAD, :] = upper.astype(BF16)
            hl[PAD:, :] = (whole - upper * 256.0).astype(BF16)
            unpick_hl = jnp.concatenate([unpick16 * 256.0, unpick16], axis=1).astype(BF16)
            root = mm(unpick_hl, hl[...])[:SLOTS, :] * (1.0 / 65535.0)
            pad_f[:SLOTS, :] = root * root * TOP
            for q in range(PIX // 128):
                out_shapes[pl.ds(q, SLOTS, stride=32), :] = pad_f[:SLOTS, q * 128 : q * 128 + 128]

        if g > 0:
            for d in (UP, DOWN, LEFT, UL, DL):
                arrived(wave_copy(g - 1, d, d), gets(g - 1, d))
            if g == 1:
                @pl.when(beside_west)
                def _():
                    sources = {d: r_wave[0, d] for d in (UP, DOWN, LEFT, UL, DL)}
                    sources[OWN] = wave[0]
                    changes(sources, 0, mate_f, mate_high, mate_low)
                    aim = jnp.where(live_own > 0, remaining(goal, v_both, mate_high, mate_low), own)
                    for at, value in enumerate((aim, own, v_own)):
                        outer[at, :4, :] = value[4:8, :128]
                        outer[at, 4:, :] = value[4:8, 128:]

                start(outer_sum, beside_west)
            for d in (RIGHT, UR, DR):
                arrived(wave_copy(g - 1, d, d), gets(g - 1, d))
            for role, first, mate, over, under, _, _ in sides:
                if g - 1 >= first:
                    arrived(mate_copy(g - 1, 0, UP, over), role & there(UP))
                    arrived(mate_copy(g - 1, 1, DOWN, under), role & there(DOWN))
            changes({**{d: r_wave[g - 1, d] for d in range(8)}, OWN: wave[g - 1]}, g - 1, call_f, c_high, c_low)
            left_over = remaining(goal, v_both, c_high, c_low)
        new = updated(g, left_over, own, live_own)
        if g < GROUPS - 1:
            pack(wave, g, new, own)
            for d in (UL, DL, LEFT, UR, DR, RIGHT, UP, DOWN):
                start(wave_copy(g, d, 7 - d), sends(g, d))
            if g < 2:
                for down in (-1, 0, 1):
                    if g == 0:
                        start(far_copy(g, down, 2), beside_west & row_ok(down))
                    start(far_copy(g, down, -2), beside_east & row_ok(down))
        own = new
        if g == 0:
            @pl.when(east)
            def _():
                joint[:, :FRAMES] = goal
                joint[:, FRAMES:] = v_own

            start(joint_copy, east)

            for t in range(2):
                start(piece_copy(t, UP), there(UP) & (c >= cols // 2))

            arrived(mate_share(3, 0, (0, -1)), east)
            arrived(mate_share(1, 2, (1, -1)), east & row_ok(1))
            arrived(mate_share(0, 3, (1, 0)), east & row_ok(1))

            @pl.when(east)
            def _():
                mate_cm[...] = r_cm[LEFT]
                r_mate[1] = share_out[2]
                live = mate_cm[:, FRAMES + 2 : FRAMES + 3]
                mate_goal[...], v_mate = joined([r_mate[k] for k in range(4)], live)
                mate_v[...] = stacked(v_mate)
                old = mate_cm[:, :FRAMES]
                pack(mate_wave, 0, updated(0, mate_goal[...], old, live), old)

            start_mate(0)

            for q in range(4):
                for k in range(GROUPS):
                    at = slice(q * SLOTS + k * 3, q * SLOTS + k * 3 + 3)
                    labels[at, :] = r_cm[LEFT, k * 4 : k * 4 + 3, FRAMES:]
            a_left = labels[:, 0:1].astype(I32)
            row = lax.broadcasted_iota(I32, (DENSE, WIDE), 0)
            quarter = (row >= SLOTS).astype(I32) + (row >= 2 * SLOTS).astype(I32) + (row >= 3 * SLOTS).astype(I32)
            below = quarter * 16 + (lax.broadcasted_iota(I32, (DENSE, WIDE), 1) >> 6) < a_left
            left_codes = packed(canvas, lambda k: k * PAD + 8).astype(I32)
            for t in range(2):
                arrived(piece_copy(t, DOWN), there(DOWN))
            merged[...] = jnp.where(below, r_piece[0].astype(I32), left_codes).astype(I16)
            start(remote(merged, r_merged, m_send, m_recv, LEFT), there(LEFT))
        elif g < GROUPS - 1:
            if g == 1:
                arrived(cm_copy(cm, RIGHT, RIGHT), west)
                arrived(joint_copy, west)

                @pl.when(west)
                def _():
                    mate_cm[...] = r_cm[RIGHT]
                    mate_goal[...] = r_joint[:, :FRAMES]
                    mate_v[...] = stacked(r_joint[:, FRAMES:])

            for down in (-1, 0, 1):
                arrived(far_copy(g - 1, -down, -2), west & row_ok(down))
                if g == 1:
                    arrived(far_copy(g - 1, -down, 2), east & row_ok(down))
                elif down:
                    arrived(outer_copy(1 - down, (down, 0)), east & row_ok(down))
            for role, first, mate, over, under, where_at, far_at in sides:
                @pl.when(role)
                def _(where_at=where_at, far_at=far_at):
                    sources = {}
                    for tile, at in where_at.items():
                        sources[tile] = wave[g - 1] if at == OWN else r_wave[g - 1, at]
                    for down, tile in enumerate(far_at):
                        sources[tile] = r_far[g - 1, down]
                    changes(sources, g - 1, mate_f, mate_high, mate_low)
                    old = mate_cm[:, :FRAMES]
                    live = mate_cm[:, FRAMES + 2 : FRAMES + 3]
                    rest = remaining(mate_goal[...], mate_v[...], mate_high, mate_low)
                    pack(mate_wave, g, updated(g, rest, old, live), old)

            start_mate(g)
            if g == 1:
                arrived(outer_sum, east)

                @pl.when(east)
                def _():
                    changes({UR: r_wave[0, UL], RIGHT: r_wave[0, LEFT], DR: r_wave[0, DL]}, 0, outer_f, outer_high, outer_low)
                    zero = jnp.zeros((4, FRAMES), F32)
                    aim, old, v = (
                        jnp.concatenate(
                            [zero, jnp.concatenate([r_outer[at, :4, :], r_outer[at, 4:, :]], axis=1), zero, zero], axis=0
                        )
                        for at in range(3)
                    )
                    value = jnp.maximum(remaining(aim, stacked(v), outer_high, outer_low), 0.0)
                    pack2 = value - old
                    outer_wave[:4, :] = pack2[4:8, :128]
                    outer_wave[4:, :] = pack2[4:8, 128:]
                    r_far[1, 1] = outer_wave[...]

                start(outer_copy(0, UP), east & there(UP))
                start(outer_copy(2, DOWN), east & there(DOWN))

    back_own = jnp.dot(unpick16, own, precision=lax.Precision.HIGHEST, preferred_element_type=F32)
    new_traces = jnp.where(alive_sub[:SLOTS, 0:1], back_own[:SLOTS, :], old_traces)
    for half in range(2):
        out_traces[pl.ds(half, SLOTS, stride=2), :] = new_traces[:, half * 128 : half * 128 + 128]

    for copy, ok in pending:
        @pl.when(ok)
        def _(copy=copy):
            copy.wait_send()


def on_device(rows, cols, movie, footprints, anchors, groups, counts, temporal, back_spatial, back_temporal, window):
    vmem = pl.BlockSpec(memory_space=pltpu.VMEM)
    dma = pltpu.SemaphoreType.DMA
    shapes, traces = pl.pallas_call(
        functools.partial(kernel, rows, cols),
        out_shape=(
            jax.ShapeDtypeStruct((SLOTS * PIX // 128, 128), F32),
            jax.ShapeDtypeStruct((SLOTS * FRAMES // 128, 128), F32),
        ),
        in_specs=[pl.BlockSpec(memory_space=pltpu.SMEM)] + [pl.BlockSpec(memory_space=pltpu.HBM)] * 8,
        out_specs=(vmem, vmem),
        scratch_shapes=[
            pltpu.SMEM((2, SLOTS), I32),
            pltpu.SMEM((1, SLOTS), I32),
            pltpu.SMEM((2,), I32),
            pltpu.VMEM((SLOTS * PIX // 128, 128), F32),
            pltpu.VMEM((SLOTS * FRAMES // 128, 128), F32),
            pltpu.VMEM((2, SIDE, SIDE), BF16),
            pltpu.VMEM((2, FRAMES), F32),
            pltpu.VMEM((PIX, FRAMES), BF16),
            pltpu.VMEM((2 * SIDE, 2 * SIDE), F32),
            pltpu.VMEM((16, PIX), F32),
            pltpu.VMEM((PAD, PIX), F32),
            pltpu.VMEM((2 * PAD, PIX), BF16),
            pltpu.VMEM((DENSE, WIDE), I16),
            pltpu.VMEM((DENSE, WIDE), I16),
            pltpu.VMEM((3, DENSE, WIDE), I16),
            pltpu.VMEM((PAD, FRAMES + 128), F32),
            pltpu.VMEM((8, PAD, FRAMES + 128), F32),
            pltpu.VMEM((NEAR, FRAMES + 128), F32),
            pltpu.VMEM((NEAR, PIX), F32),
            pltpu.VMEM((NEAR, PIX), F32),
            pltpu.VMEM((3 * NEAR + 16, PIX), BF16),
            pltpu.VMEM((NEAR, FRAMES + 128), F32),
            pltpu.VMEM((4, PAD, FRAMES + 128), F32),
            pltpu.VMEM((3, PAD, FRAMES + 128), F32),
            pltpu.VMEM((3, 8, 128), F32),
            pltpu.VMEM((3, 8, 8, 128), F32),
            pltpu.VMEM((4 * NEAR, FRAMES), F32),
            pltpu.VMEM((4 * NEAR, FRAMES), BF16),
            pltpu.VMEM((4 * NEAR, FRAMES), BF16),
            pltpu.VMEM((PAD, PIX), F32),
            pltpu.VMEM((DENSE, WIDE), F32),
            pltpu.VMEM((DENSE, 128), F32),
            pltpu.VMEM((PAD, PIX), F32),
            pltpu.VMEM((PAD, PIX), F32),
            pltpu.VMEM((4, PAD, FRAMES + 128), F32),
            pltpu.VMEM((PAD, FRAMES + 128), F32),
            pltpu.VMEM((PAD, FRAMES), F32),
            pltpu.VMEM((2 * PAD, 4 * NEAR), BF16),
            pltpu.VMEM((3, 8, 128), F32),
            pltpu.VMEM((2, 3, 8, 128), F32),
            pltpu.VMEM((4 * NEAR, FRAMES), F32),
            pltpu.VMEM((4 * NEAR, FRAMES), BF16),
            pltpu.VMEM((4 * NEAR, FRAMES), BF16),
            pltpu.VMEM((PAD, 2 * FRAMES), F32),
            pltpu.VMEM((PAD, 2 * FRAMES), F32),
            pltpu.VMEM((3, 8, 128), F32),
            pltpu.VMEM((3, 8, 128), F32),
            pltpu.VMEM((8, 128), F32),
            pltpu.VMEM((4 * NEAR, FRAMES), F32),
            pltpu.VMEM((4 * NEAR, FRAMES), BF16),
            pltpu.VMEM((4 * NEAR, FRAMES), BF16),
            pltpu.VMEM((2, DENSE, WIDE), I16),
            pltpu.VMEM((2, DENSE, WIDE), I16),
            pltpu.VMEM((DENSE, WIDE), I16),
            pltpu.VMEM((DENSE, WIDE), I16),
            dma((8,)),
            dma((8,)),
            dma((8,)),
            dma((3, PARTS)),
            dma((3, PARTS)),
            dma((3,)),
            dma((3,)),
            dma((3, 8)),
            dma((3, 8)),
            dma((2,)),
            dma((2,)),
            dma,
            dma,
            dma((4,)),
            dma((4,)),
            dma((3, 2)),
            dma((2, 3)),
            dma((2, 3)),
            dma((2,)),
            dma((2,)),
            dma((2,)),
        ],
        compiler_params=pltpu.CompilerParams(collective_id=0, has_side_effects=True, vmem_limit_bytes=32 << 20),
    )(
        counts,
        *(
            pltpu.with_memory_space_constraint(x, pltpu.HBM)
            for x in (
                anchors.reshape(SLOTS, 2).T,
                groups.reshape(1, SLOTS),
                window,
                footprints.reshape(SLOTS * PIX // 128, 128),
                temporal.reshape(SLOTS * FRAMES // 128, 128),
                back_spatial,
                back_temporal,
                movie.reshape(PIX, FRAMES),
            )
        )
    )
    return shapes.reshape(1, 1, SLOTS, PIX), traces.reshape(1, 1, SLOTS, FRAMES)


def solution(mesh):
    return jax.shard_map(
        functools.partial(on_device, mesh.shape["row"], mesh.shape["col"]),
        mesh=mesh,
        in_specs=(
            P("row", "col", None),
            P("row", "col", None, None),
            P("row", "col", None, None),
            P("row", "col", None),
            P("row", "col"),
            P("row", "col", None, None),
            P(None, "row", "col"),
            P(),
            P(),
        ),
        out_specs=(P("row", "col", None, None), P("row", "col", None, None)),
        check_vma=False,
    )
```

```python
import functools

import jax
import jax.numpy as jnp
from jax import lax
from jax.experimental import pallas as pl
from jax.experimental.pallas import tpu as pltpu
from jax.sharding import PartitionSpec as P

MESH = pl.DeviceIdType.MESH
F32 = jnp.float32
BF16 = jnp.bfloat16
I32 = jnp.int32
I16 = jnp.int16

SIDE = 64
PIX = SIDE * SIDE
FRAMES = 256
SLOTS = 12
GROUPS = 4
PAD = 16
NEAR = 4 * PAD
BIG = 1e30
DENSE = 4 * SLOTS
WIDE = PIX // 4
TOP = 8.0

DIRS = ((-1, -1), (-1, 0), (-1, 1), (0, -1), (0, 1), (1, -1), (1, 0), (1, 1))
UL, UP, UR, LEFT, RIGHT, DL, DOWN, DR = range(8)
OWN = 8
TILE_SETS = (
    (UL, UP, LEFT, OWN),
    (UP, UR, OWN, RIGHT),
    (LEFT, OWN, DL, DOWN),
    (OWN, RIGHT, DOWN, DR),
)
PARTS = 4


def nt(a, b):
    return lax.dot_general(a, b, (((1,), (1,)), ((), ())), preferred_element_type=F32)


def mm(a, b):
    return jnp.dot(a, b, preferred_element_type=F32)


def split(x):
    high = x.astype(BF16)
    return high, (x - high.astype(F32)).astype(BF16)


def turn(x, shift, forward):
    for bit in range(12):
        step = 1 << bit
        chosen = ((shift >> bit) & 1) == 1
        by = step if forward else PIX - step
        if by % 128 == 0:
            moved = jnp.concatenate([x[:, PIX - by :], x[:, : PIX - by]], axis=1)
        else:
            moved = pltpu.roll(x, by, 1)
        x = jnp.where(chosen, moved, x)
    return x


def half_turn(x, forward):
    return pltpu.roll(x, SIDE if forward else PIX - SIDE, 1)


def kernel(
    rows, cols,
    counts, anchors_in, groups_in, window_in, footprints_in, temporal_in, back_in, back_time_in, movie_in,
    out_shapes, out_traces,
    anchors, groups, window, footprints, temporal, back_raw, back_time, movie, back_even, back, pad_f, hl, code, code_right, r_code, cm, r_cm, near_cm, target, canvas, x3,
    shares, share_out, r_share, wave, r_wave, call_f, c_high, c_low, temp, dense, labels, far_f, near_f,
    r_mate, mate_cm, mate_goal, mate_v, mate_wave, r_far, mate_f, mate_high, mate_low,
    joint, r_joint, outer, r_outer, outer_wave, outer_f, outer_high, outer_low,
    piece_up, r_piece, merged, r_merged,
    load_sem, cm_send, cm_recv, r_send, r_recv, s_send, s_recv, t_send, t_recv, p_send, p_recv, m_send, m_recv,
    mate_send, mate_recv, mw_send, far_send, far_recv, joint_sem, outer_sem, ow_send,
):
    r = lax.axis_index("row")
    c = lax.axis_index("col")

    def there(d):
        down, right = DIRS[d]
        ok = None
        for at, step, count in ((r, down, rows), (c, right, cols)):
            if step:
                one = at + step >= 0 if step < 0 else at + step < count
                ok = one if ok is None else ok & one
        return ok

    def place(d):
        return (r + DIRS[d][0], c + DIRS[d][1])

    west = c == cols // 2 - 1
    east = c == cols // 2
    beside_west = c == cols // 2 - 2
    beside_east = c == cols // 2 + 1

    def row_ok(step):
        return (r + step >= 0) & (r + step < rows)

    barrier = pltpu.get_barrier_semaphore()

    loads = [
        pltpu.make_async_copy(source, target_ref, load_sem.at[at])
        for at, (source, target_ref) in enumerate(
            (
                (groups_in, groups),
                (anchors_in, anchors),
                (window_in, window),
                (temporal_in, temporal),
                (footprints_in, footprints),
                (back_time_in, back_time),
                (back_in, back_raw),
                (movie_in, movie),
            )
        )
    ]
    for load in loads:
        load.start()

    expected = 0
    for d in range(8):
        ok = there(d)
        hears = ok & jnp.logical_not(west) if d in (UR, DR) else ok
        tells = ok & jnp.logical_not(east) if d in (UL, DL) else ok

        @pl.when(tells)
        def _(d=d):
            pl.semaphore_signal(barrier, inc=1, device_id=place(d), device_id_type=MESH)

        expected = expected + hears.astype(I32)
    for down in (-1, 0, 1):
        for right, receiver, sender in ((2, west, beside_east), (-2, east, beside_west)):
            @pl.when(receiver & row_ok(down))
            def _(down=down, right=right):
                pl.semaphore_signal(barrier, inc=1, device_id=(r + down, c + right), device_id_type=MESH)

            expected = expected + (sender & row_ok(down)).astype(I32)

    for d in range(8):
        @pl.when(jnp.logical_not(there(d)))
        def _(d=d):
            r_cm[d] = jnp.zeros((PAD, FRAMES + 128), F32)
            for g in range(3):
                r_wave[g, d] = jnp.zeros((8, 128), F32)

    for t, d in ((0, DR), (1, DOWN), (2, RIGHT)):
        @pl.when(jnp.logical_not(there(d)))
        def _(t=t):
            r_share[t] = jnp.zeros((PAD, FRAMES + 128), F32)

    @pl.when(jnp.logical_not(row_ok(1)))
    def _():
        r_mate[2] = jnp.zeros((PAD, FRAMES + 128), F32)
        r_mate[3] = jnp.zeros((PAD, FRAMES + 128), F32)

    for down in (-1, 1):
        @pl.when(jnp.logical_not(row_ok(down)))
        def _(down=down):
            for g in range(2):
                r_far[g, 1 + down] = jnp.zeros((8, 128), F32)

    for ref in (call_f, c_high, c_low, far_f, near_f, mate_f, mate_high, mate_low, outer_f, outer_high, outer_low):
        ref[...] = jnp.zeros_like(ref)

    for load in loads[:4]:
        load.wait()
    sub = lax.broadcasted_iota(I32, (PAD, 128), 0)
    lane = lax.broadcasted_iota(I32, (PAD, 128), 1)
    g_sub = jnp.full((PAD, 128), -1, I32)
    g_lane = jnp.full((PAD, 128), -1, I32)
    a_lane = jnp.zeros((PAD, 128), I32)
    b_lane = jnp.zeros((PAD, 128), I32)
    count = counts[0, 0]
    for m in range(SLOTS):
        g_sub = jnp.where(sub == m, groups[0, m], g_sub)
        g_lane = jnp.where(lane == m, groups[0, m], g_lane)
        a_lane = jnp.where(lane == m, anchors[0, m], a_lane)
        b_lane = jnp.where(lane == m, anchors[1, m], b_lane)
    alive_lane = lane < count
    alive_sub = sub < count
    a_lane = jnp.where(alive_lane, a_lane, 0)
    b_lane = jnp.where(alive_lane, b_lane, 0)
    same = g_sub == g_lane
    before_lane = jnp.sum(jnp.where(same & (sub < lane), 1.0, 0.0), axis=0, keepdims=True)
    before_sub = jnp.sum(jnp.where(same & (lane < sub), 1.0, 0.0), axis=1, keepdims=True)
    pos_lane = g_lane.astype(F32) * 4.0 + before_lane
    pos_sub = g_sub.astype(F32) * 4.0 + before_sub
    pick = jnp.where((sub.astype(F32) == pos_lane) & (lane < SLOTS), 1.0, 0.0)
    unpick = jnp.where((lane.astype(F32) == pos_sub) & (sub < SLOTS), 1.0, 0.0)
    a_own = jnp.sum(pick * a_lane.astype(F32), axis=1, keepdims=True)
    b_own = jnp.sum(pick * b_lane.astype(F32), axis=1, keepdims=True)
    live_own = jnp.sum(pick * jnp.where(alive_lane, 1.0, 0.0), axis=1, keepdims=True)
    shift_own = (a_own * float(SIDE) + b_own).astype(I32)
    pick16 = pick[:, :PAD]
    unpick16 = unpick[:, :PAD]

    pad_f[SLOTS:PAD, :] = jnp.zeros((PAD - SLOTS, PIX), F32)
    for half in range(2):
        pad_f[:SLOTS, half * 128 : half * 128 + 128] = temporal[pl.ds(half, SLOTS, stride=2), :]
    old_traces = pad_f[:SLOTS, :FRAMES]
    cm[:, :FRAMES] = jnp.dot(pick16, pad_f[:, :FRAMES], precision=lax.Precision.HIGHEST, preferred_element_type=F32)
    cm[:, FRAMES:] = jnp.where(lane == 0, a_own, jnp.where(lane == 1, b_own, jnp.where(lane == 2, live_own, 0.0)))

    loads[4].wait()
    for q in range(PIX // 128):
        pad_f[:SLOTS, q * 128 : q * 128 + 128] = footprints[pl.ds(q, SLOTS, stride=32), :]
    whole = jnp.floor(pad_f[...] * 65535.0 + 0.5)
    upper = jnp.floor(whole * (1.0 / 256.0))
    hl[:PAD, :] = upper.astype(BF16)
    hl[PAD:, :] = (whole - upper * 256.0).astype(BF16)
    pick_hl = jnp.concatenate([pick16 * 256.0, pick16], axis=1).astype(BF16)
    pad_f[...] = mm(pick_hl, hl[...])
    for half in range(2):
        part = slice(half * 8, half * 8 + 8)
        pad_f[part, :] = turn(pad_f[part, :], shift_own[part], True)

    def packed(ref, row_of):
        for q in range(4):
            for g in range(GROUPS):
                at = slice(q * SLOTS + g * 3, q * SLOTS + g * 3 + 3)
                dense[at, :] = ref[row_of(g) : row_of(g) + 3, q * WIDE : (q + 1) * WIDE]
        return dense[...].astype(I32).astype(I16)

    def unpacked(codes, ref, row_of):
        codes = codes.astype(I32).astype(F32)
        for q in range(4):
            for g in range(GROUPS):
                at = slice(q * SLOTS + g * 3, q * SLOTS + g * 3 + 3)
                ref[row_of(g) : row_of(g) + 3, q * WIDE : (q + 1) * WIDE] = codes[at, :]

    pad_f[...] = pad_f[...] - 32768.0
    code[...] = packed(pad_f, lambda g: g * 4)
    temp[...] = half_turn(pad_f[...], False)
    code_right[...] = packed(temp, lambda g: g * 4)

    loads[5].wait()
    loads[6].wait()
    for i in range(2):
        back_even[i * SIDE : i * SIDE + SIDE, :SIDE] = back_raw[i].astype(F32)
    even = back_even[pl.ds(0, SIDE, stride=2), :SIDE]
    odd = back_even[pl.ds(1, SIDE, stride=2), :SIDE]
    back_even[:SIDE, :] = jnp.concatenate([even, odd], axis=1)
    for q in range(PIX // 128):
        back[:2, q * 128 : q * 128 + 128] = back_even[pl.ds(q, 2, stride=32), :]
    back[2:, :] = jnp.zeros((14, PIX), F32)
    x3[3 * NEAR :, :] = back[...].astype(BF16)

    pl.semaphore_wait(barrier, expected)

    def remote(src, dst, send, recv, d):
        target_id = place(d) if isinstance(d, int) else (r + d[0], c + d[1])
        return pltpu.make_async_remote_copy(
            src_ref=src, dst_ref=dst, send_sem=send, recv_sem=recv, device_id=target_id, device_id_type=MESH
        )

    pending = []

    def start(copy, ok):
        @pl.when(ok)
        def _():
            copy.start()

        pending.append((copy, ok))

    def arrived(copy, ok):
        @pl.when(ok)
        def _():
            copy.wait_recv()

    def cm_copy(src, slot, d):
        return remote(src, r_cm.at[slot], cm_send.at[slot], cm_recv.at[slot], d)

    def code_copy(source, slot, part, d):
        at = pl.ds(part * (WIDE // PARTS), WIDE // PARTS)
        if source is None:
            source = code_right.at[:, at] if slot == 2 else code.at[:, at]
        else:
            source = r_code.at[source, :, at]
        return remote(source, r_code.at[slot, :, at], r_send.at[slot, part], r_recv.at[slot, part], d)

    start(cm_copy(cm, LEFT, RIGHT), there(RIGHT))
    for part in range(PARTS):
        start(code_copy(None, 2, part, RIGHT), there(RIGHT))
    def own_down(role):
        start(cm_copy(cm, UP, DOWN), there(DOWN) & role)
        for part in range(PARTS):
            start(code_copy(None, 1, part, DOWN), there(DOWN) & role)

    own_down(jnp.logical_not(west))
    start(cm_copy(cm, RIGHT, LEFT), east)

    arrived(cm_copy(cm, LEFT, LEFT), there(LEFT))
    start(cm_copy(r_cm.at[LEFT], UL, DOWN), there(DOWN) & there(LEFT))
    for part in range(PARTS):
        arrived(code_copy(None, 2, part, LEFT), there(LEFT))
        start(code_copy(2, 0, part, DOWN), there(DOWN) & there(LEFT))
    own_down(west)
    arrived(cm_copy(cm, UP, UP), there(UP))
    arrived(cm_copy(cm, UL, UL), there(UL))

    def cm_of(tile, rows_at, lanes_at):
        if tile == OWN:
            return cm[rows_at, lanes_at]
        return r_cm[tile, rows_at, lanes_at]

    for g in range(GROUPS):
        for t in range(4):
            at = slice(g * PAD + t * 4, g * PAD + t * 4 + 4)
            near_cm[at, :] = cm_of(TILE_SETS[0][t], slice(g * 4, g * 4 + 4), slice(None))
    near_high, near_low = split(near_cm[:, :FRAMES])

    frame = lax.broadcasted_iota(I32, (NEAR, FRAMES), 1)
    weighted = jnp.where((frame >= window[0]) & (frame < window[1]), near_cm[:, :FRAMES], 0.0)
    w_high, w_low = split(weighted)
    w_both = jnp.concatenate([w_high, w_low], axis=0)
    q4 = nt(w_both, w_both)
    q = q4[:NEAR, :NEAR] + q4[:NEAR, NEAR:] + q4[NEAR:, :NEAR] + q4[NEAR:, NEAR:]
    a_near = near_cm[:, FRAMES : FRAMES + 1].astype(I32)
    b_near = near_cm[:, FRAMES + 1 : FRAMES + 2].astype(I32)
    live_near = near_cm[:, FRAMES + 2 : FRAMES + 3]
    eye = lax.broadcasted_iota(I32, (NEAR, NEAR), 0) == lax.broadcasted_iota(I32, (NEAR, NEAR), 1)
    mass = jnp.sum(jnp.where(eye, q, 0.0), axis=1, keepdims=True)
    inverse = 1.0 / jnp.where(live_near > 0, mass, 1.0)
    q_high, q_low = split(jnp.where(eye, 0.0, q) * inverse)
    q3 = jnp.concatenate([q_high, q_high, q_low], axis=1)
    load0 = jnp.sum(weighted * back_time[0:1, :], axis=1, keepdims=True)
    load1 = jnp.sum(weighted * back_time[1:2, :], axis=1, keepdims=True)

    tile_at = (lax.broadcasted_iota(I32, (NEAR, 1), 0) >> 2) & 3
    above = tile_at < 2
    aside = (tile_at & 1) == 0
    y_low = jnp.where(above, 0, a_near)
    y_high = jnp.where(live_near > 0, jnp.where(above, a_near, SIDE), 0)
    x_low = jnp.where(aside, 0, b_near)
    x_high = jnp.where(aside, b_near, SIDE)

    def covered(rows_at, begin, width):
        spot = lax.broadcasted_iota(I32, (1, width), 1) + begin
        y = spot >> 6
        x = spot & 63
        return (
            (y >= y_low[rows_at]) & (y < y_high[rows_at]) & (x >= x_low[rows_at]) & (x < x_high[rows_at])
        )

    loads[7].wait()
    width = 1024
    for begin in range(0, PIX, width):
        at = slice(begin, begin + width)
        pull = nt(w_high, movie[at, :])
        pull = pull - load0 * back[0:1, at] - load1 * back[1:2, at]
        target[:, at] = jnp.where(covered(slice(None), begin, width), pull * inverse, -BIG)

    for part in range(PARTS):
        arrived(code_copy(None, 1, part, UP), there(UP))
    for part in range(PARTS):
        arrived(code_copy(None, 0, part, UL), there(UL))
    for t in range(3):
        unpacked(r_code[t], canvas, lambda g: g * PAD + t * 4)
    for g in range(GROUPS):
        canvas[g * PAD + 12 : g * PAD + 16, :] = pad_f[g * 4 : g * 4 + 4, :]
    for g in range(GROUPS):
        rows_at = slice(g * PAD, g * PAD + PAD)
        value = jnp.where(covered(rows_at, 0, PIX), (canvas[rows_at, :] + 32768.0) * (1.0 / 65535.0), 0.0)
        high, low = split(value)
        x3[g * PAD : g * PAD + PAD, :] = high
        x3[NEAR + g * PAD : NEAR + g * PAD + PAD, :] = low
        x3[2 * NEAR + g * PAD : 2 * NEAR + g * PAD + PAD, :] = high

    gram = nt(x3[: 2 * NEAR, :], x3[NEAR:, :])
    gram = gram[:NEAR] + gram[NEAR:]
    overlap = gram[:, :NEAR] + gram[:, NEAR : 2 * NEAR]
    loading = gram[:, 2 * NEAR : 2 * NEAR + 2]
    drive = mm(x3[:NEAR, :], movie[...])
    drive = drive - loading[:, 0:1] * back_time[0:1, :] - loading[:, 1:2] * back_time[1:2, :]
    self_overlap = jnp.sum(jnp.where(eye, overlap, 0.0), axis=1, keepdims=True)
    overlap = jnp.where(eye, 0.0, overlap)
    o_high, o_low = split(overlap)
    product = mm(jnp.concatenate([o_high, o_low], axis=0), near_high)
    shares[:, :FRAMES] = drive - (product[:NEAR] + product[NEAR:] + mm(o_high, near_low))
    shares[:, FRAMES : FRAMES + NEAR] = overlap
    shares[:, FRAMES + NEAR :] = jnp.broadcast_to(self_overlap, (NEAR, 128 - NEAR))
    for t in range(4):
        for g in range(GROUPS):
            share_out[t, g * 4 : g * 4 + 4, :] = shares[g * PAD + t * 4 : g * PAD + t * 4 + 4, :]

    def share_copy(t, d):
        return remote(share_out.at[t], r_share.at[t], s_send.at[t], s_recv.at[t], d)

    for t, d in ((2, LEFT), (0, UL), (1, UP)):
        start(share_copy(t, d), there(d))

    def mate_share(t, k, d):
        return remote(share_out.at[t], r_mate.at[k], mate_send.at[t], mate_recv.at[k], d)

    start(mate_share(3, 0, (0, 1)), west)
    start(mate_share(0, 3, (-1, 0)), east & row_ok(-1))

    for g in range(GROUPS):
        rows_at = slice(g * PAD, g * PAD + PAD)
        value = jnp.maximum(target[rows_at, :] - mm(q3[rows_at, :], x3[: 3 * NEAR, :]), 0.0)
        canvas[rows_at, :] = jnp.floor(jnp.sqrt(value * (1.0 / TOP)) * 65535.0 + 0.5) - 32768.0
        if g < GROUPS - 1:
            high, low = split(value)
            x3[g * PAD : g * PAD + PAD, :] = high
            x3[NEAR + g * PAD : NEAR + g * PAD + PAD, :] = low
            x3[2 * NEAR + g * PAD : 2 * NEAR + g * PAD + PAD, :] = high

    for t in range(2):
        piece_up[t] = packed(canvas, lambda g: g * PAD + t * 4)

    def piece_copy(t, d):
        return remote(piece_up.at[t], r_piece.at[t], p_send.at[t], p_recv.at[t], d)

    for t in range(2):
        start(piece_copy(t, UP), there(UP) & (c < cols // 2))

    arrived(share_copy(1, DOWN), there(DOWN))
    start(remote(r_share.at[1], r_mate.at[2], mate_send.at[1], mate_recv.at[2], RIGHT), west & row_ok(1))
    for t, d in ((2, RIGHT), (0, DR)):
        arrived(share_copy(t, d), there(d))

    def joined(parts, live):
        total = parts[0] + parts[1] + parts[2] + parts[3]
        scale = 1.0 / jnp.where(live > 0, total[:, FRAMES + NEAR : FRAMES + NEAR + 1], 1.0)
        v = jnp.concatenate([part[:, FRAMES : FRAMES + NEAR] for part in parts], axis=1) * scale
        return total[:, :FRAMES] * scale, v

    def stacked(v):
        return jnp.concatenate(split(v), axis=0)

    goal, v_own = joined([share_out[3], r_share[2], r_share[1], r_share[0]], live_own)
    v_both = stacked(v_own)
    own = cm[:, :FRAMES]
    row_group = lax.broadcasted_iota(I32, (PAD, FRAMES), 0) >> 2

    def changes(sources, g, full, high_ref, low_ref):
        for k in range(4):
            for t in range(4):
                if TILE_SETS[k][t] not in sources:
                    continue
                new = sources[TILE_SETS[k][t]]
                at = slice(k * NEAR + g * PAD + t * 4, k * NEAR + g * PAD + t * 4 + 4)
                full[at, :128] = new[:4, :]
                full[at, 128:] = new[4:, :]
            at = slice(k * NEAR + g * PAD, k * NEAR + g * PAD + PAD)
            high, low = split(full[at, :])
            high_ref[at, :] = high
            low_ref[at, :] = low

    def remaining(aim, v_two, high_ref, low_ref):
        product = mm(v_two, high_ref[...])
        return aim - (product[:PAD] + product[PAD:] + mm(v_two[:PAD], low_ref[...]))

    def updated(g, left_over, old, live):
        chosen = (row_group == g) & (live > 0)
        return jnp.where(chosen, jnp.maximum(left_over, 0.0), old)

    def pack(ref, g, new, old):
        change = new - old
        ref[g, :4, :] = change[g * 4 : g * 4 + 4, :128]
        ref[g, 4:, :] = change[g * 4 : g * 4 + 4, 128:]

    def wave_copy(g, d, slot):
        return remote(wave.at[g], r_wave.at[g, slot], t_send.at[g, slot], t_recv.at[g, slot], d)

    def sends(g, d):
        ok = there(d)
        if DIRS[d][1] > 0:
            ok = ok & jnp.logical_not(west)
        if DIRS[d][1] < 0 and g > 0:
            ok = ok & jnp.logical_not(east)
        return ok

    def gets(g, d):
        ok = there(d)
        if DIRS[d][1] > 0 and g > 0:
            ok = ok & jnp.logical_not(west)
        if DIRS[d][1] < 0:
            ok = ok & jnp.logical_not(east)
        return ok

    def mate_copy(g, at, d, slot):
        return remote(mate_wave.at[g], r_wave.at[g, slot], mw_send.at[g, at], t_recv.at[g, slot], d)

    def far_copy(g, down, right):
        return remote(wave.at[g], r_far.at[g, 1 - down], far_send.at[g, 1 - down], far_recv.at[g, 1 - down], (down, right))

    def outer_copy(at, d):
        return remote(outer_wave, r_far.at[1, 2 - at], ow_send.at[at // 2], far_recv.at[1, 2 - at], d)

    joint_copy = remote(joint, r_joint, joint_sem.at[0], joint_sem.at[1], LEFT)
    outer_sum = remote(outer, r_outer, outer_sem.at[0], outer_sem.at[1], (0, 2))

    sides = (
        (west, 1, RIGHT, UR, DR, {UL: UP, LEFT: OWN, DL: DOWN, UP: UR, OWN: RIGHT, DOWN: DR}, (UR, RIGHT, DR)),
        (east, 0, LEFT, UL, DL, {UR: UP, RIGHT: OWN, DR: DOWN, UP: UL, OWN: LEFT, DOWN: DL}, (UL, LEFT, DL)),
    )

    def start_mate(g):
        for role, first, mate, over, under, _, _ in sides:
            if g < first:
                continue

            @pl.when(role)
            def _(mate=mate):
                r_wave[g, mate] = mate_wave[g]

            start(mate_copy(g, 0, UP, under), role & there(UP))
            start(mate_copy(g, 1, DOWN, over), role & there(DOWN))

    for g in range(GROUPS):
        left_over = goal
        if g == GROUPS - 1:
            arrived(remote(merged, r_merged, m_send, m_recv, RIGHT), there(RIGHT))
            spot = lax.broadcasted_iota(I32, (PAD, PIX), 1)
            y = spot >> 6
            x = spot & 63
            a_int = a_own.astype(I32)
            b_int = b_own.astype(I32)
            unpacked(r_merged[...], far_f, lambda k: k * 4)
            unpacked(r_piece[1], near_f, lambda k: k * 4)
            for k in range(GROUPS):
                temp[k * 4 : k * 4 + 4, :] = canvas[k * PAD + 12 : k * PAD + 16, :]
            near = jnp.where(y < a_int, near_f[...], temp[...])
            pad_f[...] = jnp.where(x < b_int, half_turn(far_f[...], True), near) + 32768.0
            for half in range(2):
                part = slice(half * 8, half * 8 + 8)
                pad_f[part, :] = turn(pad_f[part, :], shift_own[part], False)
            whole = pad_f[...]
            upper = jnp.floor(whole * (1.0 / 256.0))
            hl[:PAD, :] = upper.astype(BF16)
            hl[PAD:, :] = (whole - upper * 256.0).astype(BF16)
            unpick_hl = jnp.concatenate([unpick16 * 256.0, unpick16], axis=1).astype(BF16)
            root = mm(unpick_hl, hl[...])[:SLOTS, :] * (1.0 / 65535.0)
            pad_f[:SLOTS, :] = root * root * TOP
            for q in range(PIX // 128):
                out_shapes[pl.ds(q, SLOTS, stride=32), :] = pad_f[:SLOTS, q * 128 : q * 128 + 128]

        if g > 0:
            for d in (UP, DOWN, LEFT, UL, DL):
                arrived(wave_copy(g - 1, d, d), gets(g - 1, d))
            if g == 1:
                @pl.when(beside_west)
                def _():
                    sources = {d: r_wave[0, d] for d in (UP, DOWN, LEFT, UL, DL)}
                    sources[OWN] = wave[0]
                    changes(sources, 0, mate_f, mate_high, mate_low)
                    aim = jnp.where(live_own > 0, remaining(goal, v_both, mate_high, mate_low), own)
                    for at, value in enumerate((aim, own, v_own)):
                        outer[at, :4, :] = value[4:8, :128]
                        outer[at, 4:, :] = value[4:8, 128:]

                start(outer_sum, beside_west)
            for d in (RIGHT, UR, DR):
                arrived(wave_copy(g - 1, d, d), gets(g - 1, d))
            for role, first, mate, over, under, _, _ in sides:
                if g - 1 >= first:
                    arrived(mate_copy(g - 1, 0, UP, over), role & there(UP))
                    arrived(mate_copy(g - 1, 1, DOWN, under), role & there(DOWN))
            changes({**{d: r_wave[g - 1, d] for d in range(8)}, OWN: wave[g - 1]}, g - 1, call_f, c_high, c_low)
            left_over = remaining(goal, v_both, c_high, c_low)
        new = updated(g, left_over, own, live_own)
        if g < GROUPS - 1:
            pack(wave, g, new, own)
            for d in (UL, DL, LEFT, UR, DR, RIGHT, UP, DOWN):
                start(wave_copy(g, d, 7 - d), sends(g, d))
            if g < 2:
                for down in (-1, 0, 1):
                    if g == 0:
                        start(far_copy(g, down, 2), beside_west & row_ok(down))
                    start(far_copy(g, down, -2), beside_east & row_ok(down))
        own = new
        if g == 0:
            @pl.when(east)
            def _():
                joint[:, :FRAMES] = goal
                joint[:, FRAMES:] = v_own

            start(joint_copy, east)

            for t in range(2):
                start(piece_copy(t, UP), there(UP) & (c >= cols // 2))

            arrived(mate_share(3, 0, (0, -1)), east)
            arrived(mate_share(1, 2, (0, -1)), east & row_ok(1))
            arrived(mate_share(0, 3, (1, 0)), east & row_ok(1))

            @pl.when(east)
            def _():
                mate_cm[...] = r_cm[LEFT]
                r_mate[1] = share_out[2]
                live = mate_cm[:, FRAMES + 2 : FRAMES + 3]
                mate_goal[...], v_mate = joined([r_mate[k] for k in range(4)], live)
                mate_v[...] = stacked(v_mate)
                old = mate_cm[:, :FRAMES]
                pack(mate_wave, 0, updated(0, mate_goal[...], old, live), old)

            start_mate(0)

            for q in range(4):
                for k in range(GROUPS):
                    at = slice(q * SLOTS + k * 3, q * SLOTS + k * 3 + 3)
                    labels[at, :] = r_cm[LEFT, k * 4 : k * 4 + 3, FRAMES:]
            a_left = labels[:, 0:1].astype(I32)
            row = lax.broadcasted_iota(I32, (DENSE, WIDE), 0)
            quarter = (row >= SLOTS).astype(I32) + (row >= 2 * SLOTS).astype(I32) + (row >= 3 * SLOTS).astype(I32)
            below = quarter * 16 + (lax.broadcasted_iota(I32, (DENSE, WIDE), 1) >> 6) < a_left
            left_codes = packed(canvas, lambda k: k * PAD + 8).astype(I32)
            for t in range(2):
                arrived(piece_copy(t, DOWN), there(DOWN))
            merged[...] = jnp.where(below, r_piece[0].astype(I32), left_codes).astype(I16)
            start(remote(merged, r_merged, m_send, m_recv, LEFT), there(LEFT))
        elif g < GROUPS - 1:
            if g == 1:
                arrived(cm_copy(cm, RIGHT, RIGHT), west)
                arrived(joint_copy, west)

                @pl.when(west)
                def _():
                    mate_cm[...] = r_cm[RIGHT]
                    mate_goal[...] = r_joint[:, :FRAMES]
                    mate_v[...] = stacked(r_joint[:, FRAMES:])

            for down in (-1, 0, 1):
                arrived(far_copy(g - 1, -down, -2), west & row_ok(down))
                if g == 1:
                    arrived(far_copy(g - 1, -down, 2), east & row_ok(down))
                elif down:
                    arrived(outer_copy(1 - down, (down, 0)), east & row_ok(down))
            for role, first, mate, over, under, where_at, far_at in sides:
                @pl.when(role)
                def _(where_at=where_at, far_at=far_at):
                    sources = {}
                    for tile, at in where_at.items():
                        sources[tile] = wave[g - 1] if at == OWN else r_wave[g - 1, at]
                    for down, tile in enumerate(far_at):
                        sources[tile] = r_far[g - 1, down]
                    changes(sources, g - 1, mate_f, mate_high, mate_low)
                    old = mate_cm[:, :FRAMES]
                    live = mate_cm[:, FRAMES + 2 : FRAMES + 3]
                    rest = remaining(mate_goal[...], mate_v[...], mate_high, mate_low)
                    pack(mate_wave, g, updated(g, rest, old, live), old)

            start_mate(g)
            if g == 1:
                arrived(outer_sum, east)

                @pl.when(east)
                def _():
                    changes({UR: r_wave[0, UL], RIGHT: r_wave[0, LEFT], DR: r_wave[0, DL]}, 0, outer_f, outer_high, outer_low)
                    zero = jnp.zeros((4, FRAMES), F32)
                    aim, old, v = (
                        jnp.concatenate(
                            [zero, jnp.concatenate([r_outer[at, :4, :], r_outer[at, 4:, :]], axis=1), zero, zero], axis=0
                        )
                        for at in range(3)
                    )
                    value = jnp.maximum(remaining(aim, stacked(v), outer_high, outer_low), 0.0)
                    pack2 = value - old
                    outer_wave[:4, :] = pack2[4:8, :128]
                    outer_wave[4:, :] = pack2[4:8, 128:]
                    r_far[1, 1] = outer_wave[...]

                start(outer_copy(0, UP), east & there(UP))
                start(outer_copy(2, DOWN), east & there(DOWN))

    back_own = jnp.dot(unpick16, own, precision=lax.Precision.HIGHEST, preferred_element_type=F32)
    new_traces = jnp.where(alive_sub[:SLOTS, 0:1], back_own[:SLOTS, :], old_traces)
    for half in range(2):
        out_traces[pl.ds(half, SLOTS, stride=2), :] = new_traces[:, half * 128 : half * 128 + 128]

    for copy, ok in pending:
        @pl.when(ok)
        def _(copy=copy):
            copy.wait_send()


def on_device(rows, cols, movie, footprints, anchors, groups, counts, temporal, back_spatial, back_temporal, window):
    vmem = pl.BlockSpec(memory_space=pltpu.VMEM)
    dma = pltpu.SemaphoreType.DMA
    shapes, traces = pl.pallas_call(
        functools.partial(kernel, rows, cols),
        out_shape=(
            jax.ShapeDtypeStruct((SLOTS * PIX // 128, 128), F32),
            jax.ShapeDtypeStruct((SLOTS * FRAMES // 128, 128), F32),
        ),
        in_specs=[pl.BlockSpec(memory_space=pltpu.SMEM)] + [pl.BlockSpec(memory_space=pltpu.HBM)] * 8,
        out_specs=(vmem, vmem),
        scratch_shapes=[
            pltpu.SMEM((2, SLOTS), I32),
            pltpu.SMEM((1, SLOTS), I32),
            pltpu.SMEM((2,), I32),
            pltpu.VMEM((SLOTS * PIX // 128, 128), F32),
            pltpu.VMEM((SLOTS * FRAMES // 128, 128), F32),
            pltpu.VMEM((2, SIDE, SIDE), BF16),
            pltpu.VMEM((2, FRAMES), F32),
            pltpu.VMEM((PIX, FRAMES), BF16),
            pltpu.VMEM((2 * SIDE, 2 * SIDE), F32),
            pltpu.VMEM((16, PIX), F32),
            pltpu.VMEM((PAD, PIX), F32),
            pltpu.VMEM((2 * PAD, PIX), BF16),
            pltpu.VMEM((DENSE, WIDE), I16),
            pltpu.VMEM((DENSE, WIDE), I16),
            pltpu.VMEM((3, DENSE, WIDE), I16),
            pltpu.VMEM((PAD, FRAMES + 128), F32),
            pltpu.VMEM((8, PAD, FRAMES + 128), F32),
            pltpu.VMEM((NEAR, FRAMES + 128), F32),
            pltpu.VMEM((NEAR, PIX), F32),
            pltpu.VMEM((NEAR, PIX), F32),
            pltpu.VMEM((3 * NEAR + 16, PIX), BF16),
            pltpu.VMEM((NEAR, FRAMES + 128), F32),
            pltpu.VMEM((4, PAD, FRAMES + 128), F32),
            pltpu.VMEM((3, PAD, FRAMES + 128), F32),
            pltpu.VMEM((3, 8, 128), F32),
            pltpu.VMEM((3, 8, 8, 128), F32),
            pltpu.VMEM((4 * NEAR, FRAMES), F32),
            pltpu.VMEM((4 * NEAR, FRAMES), BF16),
            pltpu.VMEM((4 * NEAR, FRAMES), BF16),
            pltpu.VMEM((PAD, PIX), F32),
            pltpu.VMEM((DENSE, WIDE), F32),
            pltpu.VMEM((DENSE, 128), F32),
            pltpu.VMEM((PAD, PIX), F32),
            pltpu.VMEM((PAD, PIX), F32),
            pltpu.VMEM((4, PAD, FRAMES + 128), F32),
            pltpu.VMEM((PAD, FRAMES + 128), F32),
            pltpu.VMEM((PAD, FRAMES), F32),
            pltpu.VMEM((2 * PAD, 4 * NEAR), BF16),
            pltpu.VMEM((3, 8, 128), F32),
            pltpu.VMEM((2, 3, 8, 128), F32),
            pltpu.VMEM((4 * NEAR, FRAMES), F32),
            pltpu.VMEM((4 * NEAR, FRAMES), BF16),
            pltpu.VMEM((4 * NEAR, FRAMES), BF16),
            pltpu.VMEM((PAD, 2 * FRAMES), F32),
            pltpu.VMEM((PAD, 2 * FRAMES), F32),
            pltpu.VMEM((3, 8, 128), F32),
            pltpu.VMEM((3, 8, 128), F32),
            pltpu.VMEM((8, 128), F32),
            pltpu.VMEM((4 * NEAR, FRAMES), F32),
            pltpu.VMEM((4 * NEAR, FRAMES), BF16),
            pltpu.VMEM((4 * NEAR, FRAMES), BF16),
            pltpu.VMEM((2, DENSE, WIDE), I16),
            pltpu.VMEM((2, DENSE, WIDE), I16),
            pltpu.VMEM((DENSE, WIDE), I16),
            pltpu.VMEM((DENSE, WIDE), I16),
            dma((8,)),
            dma((8,)),
            dma((8,)),
            dma((3, PARTS)),
            dma((3, PARTS)),
            dma((3,)),
            dma((3,)),
            dma((3, 8)),
            dma((3, 8)),
            dma((2,)),
            dma((2,)),
            dma,
            dma,
            dma((4,)),
            dma((4,)),
            dma((3, 2)),
            dma((2, 3)),
            dma((2, 3)),
            dma((2,)),
            dma((2,)),
            dma((2,)),
        ],
        compiler_params=pltpu.CompilerParams(collective_id=0, has_side_effects=True, vmem_limit_bytes=32 << 20),
    )(
        counts,
        *(
            pltpu.with_memory_space_constraint(x, pltpu.HBM)
            for x in (
                anchors.reshape(SLOTS, 2).T,
                groups.reshape(1, SLOTS),
                window,
                footprints.reshape(SLOTS * PIX // 128, 128),
                temporal.reshape(SLOTS * FRAMES // 128, 128),
                back_spatial,
                back_temporal,
                movie.reshape(PIX, FRAMES),
            )
        )
    )
    return shapes.reshape(1, 1, SLOTS, PIX), traces.reshape(1, 1, SLOTS, FRAMES)


def solution(mesh):
    return jax.shard_map(
        functools.partial(on_device, mesh.shape["row"], mesh.shape["col"]),
        mesh=mesh,
        in_specs=(
            P("row", "col", None),
            P("row", "col", None, None),
            P("row", "col", None, None),
            P("row", "col", None),
            P("row", "col"),
            P("row", "col", None, None),
            P(None, "row", "col"),
            P(),
            P(),
        ),
        out_specs=(P("row", "col", None, None), P("row", "col", None, None)),
        check_vma=False,
    )
```

```python
import functools

import jax
import jax.numpy as jnp
from jax import lax
from jax.experimental import pallas as pl
from jax.experimental.pallas import tpu as pltpu
from jax.sharding import PartitionSpec as P

MESH = pl.DeviceIdType.MESH
F32 = jnp.float32
BF16 = jnp.bfloat16
I32 = jnp.int32
I16 = jnp.int16

SIDE = 64
PIX = SIDE * SIDE
FRAMES = 256
SLOTS = 12
GROUPS = 4
PAD = 16
NEAR = 4 * PAD
BIG = 1e30
DENSE = 4 * SLOTS
WIDE = PIX // 4
TOP = 8.0

DIRS = ((-1, -1), (-1, 0), (-1, 1), (0, -1), (0, 1), (1, -1), (1, 0), (1, 1))
UL, UP, UR, LEFT, RIGHT, DL, DOWN, DR = range(8)
OWN = 8
TILE_SETS = (
    (UL, UP, LEFT, OWN),
    (UP, UR, OWN, RIGHT),
    (LEFT, OWN, DL, DOWN),
    (OWN, RIGHT, DOWN, DR),
)
PARTS = 4


def nt(a, b):
    return lax.dot_general(a, b, (((1,), (1,)), ((), ())), preferred_element_type=F32)


def mm(a, b):
    return jnp.dot(a, b, preferred_element_type=F32)


def split(x):
    high = x.astype(BF16)
    return high, (x - high.astype(F32)).astype(BF16)


def turn(x, shift, forward):
    for bit in range(12):
        step = 1 << bit
        chosen = ((shift >> bit) & 1) == 1
        by = step if forward else PIX - step
        if by % 128 == 0:
            moved = jnp.concatenate([x[:, PIX - by :], x[:, : PIX - by]], axis=1)
        else:
            moved = pltpu.roll(x, by, 1)
        x = jnp.where(chosen, moved, x)
    return x


def half_turn(x, forward):
    return pltpu.roll(x, SIDE if forward else PIX - SIDE, 1)


def kernel(
    rows, cols,
    counts, anchors_in, groups_in, window_in, footprints_in, temporal_in, back_in, back_time_in, movie_in,
    out_shapes, out_traces,
    anchors, groups, window, footprints, temporal, back_raw, back_time, movie, back_even, back, pad_f, hl, code, code_right, r_code, cm, r_cm, near_cm, target, canvas, x3,
    shares, share_out, r_share, wave, r_wave, call_f, temp, dense, labels, far_f, near_f,
    r_mate, mate_cm, mate_goal, mate_v, mate_wave, r_far, mate_f,
    joint, r_joint, outer, r_outer, outer_wave, outer_f,
    piece_up, r_piece, merged, r_merged,
    load_sem, cm_send, cm_recv, r_send, r_recv, s_send, s_recv, t_send, t_recv, p_send, p_recv, m_send, m_recv,
    mate_send, mate_recv, mw_send, far_send, far_recv, joint_sem, outer_sem, ow_send,
):
    r = lax.axis_index("row")
    c = lax.axis_index("col")

    def there(d):
        down, right = DIRS[d]
        ok = None
        for at, step, count in ((r, down, rows), (c, right, cols)):
            if step:
                one = at + step >= 0 if step < 0 else at + step < count
                ok = one if ok is None else ok & one
        return ok

    def place(d):
        return (r + DIRS[d][0], c + DIRS[d][1])

    west = c == cols // 2 - 1
    east = c == cols // 2
    beside_west = c == cols // 2 - 2
    beside_east = c == cols // 2 + 1

    def row_ok(step):
        return (r + step >= 0) & (r + step < rows)

    barrier = pltpu.get_barrier_semaphore()

    loads = [
        pltpu.make_async_copy(source, target_ref, load_sem.at[at])
        for at, (source, target_ref) in enumerate(
            (
                (groups_in, groups),
                (anchors_in, anchors),
                (window_in, window),
                (temporal_in, temporal),
                (footprints_in, footprints),
                (back_time_in, back_time),
                (back_in, back_raw),
                (movie_in, movie),
            )
        )
    ]
    for load in loads:
        load.start()

    expected = 0
    for d in range(8):
        ok = there(d)
        hears = ok & jnp.logical_not(west) if d in (UR, DR) else ok
        tells = ok & jnp.logical_not(east) if d in (UL, DL) else ok

        @pl.when(tells)
        def _(d=d):
            pl.semaphore_signal(barrier, inc=1, device_id=place(d), device_id_type=MESH)

        expected = expected + hears.astype(I32)
    for down in (-1, 0, 1):
        for right, receiver, sender in ((2, west, beside_east), (-2, east, beside_west)):
            @pl.when(receiver & row_ok(down))
            def _(down=down, right=right):
                pl.semaphore_signal(barrier, inc=1, device_id=(r + down, c + right), device_id_type=MESH)

            expected = expected + (sender & row_ok(down)).astype(I32)

    for d in range(8):
        @pl.when(jnp.logical_not(there(d)))
        def _(d=d):
            r_cm[d] = jnp.zeros((PAD, FRAMES + 128), F32)
            for g in range(3):
                r_wave[g, d] = jnp.zeros((8, 128), F32)

    for t, d in ((0, DR), (1, DOWN), (2, RIGHT)):
        @pl.when(jnp.logical_not(there(d)))
        def _(t=t):
            r_share[t] = jnp.zeros((PAD, FRAMES + 128), F32)

    @pl.when(jnp.logical_not(row_ok(1)))
    def _():
        r_mate[2] = jnp.zeros((PAD, FRAMES + 128), F32)
        r_mate[3] = jnp.zeros((PAD, FRAMES + 128), F32)

    for down in (-1, 1):
        @pl.when(jnp.logical_not(row_ok(down)))
        def _(down=down):
            for g in range(2):
                r_far[g, 1 + down] = jnp.zeros((8, 128), F32)

    for ref in (far_f, near_f, mate_f, outer_f):
        ref[...] = jnp.zeros_like(ref)

    for load in loads[:4]:
        load.wait()
    sub = lax.broadcasted_iota(I32, (PAD, 128), 0)
    lane = lax.broadcasted_iota(I32, (PAD, 128), 1)
    g_sub = jnp.full((PAD, 128), -1, I32)
    g_lane = jnp.full((PAD, 128), -1, I32)
    a_lane = jnp.zeros((PAD, 128), I32)
    b_lane = jnp.zeros((PAD, 128), I32)
    count = counts[0, 0]
    for m in range(SLOTS):
        g_sub = jnp.where(sub == m, groups[0, m], g_sub)
        g_lane = jnp.where(lane == m, groups[0, m], g_lane)
        a_lane = jnp.where(lane == m, anchors[0, m], a_lane)
        b_lane = jnp.where(lane == m, anchors[1, m], b_lane)
    alive_lane = lane < count
    alive_sub = sub < count
    a_lane = jnp.where(alive_lane, a_lane, 0)
    b_lane = jnp.where(alive_lane, b_lane, 0)
    same = g_sub == g_lane
    before_lane = jnp.sum(jnp.where(same & (sub < lane), 1.0, 0.0), axis=0, keepdims=True)
    before_sub = jnp.sum(jnp.where(same & (lane < sub), 1.0, 0.0), axis=1, keepdims=True)
    pos_lane = g_lane.astype(F32) * 4.0 + before_lane
    pos_sub = g_sub.astype(F32) * 4.0 + before_sub
    pick = jnp.where((sub.astype(F32) == pos_lane) & (lane < SLOTS), 1.0, 0.0)
    unpick = jnp.where((lane.astype(F32) == pos_sub) & (sub < SLOTS), 1.0, 0.0)
    a_own = jnp.sum(pick * a_lane.astype(F32), axis=1, keepdims=True)
    b_own = jnp.sum(pick * b_lane.astype(F32), axis=1, keepdims=True)
    live_own = jnp.sum(pick * jnp.where(alive_lane, 1.0, 0.0), axis=1, keepdims=True)
    shift_own = (a_own * float(SIDE) + b_own).astype(I32)
    pick16 = pick[:, :PAD]
    unpick16 = unpick[:, :PAD]

    pad_f[SLOTS:PAD, :] = jnp.zeros((PAD - SLOTS, PIX), F32)
    for half in range(2):
        pad_f[:SLOTS, half * 128 : half * 128 + 128] = temporal[pl.ds(half, SLOTS, stride=2), :]
    old_traces = pad_f[:SLOTS, :FRAMES]
    cm[:, :FRAMES] = jnp.dot(pick16, pad_f[:, :FRAMES], precision=lax.Precision.HIGHEST, preferred_element_type=F32)
    cm[:, FRAMES:] = jnp.where(lane == 0, a_own, jnp.where(lane == 1, b_own, jnp.where(lane == 2, live_own, 0.0)))

    loads[4].wait()
    for q in range(PIX // 128):
        pad_f[:SLOTS, q * 128 : q * 128 + 128] = footprints[pl.ds(q, SLOTS, stride=32), :]
    whole = jnp.floor(pad_f[...] * 65535.0 + 0.5)
    upper = jnp.floor(whole * (1.0 / 256.0))
    hl[:PAD, :] = upper.astype(BF16)
    hl[PAD:, :] = (whole - upper * 256.0).astype(BF16)
    pick_hl = jnp.concatenate([pick16 * 256.0, pick16], axis=1).astype(BF16)
    pad_f[...] = mm(pick_hl, hl[...])
    for half in range(2):
        part = slice(half * 8, half * 8 + 8)
        pad_f[part, :] = turn(pad_f[part, :], shift_own[part], True)

    def packed(ref, row_of):
        for q in range(4):
            for g in range(GROUPS):
                at = slice(q * SLOTS + g * 3, q * SLOTS + g * 3 + 3)
                dense[at, :] = ref[row_of(g) : row_of(g) + 3, q * WIDE : (q + 1) * WIDE]
        return dense[...].astype(I32).astype(I16)

    def unpacked(codes, ref, row_of):
        codes = codes.astype(I32).astype(F32)
        for q in range(4):
            for g in range(GROUPS):
                at = slice(q * SLOTS + g * 3, q * SLOTS + g * 3 + 3)
                ref[row_of(g) : row_of(g) + 3, q * WIDE : (q + 1) * WIDE] = codes[at, :]

    pad_f[...] = pad_f[...] - 32768.0
    code[...] = packed(pad_f, lambda g: g * 4)
    temp[...] = half_turn(pad_f[...], False)
    code_right[...] = packed(temp, lambda g: g * 4)

    loads[5].wait()
    loads[6].wait()
    for i in range(2):
        back_even[i * SIDE : i * SIDE + SIDE, :SIDE] = back_raw[i].astype(F32)
    even = back_even[pl.ds(0, SIDE, stride=2), :SIDE]
    odd = back_even[pl.ds(1, SIDE, stride=2), :SIDE]
    back_even[:SIDE, :] = jnp.concatenate([even, odd], axis=1)
    for q in range(PIX // 128):
        back[:2, q * 128 : q * 128 + 128] = back_even[pl.ds(q, 2, stride=32), :]
    back[2:, :] = jnp.zeros((14, PIX), F32)
    x3[3 * NEAR :, :] = back[...].astype(BF16)

    pl.semaphore_wait(barrier, expected)

    def remote(src, dst, send, recv, d):
        target_id = place(d) if isinstance(d, int) else (r + d[0], c + d[1])
        return pltpu.make_async_remote_copy(
            src_ref=src, dst_ref=dst, send_sem=send, recv_sem=recv, device_id=target_id, device_id_type=MESH
        )

    pending = []

    def start(copy, ok):
        @pl.when(ok)
        def _():
            copy.start()

        pending.append((copy, ok))

    def arrived(copy, ok):
        @pl.when(ok)
        def _():
            copy.wait_recv()

    def cm_copy(src, slot, d):
        return remote(src, r_cm.at[slot], cm_send.at[slot], cm_recv.at[slot], d)

    def code_copy(source, slot, part, d):
        at = pl.ds(part * (WIDE // PARTS), WIDE // PARTS)
        if source is None:
            source = code_right.at[:, at] if slot == 2 else code.at[:, at]
        else:
            source = r_code.at[source, :, at]
        return remote(source, r_code.at[slot, :, at], r_send.at[slot, part], r_recv.at[slot, part], d)

    start(cm_copy(cm, LEFT, RIGHT), there(RIGHT))
    for part in range(PARTS):
        start(code_copy(None, 2, part, RIGHT), there(RIGHT))
    def own_down(role):
        start(cm_copy(cm, UP, DOWN), there(DOWN) & role)
        for part in range(PARTS):
            start(code_copy(None, 1, part, DOWN), there(DOWN) & role)

    own_down(jnp.logical_not(west))
    start(cm_copy(cm, RIGHT, LEFT), east)

    arrived(cm_copy(cm, LEFT, LEFT), there(LEFT))
    start(cm_copy(r_cm.at[LEFT], UL, DOWN), there(DOWN) & there(LEFT))
    for part in range(PARTS):
        arrived(code_copy(None, 2, part, LEFT), there(LEFT))
        start(code_copy(2, 0, part, DOWN), there(DOWN) & there(LEFT))
    own_down(west)
    arrived(cm_copy(cm, UP, UP), there(UP))
    arrived(cm_copy(cm, UL, UL), there(UL))

    def cm_of(tile, rows_at, lanes_at):
        if tile == OWN:
            return cm[rows_at, lanes_at]
        return r_cm[tile, rows_at, lanes_at]

    for g in range(GROUPS):
        for t in range(4):
            at = slice(g * PAD + t * 4, g * PAD + t * 4 + 4)
            near_cm[at, :] = cm_of(TILE_SETS[0][t], slice(g * 4, g * 4 + 4), slice(None))
    near_high, near_low = split(near_cm[:, :FRAMES])

    frame = lax.broadcasted_iota(I32, (NEAR, FRAMES), 1)
    weighted = jnp.where((frame >= window[0]) & (frame < window[1]), near_cm[:, :FRAMES], 0.0)
    w_high, w_low = split(weighted)
    w_both = jnp.concatenate([w_high, w_low], axis=0)
    q4 = nt(w_both, w_both)
    q = q4[:NEAR, :NEAR] + q4[:NEAR, NEAR:] + q4[NEAR:, :NEAR] + q4[NEAR:, NEAR:]
    a_near = near_cm[:, FRAMES : FRAMES + 1].astype(I32)
    b_near = near_cm[:, FRAMES + 1 : FRAMES + 2].astype(I32)
    live_near = near_cm[:, FRAMES + 2 : FRAMES + 3]
    eye = lax.broadcasted_iota(I32, (NEAR, NEAR), 0) == lax.broadcasted_iota(I32, (NEAR, NEAR), 1)
    mass = jnp.sum(jnp.where(eye, q, 0.0), axis=1, keepdims=True)
    inverse = 1.0 / jnp.where(live_near > 0, mass, 1.0)
    q_high, q_low = split(jnp.where(eye, 0.0, q) * inverse)
    q3 = jnp.concatenate([q_high, q_high, q_low], axis=1)
    load0 = jnp.sum(weighted * back_time[0:1, :], axis=1, keepdims=True)
    load1 = jnp.sum(weighted * back_time[1:2, :], axis=1, keepdims=True)

    tile_at = (lax.broadcasted_iota(I32, (NEAR, 1), 0) >> 2) & 3
    above = tile_at < 2
    aside = (tile_at & 1) == 0
    y_low = jnp.where(above, 0, a_near)
    y_high = jnp.where(live_near > 0, jnp.where(above, a_near, SIDE), 0)
    x_low = jnp.where(aside, 0, b_near)
    x_high = jnp.where(aside, b_near, SIDE)

    def covered(rows_at, begin, width):
        spot = lax.broadcasted_iota(I32, (1, width), 1) + begin
        y = spot >> 6
        x = spot & 63
        return (
            (y >= y_low[rows_at]) & (y < y_high[rows_at]) & (x >= x_low[rows_at]) & (x < x_high[rows_at])
        )

    loads[7].wait()
    width = 1024
    for begin in range(0, PIX, width):
        at = slice(begin, begin + width)
        pull = nt(w_high, movie[at, :])
        pull = pull - load0 * back[0:1, at] - load1 * back[1:2, at]
        target[:, at] = jnp.where(covered(slice(None), begin, width), pull * inverse, -BIG)

    for part in range(PARTS):
        arrived(code_copy(None, 1, part, UP), there(UP))
    for part in range(PARTS):
        arrived(code_copy(None, 0, part, UL), there(UL))
    for t in range(3):
        unpacked(r_code[t], canvas, lambda g: g * PAD + t * 4)
    for g in range(GROUPS):
        canvas[g * PAD + 12 : g * PAD + 16, :] = pad_f[g * 4 : g * 4 + 4, :]
    for g in range(GROUPS):
        rows_at = slice(g * PAD, g * PAD + PAD)
        value = jnp.where(covered(rows_at, 0, PIX), (canvas[rows_at, :] + 32768.0) * (1.0 / 65535.0), 0.0)
        high, low = split(value)
        x3[g * PAD : g * PAD + PAD, :] = high
        x3[NEAR + g * PAD : NEAR + g * PAD + PAD, :] = low
        x3[2 * NEAR + g * PAD : 2 * NEAR + g * PAD + PAD, :] = high

    gram = nt(x3[: 2 * NEAR, :], x3[NEAR:, :])
    gram = gram[:NEAR] + gram[NEAR:]
    overlap = gram[:, :NEAR] + gram[:, NEAR : 2 * NEAR]
    loading = gram[:, 2 * NEAR : 2 * NEAR + 2]
    drive = mm(x3[:NEAR, :], movie[...])
    drive = drive - loading[:, 0:1] * back_time[0:1, :] - loading[:, 1:2] * back_time[1:2, :]
    self_overlap = jnp.sum(jnp.where(eye, overlap, 0.0), axis=1, keepdims=True)
    overlap = jnp.where(eye, 0.0, overlap)
    o_high, o_low = split(overlap)
    product = mm(jnp.concatenate([o_high, o_low], axis=0), near_high)
    shares[:, :FRAMES] = drive - (product[:NEAR] + product[NEAR:] + mm(o_high, near_low))
    shares[:, FRAMES : FRAMES + NEAR] = overlap
    shares[:, FRAMES + NEAR :] = jnp.broadcast_to(self_overlap, (NEAR, 128 - NEAR))
    for t in range(4):
        for g in range(GROUPS):
            share_out[t, g * 4 : g * 4 + 4, :] = shares[g * PAD + t * 4 : g * PAD + t * 4 + 4, :]

    def share_copy(t, d):
        return remote(share_out.at[t], r_share.at[t], s_send.at[t], s_recv.at[t], d)

    for t, d in ((2, LEFT), (0, UL), (1, UP)):
        start(share_copy(t, d), there(d))

    def mate_share(t, k, d):
        return remote(share_out.at[t], r_mate.at[k], mate_send.at[t], mate_recv.at[k], d)

    start(mate_share(3, 0, (0, 1)), west)
    start(mate_share(0, 3, (-1, 0)), east & row_ok(-1))

    for g in range(GROUPS):
        rows_at = slice(g * PAD, g * PAD + PAD)
        value = jnp.maximum(target[rows_at, :] - mm(q3[rows_at, :], x3[: 3 * NEAR, :]), 0.0)
        canvas[rows_at, :] = jnp.floor(jnp.sqrt(value * (1.0 / TOP)) * 65535.0 + 0.5) - 32768.0
        if g < GROUPS - 1:
            high, low = split(value)
            x3[g * PAD : g * PAD + PAD, :] = high
            x3[NEAR + g * PAD : NEAR + g * PAD + PAD, :] = low
            x3[2 * NEAR + g * PAD : 2 * NEAR + g * PAD + PAD, :] = high

    for t in range(2):
        piece_up[t] = packed(canvas, lambda g: g * PAD + t * 4)

    def piece_copy(t, d):
        return remote(piece_up.at[t], r_piece.at[t], p_send.at[t], p_recv.at[t], d)

    for t in range(2):
        start(piece_copy(t, UP), there(UP) & (c < cols // 2))

    arrived(share_copy(1, DOWN), there(DOWN))
    start(remote(r_share.at[1], r_mate.at[2], mate_send.at[1], mate_recv.at[2], RIGHT), west & row_ok(1))
    for t, d in ((2, RIGHT), (0, DR)):
        arrived(share_copy(t, d), there(d))

    def joined(parts, live):
        total = parts[0] + parts[1] + parts[2] + parts[3]
        scale = 1.0 / jnp.where(live > 0, total[:, FRAMES + NEAR : FRAMES + NEAR + 1], 1.0)
        v = jnp.concatenate([part[:, FRAMES : FRAMES + NEAR] for part in parts], axis=1) * scale
        return total[:, :FRAMES] * scale, v

    def weights(v, g):
        high, low = split(jnp.concatenate([v[:, k * NEAR + g * PAD : k * NEAR + g * PAD + PAD] for k in range(4)], axis=1))
        return jnp.concatenate([high, high, low], axis=1)

    goal, v_own = joined([share_out[3], r_share[2], r_share[1], r_share[0]], live_own)
    v_parts = [weights(v_own, g) for g in range(3)]
    own = cm[:, :FRAMES]
    row_group = lax.broadcasted_iota(I32, (PAD, FRAMES), 0) >> 2

    def changes(sources, full):
        for k in range(4):
            for t in range(4):
                if TILE_SETS[k][t] not in sources:
                    continue
                new = sources[TILE_SETS[k][t]]
                at = slice(k * PAD + t * 4, k * PAD + t * 4 + 4)
                full[at, :128] = new[:4, :]
                full[at, 128:] = new[4:, :]
        high, low = split(full[...])
        return jnp.concatenate([high, low, high], axis=0)

    def updated(g, left_over, old, live):
        chosen = (row_group == g) & (live > 0)
        return jnp.where(chosen, jnp.maximum(left_over, 0.0), old)

    def pack(ref, g, new, old):
        change = new - old
        ref[g, :4, :] = change[g * 4 : g * 4 + 4, :128]
        ref[g, 4:, :] = change[g * 4 : g * 4 + 4, 128:]

    def wave_copy(g, d, slot):
        return remote(wave.at[g], r_wave.at[g, slot], t_send.at[g, slot], t_recv.at[g, slot], d)

    def sends(g, d):
        ok = there(d)
        if DIRS[d][1] > 0:
            ok = ok & jnp.logical_not(west)
        if DIRS[d][1] < 0 and g > 0:
            ok = ok & jnp.logical_not(east)
        return ok

    def gets(g, d):
        ok = there(d)
        if DIRS[d][1] > 0 and g > 0:
            ok = ok & jnp.logical_not(west)
        if DIRS[d][1] < 0:
            ok = ok & jnp.logical_not(east)
        return ok

    def mate_copy(g, at, d, slot):
        return remote(mate_wave.at[g], r_wave.at[g, slot], mw_send.at[g, at], t_recv.at[g, slot], d)

    def far_copy(g, down, right):
        return remote(wave.at[g], r_far.at[g, 1 - down], far_send.at[g, 1 - down], far_recv.at[g, 1 - down], (down, right))

    def outer_copy(at, d):
        return remote(outer_wave, r_far.at[1, 2 - at], ow_send.at[at // 2], far_recv.at[1, 2 - at], d)

    joint_copy = remote(joint, r_joint, joint_sem.at[0], joint_sem.at[1], LEFT)
    outer_sum = remote(outer, r_outer, outer_sem.at[0], outer_sem.at[1], (0, 2))

    sides = (
        (west, 1, RIGHT, UR, DR, {UL: UP, LEFT: OWN, DL: DOWN, UP: UR, OWN: RIGHT, DOWN: DR}, (UR, RIGHT, DR)),
        (east, 0, LEFT, UL, DL, {UR: UP, RIGHT: OWN, DR: DOWN, UP: UL, OWN: LEFT, DOWN: DL}, (UL, LEFT, DL)),
    )

    def start_mate(g):
        for role, first, mate, over, under, _, _ in sides:
            if g < first:
                continue

            @pl.when(role)
            def _(mate=mate):
                r_wave[g, mate] = mate_wave[g]

            start(mate_copy(g, 0, UP, under), role & there(UP))
            start(mate_copy(g, 1, DOWN, over), role & there(DOWN))

    left_over = goal
    for g in range(GROUPS):
        if g == GROUPS - 1:
            arrived(remote(merged, r_merged, m_send, m_recv, RIGHT), there(RIGHT))
            spot = lax.broadcasted_iota(I32, (PAD, PIX), 1)
            y = spot >> 6
            x = spot & 63
            a_int = a_own.astype(I32)
            b_int = b_own.astype(I32)
            unpacked(r_merged[...], far_f, lambda k: k * 4)
            unpacked(r_piece[1], near_f, lambda k: k * 4)
            for k in range(GROUPS):
                temp[k * 4 : k * 4 + 4, :] = canvas[k * PAD + 12 : k * PAD + 16, :]
            near = jnp.where(y < a_int, near_f[...], temp[...])
            pad_f[...] = jnp.where(x < b_int, half_turn(far_f[...], True), near) + 32768.0
            for half in range(2):
                part = slice(half * 8, half * 8 + 8)
                pad_f[part, :] = turn(pad_f[part, :], shift_own[part], False)
            whole = pad_f[...]
            upper = jnp.floor(whole * (1.0 / 256.0))
            hl[:PAD, :] = upper.astype(BF16)
            hl[PAD:, :] = (whole - upper * 256.0).astype(BF16)
            unpick_hl = jnp.concatenate([unpick16 * 256.0, unpick16], axis=1).astype(BF16)
            root = mm(unpick_hl, hl[...])[:SLOTS, :] * (1.0 / 65535.0)
            pad_f[:SLOTS, :] = root * root * TOP
            for q in range(PIX // 128):
                out_shapes[pl.ds(q, SLOTS, stride=32), :] = pad_f[:SLOTS, q * 128 : q * 128 + 128]

        if g > 0:
            for d in (UP, DOWN, LEFT, UL, DL):
                arrived(wave_copy(g - 1, d, d), gets(g - 1, d))
            if g == 1:
                @pl.when(beside_west)
                def _():
                    sources = {d: r_wave[0, d] for d in (UP, DOWN, LEFT, UL, DL)}
                    sources[OWN] = wave[0]
                    aim = jnp.where(live_own > 0, goal - mm(v_parts[0], changes(sources, mate_f)), own)
                    for at, value in enumerate((aim, own, v_own)):
                        outer[at, :4, :] = value[4:8, :128]
                        outer[at, 4:, :] = value[4:8, 128:]

                start(outer_sum, beside_west)
            for d in (RIGHT, UR, DR):
                arrived(wave_copy(g - 1, d, d), gets(g - 1, d))
            for role, first, mate, over, under, _, _ in sides:
                if g - 1 >= first:
                    arrived(mate_copy(g - 1, 0, UP, over), role & there(UP))
                    arrived(mate_copy(g - 1, 1, DOWN, under), role & there(DOWN))
            around = {**{d: r_wave[g - 1, d] for d in range(8)}, OWN: wave[g - 1]}
            left_over = left_over - mm(v_parts[g - 1], changes(around, call_f))
        new = updated(g, left_over, own, live_own)
        if g < GROUPS - 1:
            pack(wave, g, new, own)
            for d in (UL, DL, LEFT, UR, DR, RIGHT, UP, DOWN):
                start(wave_copy(g, d, 7 - d), sends(g, d))
            if g < 2:
                for down in (-1, 0, 1):
                    if g == 0:
                        start(far_copy(g, down, 2), beside_west & row_ok(down))
                    start(far_copy(g, down, -2), beside_east & row_ok(down))
        own = new
        if g == 0:
            @pl.when(east)
            def _():
                joint[:, :FRAMES] = goal
                joint[:, FRAMES:] = v_own

            start(joint_copy, east)

            for t in range(2):
                start(piece_copy(t, UP), there(UP) & (c >= cols // 2))

            arrived(mate_share(3, 0, (0, -1)), east)
            arrived(mate_share(1, 2, (0, -1)), east & row_ok(1))
            arrived(mate_share(0, 3, (1, 0)), east & row_ok(1))

            @pl.when(east)
            def _():
                mate_cm[...] = r_cm[LEFT]
                r_mate[1] = share_out[2]
                live = mate_cm[:, FRAMES + 2 : FRAMES + 3]
                mate_goal[...], v_mate = joined([r_mate[k] for k in range(4)], live)
                for k in range(2):
                    mate_v[k] = weights(v_mate, k)
                old = mate_cm[:, :FRAMES]
                pack(mate_wave, 0, updated(0, mate_goal[...], old, live), old)

            start_mate(0)

            for q in range(4):
                for k in range(GROUPS):
                    at = slice(q * SLOTS + k * 3, q * SLOTS + k * 3 + 3)
                    labels[at, :] = r_cm[LEFT, k * 4 : k * 4 + 3, FRAMES:]
            a_left = labels[:, 0:1].astype(I32)
            row = lax.broadcasted_iota(I32, (DENSE, WIDE), 0)
            quarter = (row >= SLOTS).astype(I32) + (row >= 2 * SLOTS).astype(I32) + (row >= 3 * SLOTS).astype(I32)
            below = quarter * 16 + (lax.broadcasted_iota(I32, (DENSE, WIDE), 1) >> 6) < a_left
            left_codes = packed(canvas, lambda k: k * PAD + 8).astype(I32)
            for t in range(2):
                arrived(piece_copy(t, DOWN), there(DOWN))
            merged[...] = jnp.where(below, r_piece[0].astype(I32), left_codes).astype(I16)
            start(remote(merged, r_merged, m_send, m_recv, LEFT), there(LEFT))
        elif g < GROUPS - 1:
            if g == 1:
                arrived(cm_copy(cm, RIGHT, RIGHT), west)
                arrived(joint_copy, west)

                @pl.when(west)
                def _():
                    mate_cm[...] = r_cm[RIGHT]
                    mate_goal[...] = r_joint[:, :FRAMES]
                    for k in range(2):
                        mate_v[k] = weights(r_joint[:, FRAMES:], k)

            for down in (-1, 0, 1):
                arrived(far_copy(g - 1, -down, -2), west & row_ok(down))
                if g == 1:
                    arrived(far_copy(g - 1, -down, 2), east & row_ok(down))
                elif down:
                    arrived(outer_copy(1 - down, (down, 0)), east & row_ok(down))
            for role, first, mate, over, under, where_at, far_at in sides:
                @pl.when(role)
                def _(where_at=where_at, far_at=far_at):
                    sources = {}
                    for tile, at in where_at.items():
                        sources[tile] = wave[g - 1] if at == OWN else r_wave[g - 1, at]
                    for down, tile in enumerate(far_at):
                        sources[tile] = r_far[g - 1, down]
                    old = mate_cm[:, :FRAMES]
                    live = mate_cm[:, FRAMES + 2 : FRAMES + 3]
                    rest = mate_goal[...] - mm(mate_v[g - 1], changes(sources, mate_f))
                    mate_goal[...] = rest
                    pack(mate_wave, g, updated(g, rest, old, live), old)

            start_mate(g)
            if g == 1:
                arrived(outer_sum, east)

                @pl.when(east)
                def _():
                    rhs = changes({UR: r_wave[0, UL], RIGHT: r_wave[0, LEFT], DR: r_wave[0, DL]}, outer_f)
                    zero = jnp.zeros((4, FRAMES), F32)
                    aim, old, v = (
                        jnp.concatenate(
                            [zero, jnp.concatenate([r_outer[at, :4, :], r_outer[at, 4:, :]], axis=1), zero, zero], axis=0
                        )
                        for at in range(3)
                    )
                    value = jnp.maximum(aim - mm(weights(v, 0), rhs), 0.0)
                    pack2 = value - old
                    outer_wave[:4, :] = pack2[4:8, :128]
                    outer_wave[4:, :] = pack2[4:8, 128:]
                    r_far[1, 1] = outer_wave[...]

                start(outer_copy(0, UP), east & there(UP))
                start(outer_copy(2, DOWN), east & there(DOWN))

    back_own = jnp.dot(unpick16, own, precision=lax.Precision.HIGHEST, preferred_element_type=F32)
    new_traces = jnp.where(alive_sub[:SLOTS, 0:1], back_own[:SLOTS, :], old_traces)
    for half in range(2):
        out_traces[pl.ds(half, SLOTS, stride=2), :] = new_traces[:, half * 128 : half * 128 + 128]

    for copy, ok in pending:
        @pl.when(ok)
        def _(copy=copy):
            copy.wait_send()


def on_device(rows, cols, movie, footprints, anchors, groups, counts, temporal, back_spatial, back_temporal, window):
    vmem = pl.BlockSpec(memory_space=pltpu.VMEM)
    dma = pltpu.SemaphoreType.DMA
    shapes, traces = pl.pallas_call(
        functools.partial(kernel, rows, cols),
        out_shape=(
            jax.ShapeDtypeStruct((SLOTS * PIX // 128, 128), F32),
            jax.ShapeDtypeStruct((SLOTS * FRAMES // 128, 128), F32),
        ),
        in_specs=[pl.BlockSpec(memory_space=pltpu.SMEM)] + [pl.BlockSpec(memory_space=pltpu.HBM)] * 8,
        out_specs=(vmem, vmem),
        scratch_shapes=[
            pltpu.SMEM((2, SLOTS), I32),
            pltpu.SMEM((1, SLOTS), I32),
            pltpu.SMEM((2,), I32),
            pltpu.VMEM((SLOTS * PIX // 128, 128), F32),
            pltpu.VMEM((SLOTS * FRAMES // 128, 128), F32),
            pltpu.VMEM((2, SIDE, SIDE), BF16),
            pltpu.VMEM((2, FRAMES), F32),
            pltpu.VMEM((PIX, FRAMES), BF16),
            pltpu.VMEM((2 * SIDE, 2 * SIDE), F32),
            pltpu.VMEM((16, PIX), F32),
            pltpu.VMEM((PAD, PIX), F32),
            pltpu.VMEM((2 * PAD, PIX), BF16),
            pltpu.VMEM((DENSE, WIDE), I16),
            pltpu.VMEM((DENSE, WIDE), I16),
            pltpu.VMEM((3, DENSE, WIDE), I16),
            pltpu.VMEM((PAD, FRAMES + 128), F32),
            pltpu.VMEM((8, PAD, FRAMES + 128), F32),
            pltpu.VMEM((NEAR, FRAMES + 128), F32),
            pltpu.VMEM((NEAR, PIX), F32),
            pltpu.VMEM((NEAR, PIX), F32),
            pltpu.VMEM((3 * NEAR + 16, PIX), BF16),
            pltpu.VMEM((NEAR, FRAMES + 128), F32),
            pltpu.VMEM((4, PAD, FRAMES + 128), F32),
            pltpu.VMEM((3, PAD, FRAMES + 128), F32),
            pltpu.VMEM((3, 8, 128), F32),
            pltpu.VMEM((3, 8, 8, 128), F32),
            pltpu.VMEM((4 * PAD, FRAMES), F32),
            pltpu.VMEM((PAD, PIX), F32),
            pltpu.VMEM((DENSE, WIDE), F32),
            pltpu.VMEM((DENSE, 128), F32),
            pltpu.VMEM((PAD, PIX), F32),
            pltpu.VMEM((PAD, PIX), F32),
            pltpu.VMEM((4, PAD, FRAMES + 128), F32),
            pltpu.VMEM((PAD, FRAMES + 128), F32),
            pltpu.VMEM((PAD, FRAMES), F32),
            pltpu.VMEM((2, PAD, 3 * NEAR), BF16),
            pltpu.VMEM((3, 8, 128), F32),
            pltpu.VMEM((2, 3, 8, 128), F32),
            pltpu.VMEM((4 * PAD, FRAMES), F32),
            pltpu.VMEM((PAD, 2 * FRAMES), F32),
            pltpu.VMEM((PAD, 2 * FRAMES), F32),
            pltpu.VMEM((3, 8, 128), F32),
            pltpu.VMEM((3, 8, 128), F32),
            pltpu.VMEM((8, 128), F32),
            pltpu.VMEM((4 * PAD, FRAMES), F32),
            pltpu.VMEM((2, DENSE, WIDE), I16),
            pltpu.VMEM((2, DENSE, WIDE), I16),
            pltpu.VMEM((DENSE, WIDE), I16),
            pltpu.VMEM((DENSE, WIDE), I16),
            dma((8,)),
            dma((8,)),
            dma((8,)),
            dma((3, PARTS)),
            dma((3, PARTS)),
            dma((3,)),
            dma((3,)),
            dma((3, 8)),
            dma((3, 8)),
            dma((2,)),
            dma((2,)),
            dma,
            dma,
            dma((4,)),
            dma((4,)),
            dma((3, 2)),
            dma((2, 3)),
            dma((2, 3)),
            dma((2,)),
            dma((2,)),
            dma((2,)),
        ],
        compiler_params=pltpu.CompilerParams(collective_id=0, has_side_effects=True, vmem_limit_bytes=32 << 20),
    )(
        counts,
        *(
            pltpu.with_memory_space_constraint(x, pltpu.HBM)
            for x in (
                anchors.reshape(SLOTS, 2).T,
                groups.reshape(1, SLOTS),
                window,
                footprints.reshape(SLOTS * PIX // 128, 128),
                temporal.reshape(SLOTS * FRAMES // 128, 128),
                back_spatial,
                back_temporal,
                movie.reshape(PIX, FRAMES),
            )
        )
    )
    return shapes.reshape(1, 1, SLOTS, PIX), traces.reshape(1, 1, SLOTS, FRAMES)


def solution(mesh):
    return jax.shard_map(
        functools.partial(on_device, mesh.shape["row"], mesh.shape["col"]),
        mesh=mesh,
        in_specs=(
            P("row", "col", None),
            P("row", "col", None, None),
            P("row", "col", None, None),
            P("row", "col", None),
            P("row", "col"),
            P("row", "col", None, None),
            P(None, "row", "col"),
            P(),
            P(),
        ),
        out_specs=(P("row", "col", None, None), P("row", "col", None, None)),
        check_vma=False,
    )
```

```python
import functools

import jax
import jax.numpy as jnp
from jax import lax
from jax.experimental import pallas as pl
from jax.experimental.pallas import tpu as pltpu
from jax.sharding import PartitionSpec as P

MESH = pl.DeviceIdType.MESH
F32 = jnp.float32
BF16 = jnp.bfloat16
I32 = jnp.int32
I16 = jnp.int16

SIDE = 64
PIX = SIDE * SIDE
FRAMES = 256
SLOTS = 12
GROUPS = 4
PAD = 16
NEAR = 4 * PAD
BIG = 1e30
DENSE = 4 * SLOTS
WIDE = PIX // 4
TOP = 8.0

DIRS = ((-1, -1), (-1, 0), (-1, 1), (0, -1), (0, 1), (1, -1), (1, 0), (1, 1))
UL, UP, UR, LEFT, RIGHT, DL, DOWN, DR = range(8)
OWN = 8
TILE_SETS = (
    (UL, UP, LEFT, OWN),
    (UP, UR, OWN, RIGHT),
    (LEFT, OWN, DL, DOWN),
    (OWN, RIGHT, DOWN, DR),
)
PARTS = 4


def nt(a, b):
    return lax.dot_general(a, b, (((1,), (1,)), ((), ())), preferred_element_type=F32)


def mm(a, b):
    return jnp.dot(a, b, preferred_element_type=F32)


def split(x):
    high = x.astype(BF16)
    return high, (x - high.astype(F32)).astype(BF16)


def turn(x, shift, forward):
    for bit in range(12):
        step = 1 << bit
        chosen = ((shift >> bit) & 1) == 1
        by = step if forward else PIX - step
        if by % 128 == 0:
            moved = jnp.concatenate([x[:, PIX - by :], x[:, : PIX - by]], axis=1)
        else:
            moved = pltpu.roll(x, by, 1)
        x = jnp.where(chosen, moved, x)
    return x


def half_turn(x, forward):
    return pltpu.roll(x, SIDE if forward else PIX - SIDE, 1)


def kernel(
    rows, cols,
    counts, anchors_in, groups_in, window_in, footprints_in, temporal_in, back_in, back_time_in, movie_in,
    out_shapes, out_traces,
    anchors, groups, window, footprints, temporal, back_raw, back_time, movie, back_even, back, pad_f, hl, code, code_right, r_code, cm, r_cm, near_cm, target, canvas, x3,
    shares, share_out, r_share, wave, r_wave, call_f, temp, dense, labels, far_f, near_f,
    r_mate, mate_cm, mate_goal, mate_v, mate_wave, r_far, mate_f,
    joint, r_joint, outer, r_outer, outer_wave, outer_f,
    piece_up, r_piece, merged, r_merged,
    load_sem, cm_send, cm_recv, r_send, r_recv, s_send, s_recv, t_send, t_recv, p_send, p_recv, m_send, m_recv,
    mate_send, mate_recv, mw_send, far_send, far_recv, joint_sem, outer_sem, ow_send,
):
    r = lax.axis_index("row")
    c = lax.axis_index("col")

    def there(d):
        down, right = DIRS[d]
        ok = None
        for at, step, count in ((r, down, rows), (c, right, cols)):
            if step:
                one = at + step >= 0 if step < 0 else at + step < count
                ok = one if ok is None else ok & one
        return ok

    def place(d):
        return (r + DIRS[d][0], c + DIRS[d][1])

    west = c == cols // 2 - 1
    east = c == cols // 2
    beside_west = c == cols // 2 - 2
    beside_east = c == cols // 2 + 1

    def row_ok(step):
        return (r + step >= 0) & (r + step < rows)

    barrier = pltpu.get_barrier_semaphore()

    loads = [
        pltpu.make_async_copy(source, target_ref, load_sem.at[at])
        for at, (source, target_ref) in enumerate(
            (
                (groups_in, groups),
                (anchors_in, anchors),
                (window_in, window),
                (temporal_in, temporal),
                (footprints_in, footprints),
                (back_time_in, back_time),
                (back_in, back_raw),
                (movie_in, movie),
            )
        )
    ]
    for load in loads:
        load.start()

    expected = 0
    for d in range(8):
        ok = there(d)
        hears = ok & jnp.logical_not(west) if d in (UR, DR) else ok
        tells = ok & jnp.logical_not(east) if d in (UL, DL) else ok

        @pl.when(tells)
        def _(d=d):
            pl.semaphore_signal(barrier, inc=1, device_id=place(d), device_id_type=MESH)

        expected = expected + hears.astype(I32)
    for down in (-1, 0, 1):
        for right, receiver, sender in ((2, west, beside_east), (-2, east, beside_west)):
            @pl.when(receiver & row_ok(down))
            def _(down=down, right=right):
                pl.semaphore_signal(barrier, inc=1, device_id=(r + down, c + right), device_id_type=MESH)

            expected = expected + (sender & row_ok(down)).astype(I32)

    for d in range(8):
        @pl.when(jnp.logical_not(there(d)))
        def _(d=d):
            r_cm[d] = jnp.zeros((PAD, FRAMES + 128), F32)
            for g in range(3):
                r_wave[g, d] = jnp.zeros((8, 128), F32)

    for t, d in ((0, DR), (1, DOWN), (2, RIGHT)):
        @pl.when(jnp.logical_not(there(d)))
        def _(t=t):
            r_share[t] = jnp.zeros((PAD, FRAMES + 128), F32)

    @pl.when(jnp.logical_not(row_ok(1)))
    def _():
        r_mate[2] = jnp.zeros((PAD, FRAMES + 128), F32)
        r_mate[3] = jnp.zeros((PAD, FRAMES + 128), F32)

    for down in (-1, 1):
        @pl.when(jnp.logical_not(row_ok(down)))
        def _(down=down):
            for g in range(2):
                r_far[g, 1 + down] = jnp.zeros((8, 128), F32)

    for ref in (far_f, near_f, mate_f, outer_f):
        ref[...] = jnp.zeros_like(ref)

    for load in loads[:4]:
        load.wait()
    sub = lax.broadcasted_iota(I32, (PAD, 128), 0)
    lane = lax.broadcasted_iota(I32, (PAD, 128), 1)
    g_sub = jnp.full((PAD, 128), -1, I32)
    g_lane = jnp.full((PAD, 128), -1, I32)
    a_lane = jnp.zeros((PAD, 128), I32)
    b_lane = jnp.zeros((PAD, 128), I32)
    count = counts[0, 0]
    for m in range(SLOTS):
        g_sub = jnp.where(sub == m, groups[0, m], g_sub)
        g_lane = jnp.where(lane == m, groups[0, m], g_lane)
        a_lane = jnp.where(lane == m, anchors[0, m], a_lane)
        b_lane = jnp.where(lane == m, anchors[1, m], b_lane)
    alive_lane = lane < count
    alive_sub = sub < count
    a_lane = jnp.where(alive_lane, a_lane, 0)
    b_lane = jnp.where(alive_lane, b_lane, 0)
    same = g_sub == g_lane
    before_lane = jnp.sum(jnp.where(same & (sub < lane), 1.0, 0.0), axis=0, keepdims=True)
    before_sub = jnp.sum(jnp.where(same & (lane < sub), 1.0, 0.0), axis=1, keepdims=True)
    pos_lane = g_lane.astype(F32) * 4.0 + before_lane
    pos_sub = g_sub.astype(F32) * 4.0 + before_sub
    pick = jnp.where((sub.astype(F32) == pos_lane) & (lane < SLOTS), 1.0, 0.0)
    unpick = jnp.where((lane.astype(F32) == pos_sub) & (sub < SLOTS), 1.0, 0.0)
    a_own = jnp.sum(pick * a_lane.astype(F32), axis=1, keepdims=True)
    b_own = jnp.sum(pick * b_lane.astype(F32), axis=1, keepdims=True)
    live_own = jnp.sum(pick * jnp.where(alive_lane, 1.0, 0.0), axis=1, keepdims=True)
    shift_own = (a_own * float(SIDE) + b_own).astype(I32)
    pick16 = pick[:, :PAD]
    unpick16 = unpick[:, :PAD]

    pad_f[SLOTS:PAD, :] = jnp.zeros((PAD - SLOTS, PIX), F32)
    for half in range(2):
        pad_f[:SLOTS, half * 128 : half * 128 + 128] = temporal[pl.ds(half, SLOTS, stride=2), :]
    old_traces = pad_f[:SLOTS, :FRAMES]
    cm[:, :FRAMES] = jnp.dot(pick16, pad_f[:, :FRAMES], precision=lax.Precision.HIGHEST, preferred_element_type=F32)
    cm[:, FRAMES:] = jnp.where(lane == 0, a_own, jnp.where(lane == 1, b_own, jnp.where(lane == 2, live_own, 0.0)))

    loads[4].wait()
    for q in range(PIX // 128):
        pad_f[:SLOTS, q * 128 : q * 128 + 128] = footprints[pl.ds(q, SLOTS, stride=32), :]
    whole = jnp.floor(pad_f[...] * 65535.0 + 0.5)
    upper = jnp.floor(whole * (1.0 / 256.0))
    hl[:PAD, :] = upper.astype(BF16)
    hl[PAD:, :] = (whole - upper * 256.0).astype(BF16)
    pick_hl = jnp.concatenate([pick16 * 256.0, pick16], axis=1).astype(BF16)
    pad_f[...] = mm(pick_hl, hl[...])
    for half in range(2):
        part = slice(half * 8, half * 8 + 8)
        pad_f[part, :] = turn(pad_f[part, :], shift_own[part], True)

    def packed(ref, row_of):
        for q in range(4):
            for g in range(GROUPS):
                at = slice(q * SLOTS + g * 3, q * SLOTS + g * 3 + 3)
                dense[at, :] = ref[row_of(g) : row_of(g) + 3, q * WIDE : (q + 1) * WIDE]
        return dense[...].astype(I32).astype(I16)

    def unpacked(codes, ref, row_of):
        codes = codes.astype(I32).astype(F32)
        for q in range(4):
            for g in range(GROUPS):
                at = slice(q * SLOTS + g * 3, q * SLOTS + g * 3 + 3)
                ref[row_of(g) : row_of(g) + 3, q * WIDE : (q + 1) * WIDE] = codes[at, :]

    pad_f[...] = pad_f[...] - 32768.0
    code[...] = packed(pad_f, lambda g: g * 4)
    temp[...] = half_turn(pad_f[...], False)
    code_right[...] = packed(temp, lambda g: g * 4)

    loads[5].wait()
    loads[6].wait()
    for i in range(2):
        back_even[i * SIDE : i * SIDE + SIDE, :SIDE] = back_raw[i].astype(F32)
    even = back_even[pl.ds(0, SIDE, stride=2), :SIDE]
    odd = back_even[pl.ds(1, SIDE, stride=2), :SIDE]
    back_even[:SIDE, :] = jnp.concatenate([even, odd], axis=1)
    for q in range(PIX // 128):
        back[:2, q * 128 : q * 128 + 128] = back_even[pl.ds(q, 2, stride=32), :]
    back[2:, :] = jnp.zeros((14, PIX), F32)
    x3[3 * NEAR :, :] = back[...].astype(BF16)

    pl.semaphore_wait(barrier, expected)

    def remote(src, dst, send, recv, d):
        target_id = place(d) if isinstance(d, int) else (r + d[0], c + d[1])
        return pltpu.make_async_remote_copy(
            src_ref=src, dst_ref=dst, send_sem=send, recv_sem=recv, device_id=target_id, device_id_type=MESH
        )

    pending = []

    def start(copy, ok):
        @pl.when(ok)
        def _():
            copy.start()

        pending.append((copy, ok))

    def arrived(copy, ok):
        @pl.when(ok)
        def _():
            copy.wait_recv()

    def cm_copy(src, slot, d):
        return remote(src, r_cm.at[slot], cm_send.at[slot], cm_recv.at[slot], d)

    def code_copy(source, slot, part, d):
        at = pl.ds(part * (WIDE // PARTS), WIDE // PARTS)
        if source is None:
            source = code_right.at[:, at] if slot == 2 else code.at[:, at]
        else:
            source = r_code.at[source, :, at]
        return remote(source, r_code.at[slot, :, at], r_send.at[slot, part], r_recv.at[slot, part], d)

    start(cm_copy(cm, LEFT, RIGHT), there(RIGHT))
    for part in range(PARTS):
        start(code_copy(None, 2, part, RIGHT), there(RIGHT))
    def own_down(role):
        start(cm_copy(cm, UP, DOWN), there(DOWN) & role)
        for part in range(PARTS):
            start(code_copy(None, 1, part, DOWN), there(DOWN) & role)

    own_down(jnp.logical_not(west))
    start(cm_copy(cm, RIGHT, LEFT), east)

    arrived(cm_copy(cm, LEFT, LEFT), there(LEFT))
    start(cm_copy(r_cm.at[LEFT], UL, DOWN), there(DOWN) & there(LEFT))
    for part in range(PARTS):
        arrived(code_copy(None, 2, part, LEFT), there(LEFT))
        start(code_copy(2, 0, part, DOWN), there(DOWN) & there(LEFT))
    own_down(west)
    arrived(cm_copy(cm, UP, UP), there(UP))
    arrived(cm_copy(cm, UL, UL), there(UL))

    def cm_of(tile, rows_at, lanes_at):
        if tile == OWN:
            return cm[rows_at, lanes_at]
        return r_cm[tile, rows_at, lanes_at]

    for g in range(GROUPS):
        for t in range(4):
            at = slice(g * PAD + t * 4, g * PAD + t * 4 + 4)
            near_cm[at, :] = cm_of(TILE_SETS[0][t], slice(g * 4, g * 4 + 4), slice(None))
    near_high, near_low = split(near_cm[:, :FRAMES])

    frame = lax.broadcasted_iota(I32, (NEAR, FRAMES), 1)
    weighted = jnp.where((frame >= window[0]) & (frame < window[1]), near_cm[:, :FRAMES], 0.0)
    w_high, w_low = split(weighted)
    w_both = jnp.concatenate([w_high, w_low], axis=0)
    q4 = nt(w_both, w_both)
    q = q4[:NEAR, :NEAR] + q4[:NEAR, NEAR:] + q4[NEAR:, :NEAR] + q4[NEAR:, NEAR:]
    a_near = near_cm[:, FRAMES : FRAMES + 1].astype(I32)
    b_near = near_cm[:, FRAMES + 1 : FRAMES + 2].astype(I32)
    live_near = near_cm[:, FRAMES + 2 : FRAMES + 3]
    eye = lax.broadcasted_iota(I32, (NEAR, NEAR), 0) == lax.broadcasted_iota(I32, (NEAR, NEAR), 1)
    mass = jnp.sum(jnp.where(eye, q, 0.0), axis=1, keepdims=True)
    inverse = 1.0 / jnp.where(live_near > 0, mass, 1.0)
    q_high, q_low = split(jnp.where(eye, 0.0, q) * inverse)
    q3 = jnp.concatenate([q_high, q_high, q_low], axis=1)
    load0 = jnp.sum(weighted * back_time[0:1, :], axis=1, keepdims=True)
    load1 = jnp.sum(weighted * back_time[1:2, :], axis=1, keepdims=True)

    tile_at = (lax.broadcasted_iota(I32, (NEAR, 1), 0) >> 2) & 3
    above = tile_at < 2
    aside = (tile_at & 1) == 0
    y_low = jnp.where(above, 0, a_near)
    y_high = jnp.where(live_near > 0, jnp.where(above, a_near, SIDE), 0)
    x_low = jnp.where(aside, 0, b_near)
    x_high = jnp.where(aside, b_near, SIDE)

    def covered(rows_at, begin, width):
        spot = lax.broadcasted_iota(I32, (1, width), 1) + begin
        y = spot >> 6
        x = spot & 63
        return (
            (y >= y_low[rows_at]) & (y < y_high[rows_at]) & (x >= x_low[rows_at]) & (x < x_high[rows_at])
        )

    loads[7].wait()
    width = 1024
    for begin in range(0, PIX, width):
        at = slice(begin, begin + width)
        pull = nt(w_high, movie[at, :])
        pull = pull - load0 * back[0:1, at] - load1 * back[1:2, at]
        target[:, at] = jnp.where(covered(slice(None), begin, width), pull * inverse, -BIG)

    for part in range(PARTS):
        arrived(code_copy(None, 1, part, UP), there(UP))
    for part in range(PARTS):
        arrived(code_copy(None, 0, part, UL), there(UL))
    for t in range(3):
        unpacked(r_code[t], canvas, lambda g: g * PAD + t * 4)
    for g in range(GROUPS):
        canvas[g * PAD + 12 : g * PAD + 16, :] = pad_f[g * 4 : g * 4 + 4, :]
    for g in range(GROUPS):
        rows_at = slice(g * PAD, g * PAD + PAD)
        value = jnp.where(covered(rows_at, 0, PIX), (canvas[rows_at, :] + 32768.0) * (1.0 / 65535.0), 0.0)
        high, low = split(value)
        x3[g * PAD : g * PAD + PAD, :] = high
        x3[NEAR + g * PAD : NEAR + g * PAD + PAD, :] = low
        x3[2 * NEAR + g * PAD : 2 * NEAR + g * PAD + PAD, :] = high

    gram = nt(x3[: 2 * NEAR, :], x3[NEAR:, :])
    gram = gram[:NEAR] + gram[NEAR:]
    overlap = gram[:, :NEAR] + gram[:, NEAR : 2 * NEAR]
    loading = gram[:, 2 * NEAR : 2 * NEAR + 2]
    drive = mm(x3[:NEAR, :], movie[...])
    drive = drive - loading[:, 0:1] * back_time[0:1, :] - loading[:, 1:2] * back_time[1:2, :]
    self_overlap = jnp.sum(jnp.where(eye, overlap, 0.0), axis=1, keepdims=True)
    overlap = jnp.where(eye, 0.0, overlap)
    o_high, o_low = split(overlap)
    product = mm(jnp.concatenate([o_high, o_low], axis=0), near_high)
    shares[:, :FRAMES] = drive - (product[:NEAR] + product[NEAR:] + mm(o_high, near_low))
    shares[:, FRAMES : FRAMES + NEAR] = overlap
    shares[:, FRAMES + NEAR :] = jnp.broadcast_to(self_overlap, (NEAR, 128 - NEAR))
    for t in range(4):
        for g in range(GROUPS):
            share_out[t, g * 4 : g * 4 + 4, :] = shares[g * PAD + t * 4 : g * PAD + t * 4 + 4, :]

    def share_copy(t, d):
        return remote(share_out.at[t], r_share.at[t], s_send.at[t], s_recv.at[t], d)

    for t, d in ((2, LEFT), (0, UL), (1, UP)):
        start(share_copy(t, d), there(d))

    def mate_share(t, k, d):
        return remote(share_out.at[t], r_mate.at[k], mate_send.at[t], mate_recv.at[k], d)

    start(mate_share(3, 0, (0, 1)), west)
    start(mate_share(0, 3, (-1, 0)), east & row_ok(-1))

    for g in range(GROUPS):
        rows_at = slice(g * PAD, g * PAD + PAD)
        value = jnp.maximum(target[rows_at, :] - mm(q3[rows_at, :], x3[: 3 * NEAR, :]), 0.0)
        canvas[rows_at, :] = jnp.floor(jnp.sqrt(value * (1.0 / TOP)) * 65535.0 + 0.5) - 32768.0
        if g < GROUPS - 1:
            high, low = split(value)
            x3[g * PAD : g * PAD + PAD, :] = high
            x3[NEAR + g * PAD : NEAR + g * PAD + PAD, :] = low
            x3[2 * NEAR + g * PAD : 2 * NEAR + g * PAD + PAD, :] = high

    for t in range(2):
        piece_up[t] = packed(canvas, lambda g: g * PAD + t * 4)

    def piece_copy(t, d):
        return remote(piece_up.at[t], r_piece.at[t], p_send.at[t], p_recv.at[t], d)

    for t in range(2):
        start(piece_copy(t, UP), there(UP) & (c < cols // 2))

    arrived(share_copy(1, DOWN), there(DOWN))
    start(remote(r_share.at[1], r_mate.at[2], mate_send.at[1], mate_recv.at[2], RIGHT), west & row_ok(1))
    for t, d in ((2, RIGHT), (0, DR)):
        arrived(share_copy(t, d), there(d))

    def joined(parts, live):
        total = parts[0] + parts[1] + parts[2] + parts[3]
        scale = 1.0 / jnp.where(live > 0, total[:, FRAMES + NEAR : FRAMES + NEAR + 1], 1.0)
        v = jnp.concatenate([part[:, FRAMES : FRAMES + NEAR] for part in parts], axis=1) * scale
        return total[:, :FRAMES] * scale, v

    def weights(v, g):
        high, low = split(jnp.concatenate([v[:, k * NEAR + g * PAD : k * NEAR + g * PAD + PAD] for k in range(4)], axis=1))
        return jnp.concatenate([high, high, low], axis=1)

    goal, v_own = joined([share_out[3], r_share[2], r_share[1], r_share[0]], live_own)
    v_parts = [weights(v_own, g) for g in range(3)]
    own = cm[:, :FRAMES]
    row_group = lax.broadcasted_iota(I32, (PAD, FRAMES), 0) >> 2

    def changes(sources, full):
        for k in range(4):
            for t in range(4):
                if TILE_SETS[k][t] not in sources:
                    continue
                new = sources[TILE_SETS[k][t]]
                at = slice(k * PAD + t * 4, k * PAD + t * 4 + 4)
                full[at, :128] = new[:4, :]
                full[at, 128:] = new[4:, :]
        high, low = split(full[...])
        return jnp.concatenate([high, low, high], axis=0)

    def updated(g, left_over, old, live):
        chosen = (row_group == g) & (live > 0)
        return jnp.where(chosen, jnp.maximum(left_over, 0.0), old)

    def pack(ref, g, new, old):
        change = new - old
        ref[g, :4, :] = change[g * 4 : g * 4 + 4, :128]
        ref[g, 4:, :] = change[g * 4 : g * 4 + 4, 128:]

    def wave_copy(g, d, slot):
        return remote(wave.at[g], r_wave.at[g, slot], t_send.at[g, slot], t_recv.at[g, slot], d)

    def sends(g, d):
        ok = there(d)
        if DIRS[d][1] > 0:
            ok = ok & jnp.logical_not(west)
        if DIRS[d][1] < 0 and g > 0:
            ok = ok & jnp.logical_not(east)
        return ok

    def gets(g, d):
        ok = there(d)
        if DIRS[d][1] > 0 and g > 0:
            ok = ok & jnp.logical_not(west)
        if DIRS[d][1] < 0:
            ok = ok & jnp.logical_not(east)
        return ok

    def mate_copy(g, at, d, slot):
        return remote(mate_wave.at[g], r_wave.at[g, slot], mw_send.at[g, at], t_recv.at[g, slot], d)

    def far_copy(g, down, right):
        return remote(wave.at[g], r_far.at[g, 1 - down], far_send.at[g, 1 - down], far_recv.at[g, 1 - down], (down, right))

    def outer_copy(at, d):
        return remote(outer_wave, r_far.at[1, 2 - at], ow_send.at[at // 2], far_recv.at[1, 2 - at], d)

    joint_copy = remote(joint, r_joint, joint_sem.at[0], joint_sem.at[1], LEFT)
    outer_sum = remote(outer, r_outer, outer_sem.at[0], outer_sem.at[1], (0, 2))

    sides = (
        (west, 1, RIGHT, UR, DR, {UL: UP, LEFT: OWN, DL: DOWN, UP: UR, OWN: RIGHT, DOWN: DR}, (UR, RIGHT, DR)),
        (east, 0, LEFT, UL, DL, {UR: UP, RIGHT: OWN, DR: DOWN, UP: UL, OWN: LEFT, DOWN: DL}, (UL, LEFT, DL)),
    )

    def start_mate(g):
        for role, first, mate, over, under, _, _ in sides:
            if g < first:
                continue

            @pl.when(role)
            def _(mate=mate):
                r_wave[g, mate] = mate_wave[g]

            start(mate_copy(g, 0, UP, under), role & there(UP))
            start(mate_copy(g, 1, DOWN, over), role & there(DOWN))

    left_over = goal
    for g in range(GROUPS):
        if g == GROUPS - 1:
            arrived(remote(merged, r_merged, m_send, m_recv, RIGHT), there(RIGHT))
            spot = lax.broadcasted_iota(I32, (PAD, PIX), 1)
            y = spot >> 6
            x = spot & 63
            a_int = a_own.astype(I32)
            b_int = b_own.astype(I32)
            unpacked(r_merged[...], far_f, lambda k: k * 4)
            unpacked(r_piece[1], near_f, lambda k: k * 4)
            for k in range(GROUPS):
                temp[k * 4 : k * 4 + 4, :] = canvas[k * PAD + 12 : k * PAD + 16, :]
            near = jnp.where(y < a_int, near_f[...], temp[...])
            pad_f[...] = jnp.where(x < b_int, half_turn(far_f[...], True), near) + 32768.0
            for half in range(2):
                part = slice(half * 8, half * 8 + 8)
                pad_f[part, :] = turn(pad_f[part, :], shift_own[part], False)
            whole = pad_f[...]
            upper = jnp.floor(whole * (1.0 / 256.0))
            hl[:PAD, :] = upper.astype(BF16)
            hl[PAD:, :] = (whole - upper * 256.0).astype(BF16)
            unpick_hl = jnp.concatenate([unpick16 * 256.0, unpick16], axis=1).astype(BF16)
            root = mm(unpick_hl, hl[...])[:SLOTS, :] * (1.0 / 65535.0)
            pad_f[:SLOTS, :] = root * root * TOP
            for q in range(PIX // 128):
                out_shapes[pl.ds(q, SLOTS, stride=32), :] = pad_f[:SLOTS, q * 128 : q * 128 + 128]

        if g > 0:
            for d in (UP, DOWN, LEFT, UL, DL):
                arrived(wave_copy(g - 1, d, d), gets(g - 1, d))
            if g == 1:
                @pl.when(beside_west)
                def _():
                    sources = {d: r_wave[0, d] for d in (UP, DOWN, LEFT, UL, DL)}
                    sources[OWN] = wave[0]
                    aim = jnp.where(live_own > 0, goal - mm(v_parts[0], changes(sources, mate_f)), own)
                    for at, value in enumerate((aim, own, v_own)):
                        outer[at, :4, :] = value[4:8, :128]
                        outer[at, 4:, :] = value[4:8, 128:]

                start(outer_sum, beside_west)
            for d in (RIGHT, UR, DR):
                arrived(wave_copy(g - 1, d, d), gets(g - 1, d))
            for role, first, mate, over, under, _, _ in sides:
                if g - 1 >= first:
                    arrived(mate_copy(g - 1, 0, UP, over), role & there(UP))
                    arrived(mate_copy(g - 1, 1, DOWN, under), role & there(DOWN))
            around = {**{d: r_wave[g - 1, d] for d in range(8)}, OWN: wave[g - 1]}
            left_over = left_over - mm(v_parts[g - 1], changes(around, call_f))
        new = updated(g, left_over, own, live_own)
        if g < GROUPS - 1:
            pack(wave, g, new, own)
            for d in (UL, DL, LEFT, UR, DR, RIGHT, UP, DOWN):
                start(wave_copy(g, d, 7 - d), sends(g, d))
            if g < 2:
                for down in (-1, 0, 1):
                    if g == 0:
                        start(far_copy(g, down, 2), beside_west & row_ok(down))
                    start(far_copy(g, down, -2), beside_east & row_ok(down))
        own = new
        if g == 0:
            @pl.when(east)
            def _():
                joint[:, :FRAMES] = goal
                joint[:, FRAMES:] = v_own

            start(joint_copy, east)

            for t in range(2):
                start(piece_copy(t, UP), there(UP) & (c >= cols // 2))

            arrived(mate_share(3, 0, (0, -1)), east)
            arrived(mate_share(1, 2, (0, -1)), east & row_ok(1))
            arrived(mate_share(0, 3, (1, 0)), east & row_ok(1))

            @pl.when(east)
            def _():
                mate_cm[...] = r_cm[LEFT]
                r_mate[1] = share_out[2]
                live = mate_cm[:, FRAMES + 2 : FRAMES + 3]
                mate_goal[...], v_mate = joined([r_mate[k] for k in range(4)], live)
                for k in range(2):
                    mate_v[k] = weights(v_mate, k)
                old = mate_cm[:, :FRAMES]
                pack(mate_wave, 0, updated(0, mate_goal[...], old, live), old)

            start_mate(0)

            for q in range(4):
                for k in range(GROUPS):
                    at = slice(q * SLOTS + k * 3, q * SLOTS + k * 3 + 3)
                    labels[at, :] = r_cm[LEFT, k * 4 : k * 4 + 3, FRAMES:]
            a_left = labels[:, 0:1].astype(I32)
            row = lax.broadcasted_iota(I32, (DENSE, WIDE), 0)
            quarter = (row >= SLOTS).astype(I32) + (row >= 2 * SLOTS).astype(I32) + (row >= 3 * SLOTS).astype(I32)
            below = quarter * 16 + (lax.broadcasted_iota(I32, (DENSE, WIDE), 1) >> 6) < a_left
            left_codes = packed(canvas, lambda k: k * PAD + 8).astype(I32)
            for t in range(2):
                arrived(piece_copy(t, DOWN), there(DOWN))
            merged[...] = jnp.where(below, r_piece[0].astype(I32), left_codes).astype(I16)
            start(remote(merged, r_merged, m_send, m_recv, LEFT), there(LEFT))
        elif g < GROUPS - 1:
            if g == 1:
                arrived(cm_copy(cm, RIGHT, RIGHT), west)
                arrived(joint_copy, west)

                @pl.when(west)
                def _():
                    mate_cm[...] = r_cm[RIGHT]
                    mate_goal[...] = r_joint[:, :FRAMES]
                    for k in range(2):
                        mate_v[k] = weights(r_joint[:, FRAMES:], k)

            for down in (-1, 0, 1):
                arrived(far_copy(g - 1, -down, -2), west & row_ok(down))
                if g == 1:
                    arrived(far_copy(g - 1, -down, 2), east & row_ok(down))
                elif down:
                    arrived(outer_copy(1 - down, (down, 0)), east & row_ok(down))
            for role, first, mate, over, under, where_at, far_at in sides:
                @pl.when(role)
                def _(where_at=where_at, far_at=far_at):
                    sources = {}
                    for tile, at in where_at.items():
                        sources[tile] = wave[g - 1] if at == OWN else r_wave[g - 1, at]
                    for down, tile in enumerate(far_at):
                        sources[tile] = r_far[g - 1, down]
                    old = mate_cm[:, :FRAMES]
                    live = mate_cm[:, FRAMES + 2 : FRAMES + 3]
                    rest = mate_goal[...] - mm(mate_v[g - 1], changes(sources, mate_f))
                    mate_goal[...] = rest
                    pack(mate_wave, g, updated(g, rest, old, live), old)

            start_mate(g)
            if g == 1:
                arrived(outer_sum, east)

                @pl.when(east)
                def _():
                    rhs = changes({UR: r_wave[0, UL], RIGHT: r_wave[0, LEFT], DR: r_wave[0, DL]}, outer_f)
                    zero = jnp.zeros((4, FRAMES), F32)
                    aim, old, v = (
                        jnp.concatenate(
                            [zero, jnp.concatenate([r_outer[at, :4, :], r_outer[at, 4:, :]], axis=1), zero, zero], axis=0
                        )
                        for at in range(3)
                    )
                    value = jnp.maximum(aim - mm(weights(v, 0), rhs), 0.0)
                    pack2 = value - old
                    outer_wave[:4, :] = pack2[4:8, :128]
                    outer_wave[4:, :] = pack2[4:8, 128:]
                    r_far[1, 1] = outer_wave[...]

                start(outer_copy(0, UP), east & there(UP))
                start(outer_copy(2, DOWN), east & there(DOWN))

    high, low = split(own)
    least = (own - high.astype(F32) - low.astype(F32)).astype(BF16)
    back_own = mm(jnp.concatenate([unpick16] * 3, axis=1).astype(BF16), jnp.concatenate([high, low, least], axis=0))
    new_traces = jnp.where(alive_sub[:SLOTS, 0:1], back_own[:SLOTS, :], old_traces)
    for half in range(2):
        out_traces[pl.ds(half, SLOTS, stride=2), :] = new_traces[:, half * 128 : half * 128 + 128]

    for copy, ok in pending:
        @pl.when(ok)
        def _(copy=copy):
            copy.wait_send()


def on_device(rows, cols, movie, footprints, anchors, groups, counts, temporal, back_spatial, back_temporal, window):
    vmem = pl.BlockSpec(memory_space=pltpu.VMEM)
    dma = pltpu.SemaphoreType.DMA
    shapes, traces = pl.pallas_call(
        functools.partial(kernel, rows, cols),
        out_shape=(
            jax.ShapeDtypeStruct((SLOTS * PIX // 128, 128), F32),
            jax.ShapeDtypeStruct((SLOTS * FRAMES // 128, 128), F32),
        ),
        in_specs=[pl.BlockSpec(memory_space=pltpu.SMEM)] + [pl.BlockSpec(memory_space=pltpu.HBM)] * 8,
        out_specs=(vmem, vmem),
        scratch_shapes=[
            pltpu.SMEM((2, SLOTS), I32),
            pltpu.SMEM((1, SLOTS), I32),
            pltpu.SMEM((2,), I32),
            pltpu.VMEM((SLOTS * PIX // 128, 128), F32),
            pltpu.VMEM((SLOTS * FRAMES // 128, 128), F32),
            pltpu.VMEM((2, SIDE, SIDE), BF16),
            pltpu.VMEM((2, FRAMES), F32),
            pltpu.VMEM((PIX, FRAMES), BF16),
            pltpu.VMEM((2 * SIDE, 2 * SIDE), F32),
            pltpu.VMEM((16, PIX), F32),
            pltpu.VMEM((PAD, PIX), F32),
            pltpu.VMEM((2 * PAD, PIX), BF16),
            pltpu.VMEM((DENSE, WIDE), I16),
            pltpu.VMEM((DENSE, WIDE), I16),
            pltpu.VMEM((3, DENSE, WIDE), I16),
            pltpu.VMEM((PAD, FRAMES + 128), F32),
            pltpu.VMEM((8, PAD, FRAMES + 128), F32),
            pltpu.VMEM((NEAR, FRAMES + 128), F32),
            pltpu.VMEM((NEAR, PIX), F32),
            pltpu.VMEM((NEAR, PIX), F32),
            pltpu.VMEM((3 * NEAR + 16, PIX), BF16),
            pltpu.VMEM((NEAR, FRAMES + 128), F32),
            pltpu.VMEM((4, PAD, FRAMES + 128), F32),
            pltpu.VMEM((3, PAD, FRAMES + 128), F32),
            pltpu.VMEM((3, 8, 128), F32),
            pltpu.VMEM((3, 8, 8, 128), F32),
            pltpu.VMEM((4 * PAD, FRAMES), F32),
            pltpu.VMEM((PAD, PIX), F32),
            pltpu.VMEM((DENSE, WIDE), F32),
            pltpu.VMEM((DENSE, 128), F32),
            pltpu.VMEM((PAD, PIX), F32),
            pltpu.VMEM((PAD, PIX), F32),
            pltpu.VMEM((4, PAD, FRAMES + 128), F32),
            pltpu.VMEM((PAD, FRAMES + 128), F32),
            pltpu.VMEM((PAD, FRAMES), F32),
            pltpu.VMEM((2, PAD, 3 * NEAR), BF16),
            pltpu.VMEM((3, 8, 128), F32),
            pltpu.VMEM((2, 3, 8, 128), F32),
            pltpu.VMEM((4 * PAD, FRAMES), F32),
            pltpu.VMEM((PAD, 2 * FRAMES), F32),
            pltpu.VMEM((PAD, 2 * FRAMES), F32),
            pltpu.VMEM((3, 8, 128), F32),
            pltpu.VMEM((3, 8, 128), F32),
            pltpu.VMEM((8, 128), F32),
            pltpu.VMEM((4 * PAD, FRAMES), F32),
            pltpu.VMEM((2, DENSE, WIDE), I16),
            pltpu.VMEM((2, DENSE, WIDE), I16),
            pltpu.VMEM((DENSE, WIDE), I16),
            pltpu.VMEM((DENSE, WIDE), I16),
            dma((8,)),
            dma((8,)),
            dma((8,)),
            dma((3, PARTS)),
            dma((3, PARTS)),
            dma((3,)),
            dma((3,)),
            dma((3, 8)),
            dma((3, 8)),
            dma((2,)),
            dma((2,)),
            dma,
            dma,
            dma((4,)),
            dma((4,)),
            dma((3, 2)),
            dma((2, 3)),
            dma((2, 3)),
            dma((2,)),
            dma((2,)),
            dma((2,)),
        ],
        compiler_params=pltpu.CompilerParams(collective_id=0, has_side_effects=True, vmem_limit_bytes=32 << 20),
    )(
        counts,
        *(
            pltpu.with_memory_space_constraint(x, pltpu.HBM)
            for x in (
                anchors.reshape(SLOTS, 2).T,
                groups.reshape(1, SLOTS),
                window,
                footprints.reshape(SLOTS * PIX // 128, 128),
                temporal.reshape(SLOTS * FRAMES // 128, 128),
                back_spatial,
                back_temporal,
                movie.reshape(PIX, FRAMES),
            )
        )
    )
    return shapes.reshape(1, 1, SLOTS, PIX), traces.reshape(1, 1, SLOTS, FRAMES)


def solution(mesh):
    return jax.shard_map(
        functools.partial(on_device, mesh.shape["row"], mesh.shape["col"]),
        mesh=mesh,
        in_specs=(
            P("row", "col", None),
            P("row", "col", None, None),
            P("row", "col", None, None),
            P("row", "col", None),
            P("row", "col"),
            P("row", "col", None, None),
            P(None, "row", "col"),
            P(),
            P(),
        ),
        out_specs=(P("row", "col", None, None), P("row", "col", None, None)),
        check_vma=False,
    )
```
